256 devices in a mesh: dp: 8 (over z), row: 8 (over y_hi, x), col: 4 (over y_lo, core).
Axes of the slice: x: 4, y: 4 (y_hi: 2, y_lo: 2; y = y_hi * 2 + y_lo), z: 8, core: 2. Of those that a mesh axis runs over, the one named last changes fastest.
Arguments:
- inputs: bfloat16 [8, 192, 64, 512], P('dp', None, 'row', 'col'), may hold values from -16 to 16
- norm_gain: float32 [192], replicated, may hold values from 0.25 to 1.75
- w_expand: bfloat16 [192, 768], replicated, may hold values from -0.4375 to 0.4375
- kernel: float32 [768, 9], replicated, may hold values from -2 to 2
- w_squeeze: float32 [768, 48], replicated, may hold values from -1.5 to 1.5
- w_excite: float32 [48, 768], replicated, may hold values from -6 to 6
- w_project: bfloat16 [768, 192], replicated, may hold values from -0.21875 to 0.21875
- cotangent: bfloat16 [8, 192, 64, 512], P('dp', None, 'row', 'col'), may hold values from -16 to 16
Outputs:
- output: bfloat16 [8, 192, 64, 512], P('dp', None, 'row', 'col')
- grad_inputs: bfloat16 [8, 192, 64, 512], P('dp', None, 'row', 'col')
- grad_gain: float32 [192], replicated
- grad_w_expand: float32 [192, 768], replicated
- grad_kernel: float32 [768, 9], replicated
- grad_w_squeeze: float32 [768, 48], replicated
- grad_w_excite: float32 [48, 768], replicated
- grad_w_project: float32 [768, 192], replicated
The draws below stay inside these ranges and needn't reach their ends.
All inputs are finite; a program needn't handle non-finite values.
Results may differ from the reference program's by a relative error of at most 0.0019.
Values may be sent and summed in bfloat16 or wider, within the bound.
No kernel may reach another device: no remote copies, remote signals or barrier semaphores. Data moves between devices by JAX's collectives and lax.ppermute only.
A program may use at most 64 MiB of HBM per device.

```python
import jax
import jax.numpy as jnp
from jax import lax

C = 192
E = 768
S = 48
SAMPLES = 8
NH = 64
NW = 512


def draw_inputs(key, part):
    keys = jax.random.split(key, 4)
    noise = jax.random.normal(keys[0], (SAMPLES, C, NH, NW), jnp.float32)
    lean = jax.random.normal(keys[3], (SAMPLES, C, 1, 1), jnp.float32)
    chan = jnp.exp(jax.random.uniform(keys[1], (1, C, 1, 1), jnp.float32, -1.15, 1.15))
    cell = jnp.exp(jax.random.uniform(keys[2], (SAMPLES, 1, NH, NW), jnp.float32, -1.15, 1.15))
    down = lax.broadcasted_iota(jnp.float32, (1, 1, NH, NW), 2) / NH
    across = lax.broadcasted_iota(jnp.float32, (1, 1, NH, NW), 3) / NW
    ramp = 0.3 + 0.9 * (down + across)
    return jnp.clip(noise * chan * cell + lean * ramp, -16.0, 16.0).astype(jnp.bfloat16)


def draw_cotangent(key, part):
    keys = jax.random.split(key, 3)
    noise = jax.random.normal(keys[0], (SAMPLES, C, NH, NW), jnp.float32)
    lean = jax.random.normal(keys[1], (SAMPLES, C, 1, 1), jnp.float32)
    cell = jnp.exp(jax.random.uniform(keys[2], (SAMPLES, 1, NH, NW), jnp.float32, -0.7, 0.7))
    return jnp.clip(noise * cell + lean, -16.0, 16.0).astype(jnp.bfloat16)


def gaussian(rng, extent, scale, reach, held_as=jnp.bfloat16):
    return jnp.clip(scale * jax.random.normal(rng, extent, jnp.float32), -reach, reach).astype(held_as)


def setup_inputs(seed: int = 0) -> dict:
    seeds = jax.random.split(jax.random.key(seed), 9)
    inputs = draw_inputs(jax.random.fold_in(seeds[8], 71), 0)
    norm_gain = jnp.clip(1.0 + 0.15 * jax.random.normal(seeds[1], (C,), jnp.float32), 0.25, 1.75)
    w_expand = gaussian(seeds[2], (C, E), C ** -0.5, 0.4375)
    kernel = gaussian(seeds[3], (E, 9), 9 ** -0.5, 2.0, jnp.float32)
    w_squeeze = gaussian(seeds[4], (E, S), (3 * E ** -0.5), 1.5, jnp.float32)
    w_excite = gaussian(seeds[5], (S, E), (4 * S ** -0.5), 6.0, jnp.float32)
    w_project = gaussian(seeds[6], (E, C), E ** -0.5, 0.21875)
    cotangent = draw_cotangent(jax.random.fold_in(seeds[8], 71), 0)
    return {"inputs": inputs, "norm_gain": norm_gain, "w_expand": w_expand, "kernel": kernel, "w_squeeze": w_squeeze, "w_excite": w_excite, "w_project": w_project, "cotangent": cotangent}


EPS = 1e-06
HIGH = lax.Precision.HIGHEST

def silu_slope(value):
    sig = jax.nn.sigmoid(value)
    return sig * (1.0 + value * (1.0 - sig))

def one_sample(inputs, cotangent, norm_gain, w_expand, kernel, w_squeeze, w_excite, w_project):
    chans, height, width = inputs.shape
    widened = inputs.astype(jnp.float32)
    inverse = lax.rsqrt(lax.optimization_barrier(jnp.mean(widened * widened, axis=0, keepdims=True)) + EPS)
    normed = widened * inverse
    scaled = (normed * norm_gain[:, None, None]).astype(jnp.bfloat16)
    pre = jnp.einsum('chw,ce->ehw', scaled.astype(jnp.float32), w_expand.astype(jnp.float32), precision=HIGH)
    hidden = jax.nn.silu(pre).astype(jnp.bfloat16)
    padded = jnp.pad(hidden, ((0, 0), (1, 1), (1, 1))).astype(jnp.float32)
    conv = jnp.zeros(pre.shape, jnp.float32)
    for tap in range(9):
        drow, dcol = (tap // 3, tap % 3)
        conv = conv + kernel[:, tap][:, None, None] * padded[:, drow:drow + height, dcol:dcol + width]
    act = jax.nn.silu(conv)
    pooled = lax.optimization_barrier(jnp.mean(act, axis=(1, 2)))
    squeeze_pre = jnp.dot(pooled, w_squeeze, precision=HIGH)
    squeezed = jax.nn.silu(squeeze_pre)
    excite_pre = jnp.dot(squeezed, w_excite, precision=HIGH)
    excite = jax.nn.sigmoid(excite_pre)
    gated = (act * excite[:, None, None]).astype(jnp.bfloat16)
    proj = jnp.einsum('ehw,ec->chw', gated.astype(jnp.float32), w_project.astype(jnp.float32), precision=HIGH)
    output = (widened + proj).astype(jnp.bfloat16)
    cot = cotangent.astype(jnp.float32)
    grad_gated = jnp.einsum('chw,ec->ehw', cot, w_project.astype(jnp.float32), precision=HIGH)
    grad_project = jnp.einsum('ehw,chw->ec', gated.astype(jnp.float32), cot, precision=HIGH)
    grad_excite = lax.optimization_barrier(jnp.sum(grad_gated * act, axis=(1, 2)))
    grad_epre = grad_excite * excite * (1.0 - excite)
    grad_wexc = squeezed[:, None] * grad_epre[None, :]
    grad_spre = jnp.dot(w_excite, grad_epre, precision=HIGH) * silu_slope(squeeze_pre)
    grad_wsq = pooled[:, None] * grad_spre[None, :]
    grad_pooled = jnp.dot(w_squeeze, grad_spre, precision=HIGH)
    grad_act = grad_gated * excite[:, None, None] + (grad_pooled / (height * width))[:, None, None]
    grad_conv = (grad_act * silu_slope(conv)).astype(jnp.bfloat16)
    grad_pad = jnp.pad(grad_conv, ((0, 0), (1, 1), (1, 1))).astype(jnp.float32)
    grad_hidden = jnp.zeros(pre.shape, jnp.float32)
    taps = []
    for tap in range(9):
        drow, dcol = (tap // 3, tap % 3)
        grad_hidden = grad_hidden + kernel[:, tap][:, None, None] * grad_pad[:, 2 - drow:2 - drow + height, 2 - dcol:2 - dcol + width]
        taps.append(lax.optimization_barrier(jnp.sum(grad_conv.astype(jnp.float32) * padded[:, drow:drow + height, dcol:dcol + width], axis=(1, 2))))
    grad_kernel = jnp.stack(taps, axis=1)
    grad_pre = (grad_hidden * silu_slope(pre)).astype(jnp.bfloat16)
    grad_wexp = jnp.einsum('chw,ehw->ce', scaled.astype(jnp.float32), grad_pre.astype(jnp.float32), precision=HIGH)
    grad_scaled = jnp.einsum('ce,ehw->chw', w_expand.astype(jnp.float32), grad_pre.astype(jnp.float32), precision=HIGH)
    grad_gain = lax.optimization_barrier(jnp.sum(grad_scaled * normed, axis=(1, 2)))
    grad_normed = grad_scaled * norm_gain[:, None, None]
    grad_in = inverse * (grad_normed - normed * lax.optimization_barrier(jnp.mean(grad_normed * normed, axis=0, keepdims=True))) + cot
    return (output, grad_in.astype(jnp.bfloat16), grad_gain, grad_wexp, grad_kernel, grad_wsq, grad_wexc, grad_project)

def reference(inputs, norm_gain, w_expand, kernel, w_squeeze, w_excite, w_project, cotangent):

    def step(pair):
        return one_sample(pair[0], pair[1], norm_gain, w_expand, kernel, w_squeeze, w_excite, w_project)
    result = lax.map(step, (inputs, cotangent))
    return (result[0], result[1], lax.optimization_barrier(jnp.sum(result[2], axis=0)), lax.optimization_barrier(jnp.sum(result[3], axis=0)), lax.optimization_barrier(jnp.sum(result[4], axis=0)), lax.optimization_barrier(jnp.sum(result[5], axis=0)), lax.optimization_barrier(jnp.sum(result[6], axis=0)), lax.optimization_barrier(jnp.sum(result[7], axis=0)))
```

```python
import jax
import jax.numpy as jnp
from jax import lax
from jax.sharding import PartitionSpec as P

EPS = 1e-06
HIGH = lax.Precision.HIGHEST
RC = ("row", "col")


def with_halo(shard, sides, width):
    for axis, dim in sides:
        count, length = (lax.axis_size(axis), shard.shape[dim])
        up = [(i, (i + 1) % count) for i in range(count - 1)]
        down = [(j, i) for i, j in up]
        last = lax.slice_in_dim(shard, length - width, length, axis=dim)
        leading = lax.slice_in_dim(shard, 0, width, axis=dim)
        before = lax.ppermute(last, axis, up)
        after = lax.ppermute(leading, axis, down)
        shard = jnp.concatenate([before, shard, after], axis=dim)
    return shard


def silu_slope(value):
    sig = jax.nn.sigmoid(value)
    return sig * (1.0 + value * (1.0 - sig))


def normalize(inputs, norm_gain):
    widened = inputs.astype(jnp.float32)
    inverse = lax.rsqrt(jnp.mean(widened * widened, axis=1, keepdims=True) + EPS)
    normed = widened * inverse
    scaled = (normed * norm_gain[None, :, None, None]).astype(jnp.bfloat16)
    return (normed, inverse, scaled)


def expand(scaled, w_expand):
    return jnp.einsum("bchw,ce->behw", scaled, w_expand, preferred_element_type=jnp.float32)


def depthwise(hidden_pad, kernel, out_rows, out_cols):
    total = jnp.zeros((hidden_pad.shape[0], hidden_pad.shape[1], out_rows, out_cols), jnp.float32)
    for tap in range(9):
        drow, dcol = (tap // 3, tap % 3)
        total = (
            total
            + kernel[:, tap][None, :, None, None]
            * hidden_pad[:, :, drow : drow + out_rows, dcol : dcol + out_cols]
        )
    return total


def gathered(block, axes, count):
    return lax.all_to_all(
        jnp.broadcast_to(block[None], (count,) + block.shape), axes, 0, 0, tiled=True
    )


def local(inputs, norm_gain, w_expand, kernel, w_squeeze, w_excite, w_project, cotangent):
    batch, chans, rows, cols = inputs.shape
    pixels = rows * cols * lax.axis_size("row") * lax.axis_size("col")
    normed, inverse, scaled = normalize(inputs, norm_gain)
    pre = expand(scaled, w_expand)
    hidden = jax.nn.silu(pre).astype(jnp.bfloat16)
    hidden_pad = with_halo(hidden, (("row", 2), ("col", 3)), 1)
    conv = depthwise(hidden_pad, kernel, rows, cols)
    act = jax.nn.silu(conv)
    grad_gated = jnp.einsum(
        "bchw,ec->behw", cotangent, w_project, preferred_element_type=jnp.float32
    )
    sums = jnp.concatenate(
        [jnp.sum(act, axis=(2, 3)), jnp.sum(grad_gated * act, axis=(2, 3))], axis=0
    ).reshape(12, 128)
    sums = jnp.sum(gathered(sums, RC, 32), axis=0).reshape(2, 768)
    pooled = sums[:1] / pixels
    grad_excite = sums[1:]
    squeeze_pre = jnp.dot(pooled, w_squeeze, precision=HIGH)
    squeezed = jax.nn.silu(squeeze_pre)
    excite_pre = jnp.dot(squeezed, w_excite, precision=HIGH)
    excite = jax.nn.sigmoid(excite_pre)
    gated = (act * excite[:, :, None, None]).astype(jnp.bfloat16)
    proj = jnp.einsum("behw,ec->bchw", gated, w_project, preferred_element_type=jnp.float32)
    output = (inputs.astype(jnp.float32) + proj).astype(jnp.bfloat16)
    grad_project = jnp.einsum("behw,bchw->ce", gated, cotangent, preferred_element_type=jnp.float32)
    grad_epre = grad_excite * excite * (1.0 - excite)
    grad_spre = jnp.einsum("be,se->bs", grad_epre, w_excite, precision=HIGH) * silu_slope(
        squeeze_pre
    )
    grad_pooled = jnp.einsum("bs,es->be", grad_spre, w_squeeze, precision=HIGH)
    grad_act = grad_gated * excite[:, :, None, None] + (grad_pooled / pixels)[:, :, None, None]
    grad_conv = (grad_act * silu_slope(conv)).astype(jnp.bfloat16)
    grad_pad = with_halo(grad_conv, (("row", 2), ("col", 3)), 1)
    grad_hidden = jnp.zeros(pre.shape, jnp.float32)
    taps = []
    for tap in range(9):
        drow, dcol = (tap // 3, tap % 3)
        grad_hidden = (
            grad_hidden
            + kernel[:, tap][None, :, None, None]
            * grad_pad[:, :, 2 - drow : 2 - drow + rows, 2 - dcol : 2 - dcol + cols]
        )
        taps.append(
            jnp.sum(
                grad_conv.astype(jnp.float32)
                * hidden_pad[:, :, drow : drow + rows, dcol : dcol + cols].astype(jnp.float32),
                axis=(0, 2, 3),
            )
        )
    grad_kernel = jnp.stack(taps, axis=0)
    grad_pre = (grad_hidden * silu_slope(pre)).astype(jnp.bfloat16)
    grad_wexp = jnp.einsum("bchw,behw->ce", scaled, grad_pre, preferred_element_type=jnp.float32)
    grad_scaled = jnp.einsum(
        "ce,behw->bchw", w_expand, grad_pre, preferred_element_type=jnp.float32
    )
    grad_gain = jnp.sum(grad_scaled * normed, axis=(0, 2, 3))
    grad_normed = grad_scaled * norm_gain[None, :, None, None]
    grad_in = inverse * (
        grad_normed - normed * jnp.mean(grad_normed * normed, axis=1, keepdims=True)
    ) + cotangent.astype(jnp.float32)

    def blocks(w):
        return w.reshape(192, 6, 128).transpose(1, 0, 2).reshape(1152, 128)

    def unblock(w):
        return w.reshape(6, 192, 128).transpose(1, 0, 2).reshape(192, 768)

    big = jnp.concatenate([blocks(grad_wexp), blocks(grad_project)], axis=0).reshape(32, 72, 128)
    small = jnp.concatenate(
        [grad_kernel.reshape(6912), grad_gain, jnp.zeros((1088,), jnp.float32)]
    ).reshape(32, 2, 128)
    packed = jnp.concatenate([big, small, jnp.zeros((32, 6, 128), jnp.float32)], axis=1)
    mine = jnp.sum(lax.all_to_all(packed, RC, 0, 0, tiled=True), axis=0)
    vecs = jnp.concatenate(
        [
            pooled.reshape(768),
            grad_epre.reshape(768),
            squeezed.reshape(48),
            grad_spre.reshape(48),
            jnp.zeros((416,), jnp.float32),
        ]
    ).reshape(16, 128)
    shared = gathered(jnp.concatenate([mine, vecs], axis=0), "dp", 8)
    total = jnp.sum(shared[:, :80], axis=0)
    vec = shared[:, 80:].reshape(8, 2048)
    pooled_s, epre_s, squeezed_s, spre_s = (
        vec[:, :768],
        vec[:, 768:1536],
        vec[:, 1536:1584],
        vec[:, 1584:1632],
    )
    grad_wexc = jnp.einsum("bs,be->se", squeezed_s, epre_s, precision=HIGH)
    grad_wsq = jnp.einsum("be,bs->es", pooled_s, spre_s, precision=HIGH)
    high = total[:74].astype(jnp.bfloat16)
    low = (total[72:74] - lax.reduce_precision(total[72:74], 8, 7)).astype(jnp.bfloat16)
    send = jnp.concatenate([high, low, jnp.zeros((4, 128), jnp.bfloat16)], axis=0)
    every = gathered(send, RC, 32).astype(jnp.float32)
    big = every[:, :72].reshape(2, 1152, 128)
    small = (every[:, 72:74] + every[:, 74:76]).reshape(8192)
    return (
        output,
        grad_in.astype(jnp.bfloat16),
        small[6912:7104],
        unblock(big[0]),
        small[:6912].reshape(9, 768).T,
        grad_wsq,
        grad_wexc,
        unblock(big[1]).T,
    )


def solution(mesh):
    placed = (
        P("dp", None, "row", "col"),
        P(),
        P(),
        P(),
        P(),
        P(),
        P(),
        P("dp", None, "row", "col"),
    )
    return jax.shard_map(
        local,
        mesh=mesh,
        in_specs=placed,
        out_specs=(
            P("dp", None, "row", "col"),
            P("dp", None, "row", "col"),
            P(),
            P(),
            P(),
            P(),
            P(),
            P(),
        ),
        check_vma=False,
    )
```

```python
import functools

import jax
import jax.numpy as jnp
from jax import lax
from jax.experimental import pallas as pl
from jax.experimental.pallas import tpu as pltpu
from jax.sharding import PartitionSpec as P

EPS = 1e-06
HIGH = lax.Precision.HIGHEST
RC = ("row", "col")
F32, BF16 = jnp.float32, jnp.bfloat16
CH, EX, SQ = 192, 768, 48
ROWS, LANES = 8, 128
EB = 128
SUB = 8
STEPS = EX // EB
XS = ROWS + 5
CS = ROWS + 3
NT = (((1,), (1,)), ((), ()))


def lane_iota(rows):
    return lax.broadcasted_iota(jnp.int32, (rows, LANES), 1)


def rounded(v):
    return v.astype(BF16).astype(F32)


def sigmoid(v):
    return 0.5 + 0.5 * jnp.tanh(0.5 * v)


def slab(s, n=1):
    return pl.ds(s * LANES, n * LANES)


def strip_kernel(x_ref, c_ref, top_ref, bot_ref, out_ref):
    lane = lane_iota(CH)
    total = jnp.zeros((CH, LANES), F32)
    for rr in range(ROWS + 4):
        if rr < 2:
            v = top_ref[rr]
        elif rr < ROWS + 2:
            v = x_ref[rr - 2]
        else:
            v = bot_ref[rr - ROWS - 2]
        v = pltpu.roll(v.astype(F32), (8 * rr + 2) % LANES, 1)
        total = jnp.where((lane >= 8 * rr) & (lane < 8 * rr + 4), v, total)
        if 1 <= rr <= ROWS + 2:
            if rr == 1:
                v = top_ref[2]
            elif rr == ROWS + 2:
                v = bot_ref[2]
            else:
                v = c_ref[rr - 2]
            v = pltpu.roll(v.astype(F32), (8 * rr + 5) % LANES, 1)
            total = jnp.where((lane >= 8 * rr + 4) & (lane < 8 * rr + 6), v, total)
    out_ref[...] = total.astype(BF16)


def input_strip(own_ref, left_ref, right_ref):
    own, left, right = (r[...].astype(F32) for r in (own_ref, left_ref, right_ref))
    pos = lane_iota(CH) % 8
    value = jnp.where(pos < 2, left, 0.0)
    value = jnp.where(pos == 2, own, value)
    value = jnp.where(pos == 4, pltpu.roll(own, 3, 1), value)
    return jnp.where((pos == 5) | (pos == 6), pltpu.roll(right, 3, 1), value)


def cotangent_strip(left_ref, right_ref):
    left, right = (r[...].astype(F32) for r in (left_ref, right_ref))
    pos = lane_iota(CH) % 8
    value = jnp.where(pos == 1, pltpu.roll(left, LANES - 3, 1), 0.0)
    return jnp.where(pos == 5, right, value)


def neighbours(v, strip, rr, first, last):
    left = jnp.where(first, pltpu.roll(strip, (LANES - 8 * rr - 1) % LANES, 1), pltpu.roll(v, 1, 1))
    right = jnp.where(
        last,
        pltpu.roll(strip, (LANES - 1 - 8 * rr - 5) % LANES, 1),
        pltpu.roll(v, LANES - 1, 1),
    )
    return left, right


def forward_kernel(
    x_ref, c_ref, top_ref, bot_ref, own_ref, left_ref, right_ref, gain_ref, wexp_ref, taps_ref,
    wproj_ref, pre_out, conv_out, sums_out, scaled_s, cot_s, pre_s, gg_s, acc_s,
):
    @pl.when(pl.program_id(0) == 0)
    def _():
        gain = gain_ref[...]
        for s in range(XS):
            if s < 2:
                x = top_ref[s].astype(F32)
            elif s < ROWS + 2:
                x = x_ref[s - 2].astype(F32)
            elif s < ROWS + 4:
                x = bot_ref[s - ROWS - 2].astype(F32)
            else:
                x = input_strip(own_ref, left_ref, right_ref)
            inverse = lax.rsqrt(jnp.sum(x * x, axis=0, keepdims=True) / CH + EPS)
            scaled_s[:, slab(s)] = (x * inverse * gain).astype(BF16)
        for r in range(ROWS):
            cot_s[:, slab(r)] = c_ref[r]

    pre_s[...] = jnp.dot(wexp_ref[...], scaled_s[...], preferred_element_type=F32)
    gg_s[...] = jnp.dot(wproj_ref[...], cot_s[...], preferred_element_type=F32)
    pre_out[...] = pre_s[:, slab(2, ROWS)]
    lane = lane_iota(SUB)
    first, last = lane == 0, lane == LANES - 1

    def body(i, carry):
        ds = pl.ds(pl.multiple_of(i * SUB, SUB), SUB)
        k = [jnp.broadcast_to(taps_ref[ds, t : t + 1], (SUB, LANES)) for t in range(9)]

        def hidden(s):
            v = pre_s[ds, slab(s)]
            return rounded(v * sigmoid(v))

        strip = hidden(XS - 1)
        acc = [None] * (ROWS + 4)
        for rr in range(ROWS + 4):
            h = hidden(rr)
            hl, hr = neighbours(h, strip, rr, first, last)
            for a in (-1, 0, 1):
                o = rr - a
                if 1 <= o <= ROWS + 2:
                    t = 3 * (a + 1)
                    term = k[t] * hl + k[t + 1] * h + k[t + 2] * hr
                    acc[o] = term if acc[o] is None else acc[o] + term
        pooled = jnp.zeros((SUB, LANES), F32)
        gexc = jnp.zeros((SUB, LANES), F32)
        for o in range(1, ROWS + 3):
            v = acc[o]
            conv_out[ds, slab(o - 1)] = v
            if 2 <= o <= ROWS + 1:
                act = v * sigmoid(v)
                pooled = pooled + act
                gexc = gexc + act * gg_s[ds, slab(o - 2)]
        edge = None
        for a in (-1, 0, 1):
            for c in (-1, 0, 1):
                shift = (-(8 * a + c)) % LANES
                term = k[3 * (a + 1) + c + 1] * (pltpu.roll(strip, shift, 1) if shift else strip)
                edge = term if edge is None else edge + term
        conv_out[ds, slab(CS - 1)] = edge
        acc_s[0, ds, :] = pooled
        acc_s[1, ds, :] = gexc
        return carry

    lax.fori_loop(0, EB // SUB, body, 0)
    ones = jnp.ones((8, LANES), F32)
    for n in range(2):
        row = lax.dot_general(ones, acc_s[n], NT, precision=HIGH, preferred_element_type=F32)
        sums_out[0, n : n + 1, :] = row[:1]


def squeeze_kernel(parts_ref, wsq_ref, wexc_ref, exc_out, gp_out, vec_out):
    pixels = 32768.0
    total = jnp.sum(parts_ref[...], axis=0)
    pooled = jnp.concatenate([total[2 * j : 2 * j + 1] for j in range(STEPS)], axis=1) / pixels
    gexc = jnp.concatenate([total[2 * j + 1 : 2 * j + 2] for j in range(STEPS)], axis=1)
    pooled = jnp.broadcast_to(pooled, (8, EX))
    gexc = jnp.broadcast_to(gexc, (8, EX))
    wsq, wexc = wsq_ref[...], wexc_ref[...]
    spre = jnp.dot(pooled, wsq, precision=HIGH, preferred_element_type=F32)
    sig = jax.nn.sigmoid(spre)
    squeezed = spre * sig
    epre = jnp.dot(squeezed, wexc, precision=HIGH, preferred_element_type=F32)
    excite = jax.nn.sigmoid(epre)
    gepre = gexc * excite * (1.0 - excite)
    gspre = lax.dot_general(gepre, wexc, NT, precision=HIGH, preferred_element_type=F32)
    gspre = gspre * (sig * (1.0 + spre * (1.0 - sig)))
    gpool = lax.dot_general(gspre, wsq, NT, precision=HIGH, preferred_element_type=F32)
    gpool = gpool / pixels
    vec_out[...] = jnp.zeros((16, LANES), F32)
    for j in range(STEPS):
        cols = slice(j * LANES, (j + 1) * LANES)
        exc_out[cols, :] = jnp.broadcast_to(excite[:1, cols], (LANES, LANES)).T
        gp_out[cols, :] = jnp.broadcast_to(gpool[:1, cols], (LANES, LANES)).T
        vec_out[j : j + 1, :] = pooled[:1, cols]
        vec_out[STEPS + j : STEPS + j + 1, :] = gepre[:1, cols]
    vec_out[12:13, :SQ] = squeezed[:1]
    vec_out[13:14, :SQ] = gspre[:1]


def backward_kernel(
    x_ref, c_ref, top_ref, bot_ref, left_ref, right_ref, gain_ref, mask_ref, pre_ref, conv_ref,
    exc_ref, gp_ref, taps_ref, wexp_ref, wproj_ref, wprojt_ref,
    out_out, gin_out, gain_out, wexp_out, wproj_out, taps_out,
    scaled_s, cot_s, inv_s, gg_s, gated_s, gpre_s, proj_s, gs_s, acc_s,
):
    step = pl.program_id(0)

    @pl.when(step == 0)
    def _():
        gain = gain_ref[...]
        for r in range(ROWS):
            x = x_ref[r].astype(F32)
            inverse = lax.rsqrt(jnp.sum(x * x, axis=0, keepdims=True) / CH + EPS)
            inv_s[r : r + 1, :] = inverse
            scaled_s[:, slab(r)] = (x * inverse * gain).astype(BF16)
            cot_s[:, slab(r + 1)] = c_ref[r]
        cot_s[:, slab(0)] = top_ref[2]
        cot_s[:, slab(ROWS + 1)] = bot_ref[2]
        cot_s[:, slab(CS - 1)] = cotangent_strip(left_ref, right_ref).astype(BF16)
        proj_s[...] = jnp.zeros_like(proj_s)
        gs_s[...] = jnp.zeros_like(gs_s)

    gg_s[...] = jnp.dot(wproj_ref[...], cot_s[...], preferred_element_type=F32)
    lane = lane_iota(SUB)
    first, last = lane == 0, lane == LANES - 1

    def body(i, carry):
        ds = pl.ds(pl.multiple_of(i * SUB, SUB), SUB)
        k = [jnp.broadcast_to(taps_ref[ds, t : t + 1], (SUB, LANES)) for t in range(9)]
        exc, gp = exc_ref[ds, :], gp_ref[ds, :]

        def grad_conv(s, mask):
            v = conv_ref[ds, slab(s)]
            sig = sigmoid(v)
            act = v * sig
            if 1 <= s <= ROWS:
                gated_s[ds, slab(s - 1)] = act * exc
            g = (gg_s[ds, slab(s)] * exc + gp) * (sig + act * (1.0 - sig))
            if mask is not None:
                g = jnp.where(mask_ref[mask : mask + 1, :] > 0.5, g, 0.0)
            return rounded(g)

        def hidden(r):
            v = pre_ref[ds, slab(r)]
            sig = sigmoid(v)
            act = v * sig
            return rounded(act), sig + act * (1.0 - sig)

        strip = grad_conv(CS - 1, 2)
        tap = [None] * 9
        state = {}
        gh = {}
        for s in range(ROWS + 2):
            g = grad_conv(s, 0 if s == 0 else 1 if s == ROWS + 1 else None)
            gl, gr = neighbours(g, strip, s + 1, first, last)
            for a in (-1, 0, 1):
                r = s + a - 1
                if 0 <= r < ROWS:
                    if r not in state:
                        state[r] = hidden(r)
                    h = state[r][0]
                    t = 3 * (a + 1)
                    term = k[t] * gr + k[t + 1] * g + k[t + 2] * gl
                    gh[r] = term if r not in gh else gh[r] + term
                    for c, v in enumerate((gr, g, gl)):
                        tap[t + c] = h * v if tap[t + c] is None else tap[t + c] + h * v
            r = s - 2
            if 0 <= r:
                gpre_s[ds, slab(r)] = gh.pop(r) * state.pop(r)[1]
        for t in range(9):
            acc_s[t, ds, :] = tap[t]
        return carry

    lax.fori_loop(0, EB // SUB, body, 0)
    gated = gated_s[...].astype(BF16)
    gpre = gpre_s[...].astype(BF16)
    wproj_out[...] = lax.dot_general(
        cot_s[:, slab(1, ROWS)], gated, NT, preferred_element_type=F32
    )
    wexp_out[...] = lax.dot_general(scaled_s[...], gpre, NT, preferred_element_type=F32)
    proj_s[...] += jnp.dot(wprojt_ref[...], gated, preferred_element_type=F32)
    gs_s[...] += jnp.dot(wexp_ref[...], gpre, preferred_element_type=F32)
    ones = jnp.ones((8, LANES), F32)
    for t in range(9):
        row = lax.dot_general(ones, acc_s[t], NT, precision=HIGH, preferred_element_type=F32)
        taps_out[t : t + 1, :] = row[:1]

    @pl.when(step == STEPS - 1)
    def _():
        gain = gain_ref[...]
        ggain = jnp.zeros((CH, LANES), F32)
        for r in range(ROWS):
            x = x_ref[r].astype(F32)
            out_out[r] = (x + proj_s[:, slab(r)]).astype(BF16)
            inverse = inv_s[r : r + 1, :]
            normed = x * inverse
            gs = gs_s[:, slab(r)]
            prod = gs * normed
            ggain = ggain + prod
            mean = jnp.sum(prod * gain, axis=0, keepdims=True) / CH
            gin = inverse * (gs * gain - normed * mean) + c_ref[r].astype(F32)
            gin_out[r] = gin.astype(BF16)
        gain_out[...] = lax.dot_general(
            jnp.ones((8, LANES), F32), ggain, NT, precision=HIGH, preferred_element_type=F32
        )


def shape(*dims, dtype=F32):
    return jax.ShapeDtypeStruct(dims, dtype)


def full(*dims):
    return pl.BlockSpec(dims, lambda j: (0,) * len(dims))


def params():
    return pltpu.CompilerParams(
        dimension_semantics=("arbitrary",), vmem_limit_bytes=40 * 1024 * 1024
    )


def gathered(block, axes, count):
    return lax.all_to_all(
        jnp.broadcast_to(block[None], (count,) + block.shape), axes, 0, 0, tiled=True
    )


def exponent(v):
    return jnp.ceil(jnp.log2(jnp.maximum(jnp.max(jnp.abs(v)), 1e-30)))


def local(inputs, norm_gain, w_expand, kernel, w_squeeze, w_excite, w_project, cotangent):
    nrow, ncol = lax.axis_size("row"), lax.axis_size("col")
    row, col = lax.axis_index("row"), lax.axis_index("col")
    x = inputs[0].transpose(1, 0, 2)
    c = cotangent[0].transpose(1, 0, 2)
    fwd_row = [(i, i + 1) for i in range(nrow - 1)]
    bwd_row = [(i + 1, i) for i in range(nrow - 1)]
    fwd_col = [(i, i + 1) for i in range(ncol - 1)]
    bwd_col = [(i + 1, i) for i in range(ncol - 1)]
    top = lax.ppermute(jnp.concatenate([x[6:8], c[7:8]], axis=0), "row", fwd_row)
    bot = lax.ppermute(jnp.concatenate([x[0:2], c[0:1]], axis=0), "row", bwd_row)
    own = pl.pallas_call(strip_kernel, out_shape=shape(CH, LANES, dtype=BF16), name="strip")(
        x, c, top, bot
    )
    left = lax.ppermute(own, "col", fwd_col)
    right = lax.ppermute(own, "col", bwd_col)

    lane = jnp.arange(LANES)
    line, pos = lane // 8, lane % 8
    top_ok, bot_ok = row > 0, row < nrow - 1
    strip_ok = ((pos == 1) & (col > 0)) | ((pos == 5) & (col < ncol - 1))
    strip_ok &= ((line > 1) | top_ok) & ((line < ROWS + 2) | bot_ok)
    mask = jnp.stack(
        [jnp.broadcast_to(top_ok, (LANES,)), jnp.broadcast_to(bot_ok, (LANES,)), strip_ok]
        + [jnp.zeros((LANES,), bool)] * 5
    ).astype(F32)
    gain = norm_gain[:, None]
    wexpt, wprojt = w_expand.T, w_project.T
    halo = full(3, CH, LANES)
    tile = full(ROWS, CH, LANES)
    edge = full(CH, LANES)
    chunk_rows = lambda width: pl.BlockSpec((EB, width), lambda j: (j, 0))
    chunk_cols = pl.BlockSpec((CH, EB), lambda j: (0, j))
    pre, conv, sums = pl.pallas_call(
        forward_kernel,
        grid=(STEPS,),
        in_specs=[tile, tile, halo, halo, edge, edge, edge, full(CH, 1),
                  chunk_rows(CH), chunk_rows(9), chunk_rows(CH)],
        out_specs=[chunk_rows(ROWS * LANES), chunk_rows(CS * LANES),
                   pl.BlockSpec((1, 2, LANES), lambda j: (j, 0, 0))],
        out_shape=[shape(EX, ROWS * LANES), shape(EX, CS * LANES), shape(STEPS, 2, LANES)],
        scratch_shapes=[
            pltpu.VMEM((CH, XS * LANES), BF16),
            pltpu.VMEM((CH, ROWS * LANES), BF16),
            pltpu.VMEM((EB, XS * LANES), F32),
            pltpu.VMEM((EB, ROWS * LANES), F32),
            pltpu.VMEM((2, EB, LANES), F32),
        ],
        compiler_params=params(),
        name="forward",
    )(x, c, top, bot, own, left, right, gain, wexpt, kernel, w_project)

    exc, gp, vec = pl.pallas_call(
        squeeze_kernel,
        out_shape=[shape(EX, LANES), shape(EX, LANES), shape(16, LANES)],
        name="squeeze",
    )(gathered(sums.reshape(2 * STEPS, LANES), RC, 32), w_squeeze, w_excite)

    out, gin, ggain, wexp, wproj, taps = pl.pallas_call(
        backward_kernel,
        grid=(STEPS,),
        in_specs=[tile, tile, halo, halo, edge, edge, full(CH, 1), full(8, LANES),
                  chunk_rows(ROWS * LANES), chunk_rows(CS * LANES), chunk_rows(LANES),
                  chunk_rows(LANES), chunk_rows(9), chunk_cols, chunk_rows(CH), chunk_cols],
        out_specs=[tile, tile, full(8, CH), pl.BlockSpec((CH, EB), lambda j: (j, 0)),
                   pl.BlockSpec((CH, EB), lambda j: (j, 0)),
                   pl.BlockSpec((9, EB), lambda j: (0, j))],
        out_shape=[shape(ROWS, CH, LANES, dtype=BF16), shape(ROWS, CH, LANES, dtype=BF16),
                   shape(8, CH), shape(STEPS * CH, EB), shape(STEPS * CH, EB), shape(9, EX)],
        scratch_shapes=[
            pltpu.VMEM((CH, ROWS * LANES), BF16),
            pltpu.VMEM((CH, CS * LANES), BF16),
            pltpu.VMEM((ROWS, LANES), F32),
            pltpu.VMEM((EB, CS * LANES), F32),
            pltpu.VMEM((EB, ROWS * LANES), F32),
            pltpu.VMEM((EB, ROWS * LANES), F32),
            pltpu.VMEM((CH, ROWS * LANES), F32),
            pltpu.VMEM((CH, ROWS * LANES), F32),
            pltpu.VMEM((9, EB, LANES), F32),
        ],
        compiler_params=params(),
        name="backward",
    )(x, c, top, bot, left, right, gain, mask, pre, conv, exc, gp, kernel, w_expand, w_project,
      wprojt)

    big = jnp.concatenate([wexp, wproj], axis=0).reshape(32, 72, 128)
    small = jnp.concatenate(
        [taps.reshape(6912), ggain[0], jnp.zeros((1088,), F32)]
    ).reshape(32, 2, 128)
    packed = jnp.concatenate([big, small, jnp.zeros((32, 6, 128), F32)], axis=1)
    mine = jnp.sum(lax.all_to_all(packed, RC, 0, 0, tiled=True), axis=0)
    shared = gathered(jnp.concatenate([mine, vec], axis=0), "dp", 8)
    total = jnp.sum(shared[:, :80], axis=0)
    vecs = shared[:, 80:].reshape(8, 2048)
    grad_wexc = jnp.einsum("bs,be->se", vecs[:, 1536:1584], vecs[:, 768:1536], precision=HIGH)
    grad_wsq = jnp.einsum("be,bs->es", vecs[:, :768], vecs[:, 1664:1712], precision=HIGH)
    e_big, e_small = exponent(total[:72]), exponent(total[72:74])
    send = jnp.concatenate(
        [
            total[:72] * jnp.exp2(-e_big),
            total[72:74] * jnp.exp2(-e_small),
            jnp.full((3, 128), e_big),
            jnp.full((3, 128), e_small),
        ],
        axis=0,
    ).astype(jnp.float16)
    every = gathered(send, RC, 32).astype(F32)
    big = (every[:, :72] * jnp.exp2(every[:, 74:75])).reshape(2, STEPS, CH, EB)
    small = (every[:, 72:74] * jnp.exp2(every[:, 77:78])).reshape(8192)
    return (
        out.transpose(1, 0, 2)[None],
        gin.transpose(1, 0, 2)[None],
        small[6912:7104],
        big[0].transpose(1, 0, 2).reshape(CH, EX),
        small[:6912].reshape(9, 768).T,
        grad_wsq,
        grad_wexc,
        big[1].transpose(0, 2, 1).reshape(EX, CH),
    )


def solution(mesh):
    placed = (
        P("dp", None, "row", "col"),
        P(),
        P(),
        P(),
        P(),
        P(),
        P(),
        P("dp", None, "row", "col"),
    )
    return jax.shard_map(
        local,
        mesh=mesh,
        in_specs=placed,
        out_specs=(
            P("dp", None, "row", "col"),
            P("dp", None, "row", "col"),
            P(),
            P(),
            P(),
            P(),
            P(),
            P(),
        ),
        check_vma=False,
    )
```

```python
import functools

import jax
import jax.numpy as jnp
from jax import lax
from jax.experimental import pallas as pl
from jax.experimental.pallas import tpu as pltpu
from jax.sharding import PartitionSpec as P

EPS = 1e-06
HIGH = lax.Precision.HIGHEST
RC = ("row", "col")
F32, BF16 = jnp.float32, jnp.bfloat16
CH, EX, SQ = 192, 768, 48
ROWS, LANES = 8, 128
EB = 256
SUB = 16
STEPS = EX // EB
BLOCKS = EX // LANES
XS = ROWS + 5
CS = ROWS + 3
NT = (((1,), (1,)), ((), ()))


def lane_iota(rows):
    return lax.broadcasted_iota(jnp.int32, (rows, LANES), 1)


def rounded(v):
    return v.astype(BF16).astype(F32)


def lane_sum(v):
    return jnp.sum(v, axis=1, keepdims=True)


def sigmoid(v):
    return 0.5 + 0.5 * jnp.tanh(0.5 * v)


def slab(s, n=1):
    return pl.ds(s * LANES, n * LANES)


def strip_kernel(x_ref, c_ref, top_ref, bot_ref, out_ref):
    lane = lane_iota(CH)
    total = jnp.zeros((CH, LANES), F32)
    for rr in range(ROWS + 4):
        if rr < 2:
            v = top_ref[rr]
        elif rr < ROWS + 2:
            v = x_ref[rr - 2]
        else:
            v = bot_ref[rr - ROWS - 2]
        v = pltpu.roll(v.astype(F32), (8 * rr + 2) % LANES, 1)
        total = jnp.where((lane >= 8 * rr) & (lane < 8 * rr + 4), v, total)
        if 1 <= rr <= ROWS + 2:
            if rr == 1:
                v = top_ref[2]
            elif rr == ROWS + 2:
                v = bot_ref[2]
            else:
                v = c_ref[rr - 2]
            v = pltpu.roll(v.astype(F32), (8 * rr + 5) % LANES, 1)
            total = jnp.where((lane >= 8 * rr + 4) & (lane < 8 * rr + 6), v, total)
    out_ref[...] = total.astype(BF16)


def input_strip(own_ref, left_ref, right_ref):
    own, left, right = (r[...].astype(F32) for r in (own_ref, left_ref, right_ref))
    pos = lane_iota(CH) % 8
    value = jnp.where(pos == 0, pltpu.roll(own, LANES - 1, 1), 0.0)
    value = jnp.where(pos == 1, pltpu.roll(left, 1, 1), value)
    value = jnp.where(pos == 2, right, value)
    value = jnp.where(pos == 3, pltpu.roll(left, 2, 1), value)
    value = jnp.where(pos == 4, pltpu.roll(right, 1, 1), value)
    return jnp.where(pos == 5, pltpu.roll(own, 3, 1), value)


def cotangent_strip(left_ref, right_ref):
    left, right = (r[...].astype(F32) for r in (left_ref, right_ref))
    pos = lane_iota(CH) % 8
    value = jnp.where(pos == 3, pltpu.roll(left, LANES - 1, 1), 0.0)
    return jnp.where(pos == 2, pltpu.roll(right, LANES - 3, 1), value)


def neighbours(v, strip, rr, first, last):
    edge = pltpu.roll(strip, (LANES - 8 * rr - 3) % LANES, 1)
    left = jnp.where(first, edge, pltpu.roll(v, 1, 1))
    right = jnp.where(last, edge, pltpu.roll(v, LANES - 1, 1))
    return left, right


def forward_kernel(
    x_ref, c_ref, top_ref, bot_ref, own_ref, left_ref, right_ref, gain_ref, wexp_ref, taps_ref,
    wproj_ref, pre_out, conv_out, sums_out, scaled_s, cot_s, pre_s, gg_s, acc_s,
):
    @pl.when(pl.program_id(0) == 0)
    def _():
        gain = gain_ref[...]
        for s in range(XS):
            if s < 2:
                x = top_ref[s].astype(F32)
            elif s < ROWS + 2:
                x = x_ref[s - 2].astype(F32)
            elif s < ROWS + 4:
                x = bot_ref[s - ROWS - 2].astype(F32)
            else:
                x = input_strip(own_ref, left_ref, right_ref)
            inverse = lax.rsqrt(jnp.sum(x * x, axis=0, keepdims=True) / CH + EPS)
            place = s - 2 if 2 <= s < ROWS + 2 else s + ROWS if s < 2 else s
            scaled_s[:, slab(place)] = (x * inverse * gain).astype(BF16)
        for r in range(ROWS):
            cot_s[:, slab(r)] = c_ref[r]

    pre_out[...] = jnp.dot(
        wexp_ref[...], scaled_s[:, slab(0, ROWS)], preferred_element_type=F32
    )
    pre_s[...] = jnp.dot(
        wexp_ref[...], scaled_s[:, slab(ROWS, XS - ROWS)], preferred_element_type=F32
    )
    gg_s[...] = jnp.dot(wproj_ref[...], cot_s[...], preferred_element_type=F32)
    lane = lane_iota(SUB)
    first, last = lane == 0, lane == LANES - 1

    def body(i, carry):
        ds = pl.ds(pl.multiple_of(i * SUB, SUB), SUB)
        k = [taps_ref[ds, slab(t)] for t in range(9)]

        def hidden(s):
            if 2 <= s < ROWS + 2:
                v = pre_out[ds, slab(s - 2)]
            else:
                v = pre_s[ds, slab(s if s < 2 else s - ROWS)]
            v = 0.5 * v
            return rounded(v + v * jnp.tanh(v))

        strip = hidden(XS - 1)
        acc = [None] * (ROWS + 4)
        for rr in range(ROWS + 4):
            h = hidden(rr)
            hl, hr = neighbours(h, strip, rr, first, last)
            for a in (-1, 0, 1):
                o = rr - a
                if 1 <= o <= ROWS + 2:
                    t = 3 * (a + 1)
                    term = k[t] * hl + k[t + 1] * h + k[t + 2] * hr
                    acc[o] = term if acc[o] is None else acc[o] + term
        pooled = jnp.zeros((SUB, LANES), F32)
        gexc = jnp.zeros((SUB, LANES), F32)
        for o in range(1, ROWS + 3):
            v = acc[o]
            conv_out[ds, slab(o - 1)] = v
            if 2 <= o <= ROWS + 1:
                act = v * sigmoid(v)
                pooled = pooled + act
                gexc = gexc + act * gg_s[ds, slab(o - 2)]
        edge = None
        for a in (-1, 0, 1):
            for c in (-1, 0, 1):
                shift = (-(8 * a + 2 * c)) % LANES
                term = k[3 * (a + 1) + c + 1] * (pltpu.roll(strip, shift, 1) if shift else strip)
                edge = term if edge is None else edge + term
        conv_out[ds, slab(CS - 1)] = edge
        acc_s[ds, :] = jnp.where(first, lane_sum(pooled), lane_sum(gexc))
        return carry

    lax.fori_loop(0, EB // SUB, body, 0)
    for n in range(EB // LANES):
        sums_out[n] = acc_s[n * LANES : (n + 1) * LANES, :].T[:2]


def squeeze_kernel(parts_ref, wsq_ref, wexc_ref, exc_out, gp_out, vec_out):
    pixels = 32768.0
    total = jnp.sum(parts_ref[...], axis=0)
    pooled = jnp.concatenate([total[2 * j : 2 * j + 1] for j in range(BLOCKS)], axis=1) / pixels
    gexc = jnp.concatenate([total[2 * j + 1 : 2 * j + 2] for j in range(BLOCKS)], axis=1)
    pooled = jnp.broadcast_to(pooled, (8, EX))
    gexc = jnp.broadcast_to(gexc, (8, EX))
    wsq, wexc = wsq_ref[...], wexc_ref[...]
    spre = jnp.dot(pooled, wsq, precision=HIGH, preferred_element_type=F32)
    sig = jax.nn.sigmoid(spre)
    squeezed = spre * sig
    epre = jnp.dot(squeezed, wexc, precision=HIGH, preferred_element_type=F32)
    excite = jax.nn.sigmoid(epre)
    gepre = gexc * excite * (1.0 - excite)
    gspre = lax.dot_general(gepre, wexc, NT, precision=HIGH, preferred_element_type=F32)
    gspre = gspre * (sig * (1.0 + spre * (1.0 - sig)))
    gpool = lax.dot_general(gspre, wsq, NT, precision=HIGH, preferred_element_type=F32)
    gpool = gpool / pixels
    vec_out[...] = jnp.zeros((16, LANES), F32)
    for j in range(BLOCKS):
        cols = slice(j * LANES, (j + 1) * LANES)
        exc_out[cols, :] = jnp.broadcast_to(excite[:1, cols], (LANES, LANES)).T
        gp_out[cols, :] = jnp.broadcast_to(gpool[:1, cols], (LANES, LANES)).T
        vec_out[j : j + 1, :] = pooled[:1, cols]
        vec_out[BLOCKS + j : BLOCKS + j + 1, :] = gepre[:1, cols]
    vec_out[12:13, :SQ] = squeezed[:1]
    vec_out[13:14, :SQ] = gspre[:1]


def backward_kernel(
    x_ref, c_ref, top_ref, bot_ref, left_ref, right_ref, gain_ref, mask_ref, pre_ref, conv_ref,
    exc_ref, gp_ref, taps_ref, wexp_ref, wproj_ref, wprojt_ref,
    out_out, gin_out, gain_out, wexp_out, wproj_out, taps_out,
    scaled_s, cot_s, inv_s, gg_s, gated_s, gpre_s, proj_s, gs_s, acc_s,
):
    step = pl.program_id(0)

    @pl.when(step == 0)
    def _():
        gain = gain_ref[...]
        for r in range(ROWS):
            x = x_ref[r].astype(F32)
            inverse = lax.rsqrt(jnp.sum(x * x, axis=0, keepdims=True) / CH + EPS)
            inv_s[r : r + 1, :] = inverse
            scaled_s[:, slab(r)] = (x * inverse * gain).astype(BF16)
            cot_s[:, slab(r + 1)] = c_ref[r]
        cot_s[:, slab(0)] = top_ref[2]
        cot_s[:, slab(ROWS + 1)] = bot_ref[2]
        cot_s[:, slab(CS - 1)] = cotangent_strip(left_ref, right_ref).astype(BF16)
        proj_s[...] = jnp.zeros_like(proj_s)
        gs_s[...] = jnp.zeros_like(gs_s)

    gg_s[...] = jnp.dot(wproj_ref[...], cot_s[...], preferred_element_type=F32)
    lane = lane_iota(SUB)
    first, last = lane == 0, lane == LANES - 1

    def body(i, carry):
        ds = pl.ds(pl.multiple_of(i * SUB, SUB), SUB)
        k = [taps_ref[ds, slab(t)] for t in range(9)]
        exc, gp = exc_ref[ds, :], gp_ref[ds, :]

        def grad_conv(s, mask):
            v = conv_ref[ds, slab(s)]
            sig = sigmoid(v)
            act = v * sig
            if 1 <= s <= ROWS:
                gated_s[ds, slab(s - 1)] = act * exc
            g = (gg_s[ds, slab(s)] * exc + gp) * (sig + act * (1.0 - sig))
            if mask is not None:
                g = jnp.where(mask_ref[mask : mask + 1, :] > 0.5, g, 0.0)
            return rounded(g)

        def hidden(r):
            v = pre_ref[ds, slab(r)]
            sig = sigmoid(v)
            act = v * sig
            return rounded(act), sig + act * (1.0 - sig)

        strip = grad_conv(CS - 1, 2)
        tap = [None] * 9
        state = {}
        gh = {}
        for s in range(ROWS + 2):
            g = grad_conv(s, 0 if s == 0 else 1 if s == ROWS + 1 else None)
            gl, gr = neighbours(g, strip, s + 1, first, last)
            for a in (-1, 0, 1):
                r = s + a - 1
                if 0 <= r < ROWS:
                    if r not in state:
                        state[r] = hidden(r)
                    h = state[r][0]
                    t = 3 * (a + 1)
                    term = k[t] * gr + k[t + 1] * g + k[t + 2] * gl
                    gh[r] = term if r not in gh else gh[r] + term
                    for c, v in enumerate((gr, g, gl)):
                        tap[t + c] = h * v if tap[t + c] is None else tap[t + c] + h * v
            r = s - 2
            if 0 <= r:
                gpre_s[ds, slab(r)] = gh.pop(r) * state.pop(r)[1]
        total = jnp.zeros((SUB, LANES), F32)
        for t in range(9):
            total = jnp.where(lane == t, lane_sum(tap[t]), total)
        acc_s[ds, :] = total
        return carry

    lax.fori_loop(0, EB // SUB, body, 0)
    gated = gated_s[...].astype(BF16)
    gpre = gpre_s[...].astype(BF16)
    wproj = lax.dot_general(cot_s[:, slab(1, ROWS)], gated, NT, preferred_element_type=F32)
    wexp = lax.dot_general(scaled_s[...], gpre, NT, preferred_element_type=F32)
    for n in range(EB // LANES):
        wproj_out[n * CH : (n + 1) * CH, :] = wproj[:, n * LANES : (n + 1) * LANES]
        wexp_out[n * CH : (n + 1) * CH, :] = wexp[:, n * LANES : (n + 1) * LANES]
        taps_out[:, n * LANES : (n + 1) * LANES] = acc_s[n * LANES : (n + 1) * LANES, :].T[:9]
    proj_s[...] += jnp.dot(wprojt_ref[...], gated, preferred_element_type=F32)
    gs_s[...] += jnp.dot(wexp_ref[...], gpre, preferred_element_type=F32)

    @pl.when(step == STEPS - 1)
    def _():
        gain = gain_ref[...]
        ggain = jnp.zeros((CH, LANES), F32)
        for r in range(ROWS):
            x = x_ref[r].astype(F32)
            out_out[r] = (x + proj_s[:, slab(r)]).astype(BF16)
            inverse = inv_s[r : r + 1, :]
            normed = x * inverse
            gs = gs_s[:, slab(r)]
            prod = gs * normed
            ggain = ggain + prod
            mean = jnp.sum(prod * gain, axis=0, keepdims=True) / CH
            gin = inverse * (gs * gain - normed * mean) + c_ref[r].astype(F32)
            gin_out[r] = gin.astype(BF16)
        gain_out[...] = lane_sum(ggain)


def shape(*dims, dtype=F32):
    return jax.ShapeDtypeStruct(dims, dtype)


def full(*dims):
    return pl.BlockSpec(dims, lambda j: (0,) * len(dims))


def params(mib, grid=True):
    return pltpu.CompilerParams(
        dimension_semantics=("arbitrary",) if grid else None, vmem_limit_bytes=mib * 1024 * 1024
    )


def gathered(block, axes, count):
    return lax.all_to_all(
        jnp.broadcast_to(block[None], (count,) + block.shape), axes, 0, 0, tiled=True
    )


def exponent(v):
    return jnp.ceil(jnp.log2(jnp.maximum(jnp.max(jnp.abs(v)), 1e-30)))


def local(inputs, norm_gain, w_expand, kernel, w_squeeze, w_excite, w_project, cotangent):
    nrow, ncol = lax.axis_size("row"), lax.axis_size("col")
    row, col = lax.axis_index("row"), lax.axis_index("col")
    x = inputs[0].transpose(1, 0, 2)
    c = cotangent[0].transpose(1, 0, 2)
    fwd_row = [(i, i + 1) for i in range(nrow - 1)]
    bwd_row = [(i + 1, i) for i in range(nrow - 1)]
    fwd_col = [(i, i + 1) for i in range(ncol - 1)]
    bwd_col = [(i + 1, i) for i in range(ncol - 1)]
    top = lax.ppermute(jnp.concatenate([x[6:8], c[7:8]], axis=0), "row", fwd_row)
    bot = lax.ppermute(jnp.concatenate([x[0:2], c[0:1]], axis=0), "row", bwd_row)
    own = pl.pallas_call(
        strip_kernel,
        out_shape=shape(CH, LANES, dtype=BF16),
        compiler_params=params(8, False),
        name="strip",
    )(x, c, top, bot)
    left = lax.ppermute(own, "col", fwd_col)
    right = lax.ppermute(own, "col", bwd_col)

    lane = jnp.arange(LANES)
    line, pos = lane // 8, lane % 8
    top_ok, bot_ok = row > 0, row < nrow - 1
    strip_ok = ((pos == 3) & (col > 0)) | ((pos == 2) & (col < ncol - 1))
    strip_ok &= ((line > 1) | top_ok) & ((line < ROWS + 2) | bot_ok)
    mask = jnp.stack(
        [jnp.broadcast_to(top_ok, (LANES,)), jnp.broadcast_to(bot_ok, (LANES,)), strip_ok]
        + [jnp.zeros((LANES,), bool)] * 5
    ).astype(F32)
    gain = norm_gain[:, None]
    spread = jnp.broadcast_to(kernel[:, :, None], (EX, 9, LANES)).reshape(EX, 9 * LANES)
    wexpt, wprojt = w_expand.T, w_project.T
    halo = full(3, CH, LANES)
    tile = full(ROWS, CH, LANES)
    edge = full(CH, LANES)
    chunk_rows = lambda width: pl.BlockSpec((EB, width), lambda j: (j, 0))
    chunk_cols = pl.BlockSpec((CH, EB), lambda j: (0, j))
    pre, conv, sums = pl.pallas_call(
        forward_kernel,
        grid=(STEPS,),
        in_specs=[tile, tile, halo, halo, edge, edge, edge, full(CH, 1),
                  chunk_rows(CH), chunk_rows(9 * LANES), chunk_rows(CH)],
        out_specs=[chunk_rows(ROWS * LANES), chunk_rows(CS * LANES),
                   pl.BlockSpec((EB // LANES, 2, LANES), lambda j: (j, 0, 0))],
        out_shape=[shape(EX, ROWS * LANES), shape(EX, CS * LANES), shape(BLOCKS, 2, LANES)],
        scratch_shapes=[
            pltpu.VMEM((CH, XS * LANES), BF16),
            pltpu.VMEM((CH, ROWS * LANES), BF16),
            pltpu.VMEM((EB, (XS - ROWS) * LANES), F32),
            pltpu.VMEM((EB, ROWS * LANES), F32),
            pltpu.VMEM((EB, LANES), F32),
        ],
        compiler_params=params(20),
        name="forward",
    )(x, c, top, bot, own, left, right, gain, wexpt, spread, w_project)

    exc, gp, vec = pl.pallas_call(
        squeeze_kernel,
        out_shape=[shape(EX, LANES), shape(EX, LANES), shape(16, LANES)],
        compiler_params=params(8, False),
        name="squeeze",
    )(gathered(sums.reshape(2 * BLOCKS, LANES), RC, 32), w_squeeze, w_excite)

    out, gin, ggain, wexp, wproj, taps = pl.pallas_call(
        backward_kernel,
        grid=(STEPS,),
        in_specs=[tile, tile, halo, halo, edge, edge, full(CH, 1), full(8, LANES),
                  chunk_rows(ROWS * LANES), chunk_rows(CS * LANES), chunk_rows(LANES),
                  chunk_rows(LANES), chunk_rows(9 * LANES), chunk_cols, chunk_rows(CH), chunk_cols],
        out_specs=[tile, tile, full(CH, 1), pl.BlockSpec((CH * EB // LANES, LANES), lambda j: (j, 0)),
                   pl.BlockSpec((CH * EB // LANES, LANES), lambda j: (j, 0)),
                   pl.BlockSpec((9, EB), lambda j: (0, j))],
        out_shape=[shape(ROWS, CH, LANES, dtype=BF16), shape(ROWS, CH, LANES, dtype=BF16),
                   shape(CH, 1), shape(BLOCKS * CH, LANES), shape(BLOCKS * CH, LANES), shape(9, EX)],
        scratch_shapes=[
            pltpu.VMEM((CH, ROWS * LANES), BF16),
            pltpu.VMEM((CH, CS * LANES), BF16),
            pltpu.VMEM((ROWS, LANES), F32),
            pltpu.VMEM((EB, CS * LANES), F32),
            pltpu.VMEM((EB, ROWS * LANES), F32),
            pltpu.VMEM((EB, ROWS * LANES), F32),
            pltpu.VMEM((CH, ROWS * LANES), F32),
            pltpu.VMEM((CH, ROWS * LANES), F32),
            pltpu.VMEM((EB, LANES), F32),
        ],
        compiler_params=params(26),
        name="backward",
    )(x, c, top, bot, left, right, gain, mask, pre, conv, exc, gp, spread, w_expand, w_project,
      wprojt)

    big = jnp.concatenate([wexp, wproj], axis=0).reshape(32, 72, 128)
    small = jnp.concatenate(
        [taps.reshape(6912), ggain[:, 0], jnp.zeros((1088,), F32)]
    ).reshape(32, 2, 128)
    packed = jnp.concatenate([big, small, jnp.zeros((32, 6, 128), F32)], axis=1)
    mine = jnp.sum(lax.all_to_all(packed, RC, 0, 0, tiled=True), axis=0)
    shared = gathered(jnp.concatenate([mine, vec], axis=0), "dp", 8)
    total = jnp.sum(shared[:, :80], axis=0)
    vecs = shared[:, 80:].reshape(8, 2048)
    grad_wexc = jnp.einsum("bs,be->se", vecs[:, 1536:1584], vecs[:, 768:1536], precision=HIGH)
    grad_wsq = jnp.einsum("be,bs->es", vecs[:, :768], vecs[:, 1664:1712], precision=HIGH)
    e_big, e_small = exponent(total[:72]), exponent(total[72:74])
    send = jnp.concatenate(
        [
            total[:72] * jnp.exp2(-e_big),
            total[72:74] * jnp.exp2(-e_small),
            jnp.full((3, 128), e_big),
            jnp.full((3, 128), e_small),
        ],
        axis=0,
    ).astype(jnp.float16)
    every = gathered(send, RC, 32).astype(F32)
    big = (every[:, :72] * jnp.exp2(every[:, 74:75])).reshape(2, BLOCKS, CH, LANES)
    small = (every[:, 72:74] * jnp.exp2(every[:, 77:78])).reshape(8192)
    return (
        out.transpose(1, 0, 2)[None],
        gin.transpose(1, 0, 2)[None],
        small[6912:7104],
        big[0].transpose(1, 0, 2).reshape(CH, EX),
        small[:6912].reshape(9, 768).T,
        grad_wsq,
        grad_wexc,
        big[1].transpose(0, 2, 1).reshape(EX, CH),
    )


def solution(mesh):
    placed = (
        P("dp", None, "row", "col"),
        P(),
        P(),
        P(),
        P(),
        P(),
        P(),
        P("dp", None, "row", "col"),
    )
    return jax.shard_map(
        local,
        mesh=mesh,
        in_specs=placed,
        out_specs=(
            P("dp", None, "row", "col"),
            P("dp", None, "row", "col"),
            P(),
            P(),
            P(),
            P(),
            P(),
            P(),
        ),
        check_vma=False,
    )
```

```python
import functools

import jax
import jax.numpy as jnp
from jax import lax
from jax.experimental import pallas as pl
from jax.experimental.pallas import tpu as pltpu
from jax.sharding import PartitionSpec as P

EPS = 1e-06
HIGH = lax.Precision.HIGHEST
RC = ("row", "col")
F32, BF16 = jnp.float32, jnp.bfloat16
CH, EX, SQ = 192, 768, 48
ROWS, LANES = 8, 128
EB = 256
SUB = 16
STEPS = EX // EB
BLOCKS = EX // LANES
PARTS, PACK = 32, 80
VMEM = 60 * 1024 * 1024
XS = ROWS + 5
CS = ROWS + 3
NT = (((1,), (1,)), ((), ()))
TN = (((0,), (0,)), ((), ()))


def lane_iota(rows):
    return lax.broadcasted_iota(jnp.int32, (rows, LANES), 1)


def rounded(v):
    return v.astype(BF16).astype(F32)


def tn_dot(a, b):
    return lax.dot_general(a, b, TN, preferred_element_type=F32)


def lane_sum(v):
    return jnp.sum(v, axis=1, keepdims=True)


def sigmoid(v):
    return 0.5 + 0.5 * jnp.tanh(0.5 * v)


def slab(s, n=1):
    return pl.ds(s * LANES, n * LANES)


def strip_kernel(x_ref, c_ref, top_ref, bot_ref, out_ref):
    lane = lane_iota(CH)
    total = jnp.zeros((CH, LANES), F32)
    for rr in range(ROWS + 4):
        if rr < 2:
            v = top_ref[rr]
        elif rr < ROWS + 2:
            v = x_ref[rr - 2]
        else:
            v = bot_ref[rr - ROWS - 2]
        v = pltpu.roll(v.astype(F32), (8 * rr + 2) % LANES, 1)
        total = jnp.where((lane >= 8 * rr) & (lane < 8 * rr + 4), v, total)
        if 1 <= rr <= ROWS + 2:
            if rr == 1:
                v = top_ref[2]
            elif rr == ROWS + 2:
                v = bot_ref[2]
            else:
                v = c_ref[rr - 2]
            v = pltpu.roll(v.astype(F32), (8 * rr + 5) % LANES, 1)
            total = jnp.where((lane >= 8 * rr + 4) & (lane < 8 * rr + 6), v, total)
    out_ref[...] = total.astype(BF16)


def input_strip(own_ref, left_ref, right_ref):
    own, left, right = (r[...].astype(F32) for r in (own_ref, left_ref, right_ref))
    pos = lane_iota(CH) % 8
    value = jnp.where(pos == 0, pltpu.roll(own, LANES - 1, 1), 0.0)
    value = jnp.where(pos == 1, pltpu.roll(left, 1, 1), value)
    value = jnp.where(pos == 2, right, value)
    value = jnp.where(pos == 3, pltpu.roll(left, 2, 1), value)
    value = jnp.where(pos == 4, pltpu.roll(right, 1, 1), value)
    return jnp.where(pos == 5, pltpu.roll(own, 3, 1), value)


def cotangent_strip(left_ref, right_ref):
    left, right = (r[...].astype(F32) for r in (left_ref, right_ref))
    pos = lane_iota(CH) % 8
    value = jnp.where(pos == 3, pltpu.roll(left, LANES - 1, 1), 0.0)
    return jnp.where(pos == 2, pltpu.roll(right, LANES - 3, 1), value)


def neighbours(v, strip, rr, first, last):
    edge = pltpu.roll(strip, (LANES - 8 * rr - 3) % LANES, 1)
    left = jnp.where(first, edge, pltpu.roll(v, 1, 1))
    right = jnp.where(last, edge, pltpu.roll(v, LANES - 1, 1))
    return left, right


def forward_kernel(
    x_ref, c_ref, top_ref, bot_ref, own_ref, left_ref, right_ref, gain_ref, wexp_ref, taps_ref,
    wprojt_ref, pre_out, conv_out, sums_out, scaled_s, cot_s, pre_s, gg_s, acc_s,
):
    @pl.when(pl.program_id(0) == 0)
    def _():
        gain = gain_ref[...]
        for s in range(XS):
            if s < 2:
                x = top_ref[s].astype(F32)
            elif s < ROWS + 2:
                x = x_ref[s - 2].astype(F32)
            elif s < ROWS + 4:
                x = bot_ref[s - ROWS - 2].astype(F32)
            else:
                x = input_strip(own_ref, left_ref, right_ref)
            inverse = lax.rsqrt(jnp.sum(x * x, axis=0, keepdims=True) / CH + EPS)
            place = s - 2 if 2 <= s < ROWS + 2 else s + ROWS if s < 2 else s
            scaled_s[:, slab(place)] = (x * inverse * gain).astype(BF16)
        for r in range(ROWS):
            cot_s[:, slab(r)] = c_ref[r]

    wexp = wexp_ref[...]
    pre_out[...] = tn_dot(wexp, scaled_s[:, slab(0, ROWS)])
    pre_s[...] = tn_dot(wexp, scaled_s[:, slab(ROWS, XS - ROWS)])
    gg_s[...] = tn_dot(wprojt_ref[...], cot_s[...])
    lane = lane_iota(SUB)
    first, last = lane == 0, lane == LANES - 1

    def body(i, carry):
        ds = pl.ds(pl.multiple_of(i * SUB, SUB), SUB)
        k = [jnp.broadcast_to(taps_ref[ds, t : t + 1], (SUB, LANES)) for t in range(9)]

        def hidden(s):
            if 2 <= s < ROWS + 2:
                v = pre_out[ds, slab(s - 2)]
            else:
                v = pre_s[ds, slab(s if s < 2 else s - ROWS)]
            v = 0.5 * v
            return rounded(v + v * jnp.tanh(v))

        strip = hidden(XS - 1)
        acc = [None] * (ROWS + 4)
        for rr in range(ROWS + 4):
            h = hidden(rr)
            hl, hr = neighbours(h, strip, rr, first, last)
            for a in (-1, 0, 1):
                o = rr - a
                if 1 <= o <= ROWS + 2:
                    t = 3 * (a + 1)
                    term = k[t] * hl + k[t + 1] * h + k[t + 2] * hr
                    acc[o] = term if acc[o] is None else acc[o] + term
        pooled = jnp.zeros((SUB, LANES), F32)
        gexc = jnp.zeros((SUB, LANES), F32)
        for o in range(1, ROWS + 3):
            v = acc[o]
            conv_out[ds, slab(o - 1)] = v
            if 2 <= o <= ROWS + 1:
                act = v * sigmoid(v)
                pooled = pooled + act
                gexc = gexc + act * gg_s[ds, slab(o - 2)]
        edge = None
        for a in (-1, 0, 1):
            for c in (-1, 0, 1):
                shift = (-(8 * a + 2 * c)) % LANES
                term = k[3 * (a + 1) + c + 1] * (pltpu.roll(strip, shift, 1) if shift else strip)
                edge = term if edge is None else edge + term
        conv_out[ds, slab(CS - 1)] = edge
        acc_s[ds, :] = jnp.where(first, lane_sum(pooled), lane_sum(gexc))
        return carry

    lax.fori_loop(0, EB // SUB, body, 0)
    for n in range(EB // LANES):
        sums_out[n] = acc_s[n * LANES : (n + 1) * LANES, :].T[:2]


def squeeze_kernel(parts_ref, wsq_ref, wexc_ref, exc_out, gp_out, vec_out):
    pixels = 32768.0
    total = jnp.sum(parts_ref[...], axis=0)
    pooled = jnp.concatenate([total[2 * j : 2 * j + 1] for j in range(BLOCKS)], axis=1) / pixels
    gexc = jnp.concatenate([total[2 * j + 1 : 2 * j + 2] for j in range(BLOCKS)], axis=1)
    pooled = jnp.broadcast_to(pooled, (8, EX))
    gexc = jnp.broadcast_to(gexc, (8, EX))
    wsq, wexc = wsq_ref[...], wexc_ref[...]
    spre = lax.dot_general(pooled, wsq, NT, precision=HIGH, preferred_element_type=F32)
    sig = jax.nn.sigmoid(spre)
    squeezed = spre * sig
    epre = jnp.dot(squeezed, wexc, precision=HIGH, preferred_element_type=F32)
    excite = jax.nn.sigmoid(epre)
    gepre = gexc * excite * (1.0 - excite)
    gspre = lax.dot_general(gepre, wexc, NT, precision=HIGH, preferred_element_type=F32)
    gspre = gspre * (sig * (1.0 + spre * (1.0 - sig)))
    gpool = jnp.dot(gspre, wsq, precision=HIGH, preferred_element_type=F32)
    gpool = gpool / pixels
    vec_out[...] = jnp.zeros((16, LANES), F32)
    for j in range(BLOCKS):
        cols = slice(j * LANES, (j + 1) * LANES)
        exc_out[cols, :] = jnp.broadcast_to(excite[:1, cols], (LANES, LANES)).T
        gp_out[cols, :] = jnp.broadcast_to(gpool[:1, cols], (LANES, LANES)).T
        vec_out[j : j + 1, :] = pooled[:1, cols]
        vec_out[BLOCKS + j : BLOCKS + j + 1, :] = gepre[:1, cols]
    vec_out[12:13, :SQ] = squeezed[:1]
    vec_out[13:14, :SQ] = gspre[:1]


def big_rows(group):
    return pl.ds(pl.multiple_of(PACK * (group // 3) + 24 * (group % 3), 8), 24)


def small_row(row):
    return pl.ds(PACK * (row // 2) + 72 + row % 2, 1)


def backward_kernel(
    x_ref, c_ref, top_ref, bot_ref, left_ref, right_ref, gain_ref, mask_ref, pre_ref, conv_ref,
    exc_ref, gp_ref, taps_ref, wexp_ref, wprojt_ref,
    out_out, gin_out, packed_out,
    scaled_s, cot_s, inv_s, gg_s, gated_s, gpre_s, proj_s, gs_s, acc_s,
):
    step = pl.program_id(0)

    @pl.when(step == 0)
    def _():
        gain = gain_ref[...]
        for r in range(ROWS):
            x = x_ref[r].astype(F32)
            inverse = lax.rsqrt(jnp.sum(x * x, axis=0, keepdims=True) / CH + EPS)
            inv_s[r : r + 1, :] = inverse
            scaled_s[:, slab(r)] = (x * inverse * gain).astype(BF16)
            cot_s[:, slab(r + 1)] = c_ref[r]
        cot_s[:, slab(0)] = top_ref[2]
        cot_s[:, slab(ROWS + 1)] = bot_ref[2]
        cot_s[:, slab(CS - 1)] = cotangent_strip(left_ref, right_ref).astype(BF16)
        proj_s[...] = jnp.zeros_like(proj_s)
        gs_s[...] = jnp.zeros_like(gs_s)
        for d in range(PARTS):
            packed_out[d * PACK + 72 : (d + 1) * PACK, :] = jnp.zeros((8, LANES), F32)

    gg_s[...] = tn_dot(wprojt_ref[...], cot_s[...])
    lane = lane_iota(SUB)
    first, last = lane == 0, lane == LANES - 1

    def body(i, carry):
        ds = pl.ds(pl.multiple_of(i * SUB, SUB), SUB)
        k = [jnp.broadcast_to(taps_ref[ds, t : t + 1], (SUB, LANES)) for t in range(9)]
        exc, gp = exc_ref[ds, :], gp_ref[ds, :]

        def grad_conv(s, mask):
            v = conv_ref[ds, slab(s)]
            sig = sigmoid(v)
            act = v * sig
            if 1 <= s <= ROWS:
                gated_s[ds, slab(s - 1)] = act * exc
            g = (gg_s[ds, slab(s)] * exc + gp) * (sig + act * (1.0 - sig))
            if mask is not None:
                g = jnp.where(mask_ref[mask : mask + 1, :] > 0.5, g, 0.0)
            return rounded(g)

        def hidden(r):
            v = pre_ref[ds, slab(r)]
            sig = sigmoid(v)
            act = v * sig
            return rounded(act), sig + act * (1.0 - sig)

        strip = grad_conv(CS - 1, 2)
        tap = [None] * 9
        state = {}
        gh = {}
        for s in range(ROWS + 2):
            g = grad_conv(s, 0 if s == 0 else 1 if s == ROWS + 1 else None)
            gl, gr = neighbours(g, strip, s + 1, first, last)
            for a in (-1, 0, 1):
                r = s + a - 1
                if 0 <= r < ROWS:
                    if r not in state:
                        state[r] = hidden(r)
                    h = state[r][0]
                    t = 3 * (a + 1)
                    term = k[t] * gr + k[t + 1] * g + k[t + 2] * gl
                    gh[r] = term if r not in gh else gh[r] + term
                    for c, v in enumerate((gr, g, gl)):
                        tap[t + c] = h * v if tap[t + c] is None else tap[t + c] + h * v
            r = s - 2
            if 0 <= r:
                gpre_s[ds, slab(r)] = gh.pop(r) * state.pop(r)[1]
        total = jnp.zeros((SUB, LANES), F32)
        for t in range(9):
            total = jnp.where(lane == t, lane_sum(tap[t]), total)
        acc_s[ds, :] = total
        return carry

    lax.fori_loop(0, EB // SUB, body, 0)
    gated = gated_s[...].astype(BF16)
    gpre = gpre_s[...].astype(BF16)
    wproj = lax.dot_general(cot_s[:, slab(1, ROWS)], gated, NT, preferred_element_type=F32)
    wexp = lax.dot_general(scaled_s[...], gpre, NT, preferred_element_type=F32)
    groups = CH // 24
    for n in range(EB // LANES):
        block = step * (EB // LANES) + n
        for w, which in ((wexp, 0), (wproj, BLOCKS * groups)):
            for i in range(groups):
                packed_out[big_rows(which + block * groups + i), :] = w[
                    24 * i : 24 * i + 24, n * LANES : (n + 1) * LANES
                ]
        taps = acc_s[n * LANES : (n + 1) * LANES, :].T
        for t in range(9):
            packed_out[small_row(BLOCKS * t + block), :] = taps[t : t + 1]
    proj_s[...] += jnp.dot(wprojt_ref[...], gated, preferred_element_type=F32)
    gs_s[...] += jnp.dot(wexp_ref[...], gpre, preferred_element_type=F32)

    @pl.when(step == STEPS - 1)
    def _():
        gain = gain_ref[...]
        ggain = jnp.zeros((CH, LANES), F32)
        for r in range(ROWS):
            x = x_ref[r].astype(F32)
            out_out[r] = (x + proj_s[:, slab(r)]).astype(BF16)
            inverse = inv_s[r : r + 1, :]
            normed = x * inverse
            gs = gs_s[:, slab(r)]
            prod = gs * normed
            ggain = ggain + prod
            mean = jnp.sum(prod * gain, axis=0, keepdims=True) / CH
            gin = inverse * (gs * gain - normed * mean) + c_ref[r].astype(F32)
            gin_out[r] = gin.astype(BF16)
        sums = jnp.broadcast_to(lane_sum(ggain), (CH, LANES)).T[:1]
        packed_out[small_row(9 * BLOCKS), :] = sums[:, :LANES]
        packed_out[pl.ds(9 * BLOCKS // 2 * PACK + 73, 1), : CH - LANES] = sums[:, LANES:]


def shape(*dims, dtype=F32):
    return jax.ShapeDtypeStruct(dims, dtype)


def full(*dims):
    return pl.BlockSpec(dims, lambda j: (0,) * len(dims))


def params(grid=True):
    return pltpu.CompilerParams(
        dimension_semantics=("arbitrary",) if grid else None, vmem_limit_bytes=VMEM
    )


def gathered(block, axes, count):
    return lax.all_to_all(
        jnp.broadcast_to(block[None], (count,) + block.shape), axes, 0, 0, tiled=True
    )


def exponent(v):
    return jnp.ceil(jnp.log2(jnp.maximum(jnp.max(jnp.abs(v)), 1e-30)))


def local(inputs, norm_gain, w_expand, kernel, w_squeeze, w_excite, w_project, cotangent):
    nrow, ncol = lax.axis_size("row"), lax.axis_size("col")
    row, col = lax.axis_index("row"), lax.axis_index("col")
    x = inputs[0].transpose(1, 0, 2)
    c = cotangent[0].transpose(1, 0, 2)
    fwd_row = [(i, i + 1) for i in range(nrow - 1)]
    bwd_row = [(i + 1, i) for i in range(nrow - 1)]
    fwd_col = [(i, i + 1) for i in range(ncol - 1)]
    bwd_col = [(i + 1, i) for i in range(ncol - 1)]
    top = lax.ppermute(jnp.concatenate([x[6:8], c[7:8]], axis=0), "row", fwd_row)
    bot = lax.ppermute(jnp.concatenate([x[0:2], c[0:1]], axis=0), "row", bwd_row)
    own = pl.pallas_call(
        strip_kernel,
        out_shape=shape(CH, LANES, dtype=BF16),
        compiler_params=params(False),
        name="strip",
    )(x, c, top, bot)
    left = lax.ppermute(own, "col", fwd_col)
    right = lax.ppermute(own, "col", bwd_col)

    line = lax.broadcasted_iota(jnp.int32, (8, LANES), 1) // 8
    pos = lax.broadcasted_iota(jnp.int32, (8, LANES), 1) % 8
    kind = lax.broadcasted_iota(jnp.int32, (8, LANES), 0)
    top_ok, bot_ok = row > 0, row < nrow - 1
    strip_ok = ((pos == 3) & (col > 0)) | ((pos == 2) & (col < ncol - 1))
    strip_ok &= ((line > 1) | top_ok) & ((line < ROWS + 2) | bot_ok)
    mask = ((kind == 0) & top_ok) | ((kind == 1) & bot_ok) | ((kind == 2) & strip_ok)
    mask = mask.astype(F32)
    gain = norm_gain[:, None]
    wprojt = w_project.T
    halo = full(3, CH, LANES)
    tile = full(ROWS, CH, LANES)
    edge = full(CH, LANES)
    chunk_rows = lambda width: pl.BlockSpec((EB, width), lambda j: (j, 0))
    chunk_cols = pl.BlockSpec((CH, EB), lambda j: (0, j))
    pre, conv, sums = pl.pallas_call(
        forward_kernel,
        grid=(STEPS,),
        in_specs=[tile, tile, halo, halo, edge, edge, edge, full(CH, 1),
                  chunk_cols, chunk_rows(9), chunk_cols],
        out_specs=[chunk_rows(ROWS * LANES), chunk_rows(CS * LANES),
                   pl.BlockSpec((EB // LANES, 2, LANES), lambda j: (j, 0, 0))],
        out_shape=[shape(EX, ROWS * LANES), shape(EX, CS * LANES), shape(BLOCKS, 2, LANES)],
        scratch_shapes=[
            pltpu.VMEM((CH, XS * LANES), BF16),
            pltpu.VMEM((CH, ROWS * LANES), BF16),
            pltpu.VMEM((EB, (XS - ROWS) * LANES), F32),
            pltpu.VMEM((EB, ROWS * LANES), F32),
            pltpu.VMEM((EB, LANES), F32),
        ],
        compiler_params=params(),
        name="forward",
    )(x, c, top, bot, own, left, right, gain, w_expand, kernel, wprojt)

    exc, gp, vec = pl.pallas_call(
        squeeze_kernel,
        out_shape=[shape(EX, LANES), shape(EX, LANES), shape(16, LANES)],
        compiler_params=params(False),
        name="squeeze",
    )(gathered(sums.reshape(2 * BLOCKS, LANES), RC, 32), w_squeeze.T, w_excite)

    out, gin, packed = pl.pallas_call(
        backward_kernel,
        grid=(STEPS,),
        in_specs=[tile, tile, halo, halo, edge, edge, full(CH, 1), full(8, LANES),
                  chunk_rows(ROWS * LANES), chunk_rows(CS * LANES), chunk_rows(LANES),
                  chunk_rows(LANES), chunk_rows(9), chunk_cols, chunk_cols],
        out_specs=[tile, tile, full(PARTS * PACK, LANES)],
        out_shape=[shape(ROWS, CH, LANES, dtype=BF16), shape(ROWS, CH, LANES, dtype=BF16),
                   shape(PARTS * PACK, LANES)],
        scratch_shapes=[
            pltpu.VMEM((CH, ROWS * LANES), BF16),
            pltpu.VMEM((CH, CS * LANES), BF16),
            pltpu.VMEM((ROWS, LANES), F32),
            pltpu.VMEM((EB, CS * LANES), F32),
            pltpu.VMEM((EB, ROWS * LANES), F32),
            pltpu.VMEM((EB, ROWS * LANES), F32),
            pltpu.VMEM((CH, ROWS * LANES), F32),
            pltpu.VMEM((CH, ROWS * LANES), F32),
            pltpu.VMEM((EB, LANES), F32),
        ],
        compiler_params=params(),
        name="backward",
    )(x, c, top, bot, left, right, gain, mask, pre, conv, exc, gp, kernel, w_expand, wprojt)

    packed = packed.reshape(PARTS, PACK, LANES)
    mine = jnp.sum(lax.all_to_all(packed, RC, 0, 0, tiled=True), axis=0)
    shared = gathered(jnp.concatenate([mine, vec], axis=0), "dp", 8)
    total = jnp.sum(shared[:, :80], axis=0)
    vecs = shared[:, 80:].reshape(8, 2048)
    grad_wexc = jnp.einsum("bs,be->se", vecs[:, 1536:1584], vecs[:, 768:1536], precision=HIGH)
    grad_wsq = jnp.einsum("be,bs->es", vecs[:, :768], vecs[:, 1664:1712], precision=HIGH)
    e_big, e_small = exponent(total[:72]), exponent(total[72:74])
    send = jnp.concatenate(
        [
            total[:72] * jnp.exp2(-e_big),
            total[72:74] * jnp.exp2(-e_small),
            jnp.full((3, 128), e_big),
            jnp.full((3, 128), e_small),
        ],
        axis=0,
    ).astype(jnp.float16)
    every = gathered(send, RC, 32).astype(F32)
    big = (every[:, :72] * jnp.exp2(every[:, 74:75])).reshape(2, BLOCKS, CH, LANES)
    small = (every[:, 72:74] * jnp.exp2(every[:, 77:78])).reshape(8192)
    return (
        out.transpose(1, 0, 2)[None],
        gin.transpose(1, 0, 2)[None],
        small[6912:7104],
        big[0].transpose(1, 0, 2).reshape(CH, EX),
        small[:6912].reshape(9, 768).T,
        grad_wsq,
        grad_wexc,
        big[1].transpose(0, 2, 1).reshape(EX, CH),
    )


def solution(mesh):
    placed = (
        P("dp", None, "row", "col"),
        P(),
        P(),
        P(),
        P(),
        P(),
        P(),
        P("dp", None, "row", "col"),
    )
    return jax.shard_map(
        local,
        mesh=mesh,
        in_specs=placed,
        out_specs=(
            P("dp", None, "row", "col"),
            P("dp", None, "row", "col"),
            P(),
            P(),
            P(),
            P(),
            P(),
            P(),
        ),
        check_vma=False,
    )
```

```python
import jax
import jax.numpy as jnp
from jax import lax
from jax.experimental import pallas as pl
from jax.experimental.pallas import tpu as pltpu
from jax.sharding import PartitionSpec as P

EPS = 1e-06
HIGH = lax.Precision.HIGHEST
RC = ("row", "col")
F32, BF16 = jnp.float32, jnp.bfloat16
CH, EX, SQ = 192, 768, 48
ROWS, LANES = 8, 128
EB = 256
SUB = 16
STEPS = EX // EB
BLOCKS = EX // LANES
PARTS, PACK = 32, 80
VMEM = 60 * 1024 * 1024
CHIPS = [[2 * q + core for q in range(PARTS // 2)] for core in range(2)]
XS = ROWS + 5
CS = ROWS + 3
NT = (((1,), (1,)), ((), ()))
TN = (((0,), (0,)), ((), ()))


def lane_iota(rows):
    return lax.broadcasted_iota(jnp.int32, (rows, LANES), 1)


def rounded(v):
    return v.astype(BF16).astype(F32)


def tn_dot(a, b):
    return lax.dot_general(a, b, TN, preferred_element_type=F32)


def lane_sum(v):
    return jnp.sum(v, axis=1, keepdims=True)


def sigmoid(v):
    return 0.5 + 0.5 * jnp.tanh(0.5 * v)


def slab(s, n=1):
    return pl.ds(s * LANES, n * LANES)


def strip_kernel(x_ref, c_ref, top_ref, bot_ref, out_ref):
    lane = lane_iota(CH)
    total = jnp.zeros((CH, LANES), F32)
    for rr in range(ROWS + 4):
        if rr < 2:
            v = top_ref[rr]
        elif rr < ROWS + 2:
            v = x_ref[rr - 2]
        else:
            v = bot_ref[rr - ROWS - 2]
        v = pltpu.roll(v.astype(F32), (8 * rr + 2) % LANES, 1)
        total = jnp.where((lane >= 8 * rr) & (lane < 8 * rr + 4), v, total)
        if 1 <= rr <= ROWS + 2:
            if rr == 1:
                v = top_ref[2]
            elif rr == ROWS + 2:
                v = bot_ref[2]
            else:
                v = c_ref[rr - 2]
            v = pltpu.roll(v.astype(F32), (8 * rr + 5) % LANES, 1)
            total = jnp.where((lane >= 8 * rr + 4) & (lane < 8 * rr + 6), v, total)
    out_ref[...] = total.astype(BF16)


def input_strip(own_ref, left_ref, right_ref):
    own, left, right = (r[...].astype(F32) for r in (own_ref, left_ref, right_ref))
    pos = lane_iota(CH) % 8
    value = jnp.where(pos == 0, pltpu.roll(own, LANES - 1, 1), 0.0)
    value = jnp.where(pos == 1, pltpu.roll(left, 1, 1), value)
    value = jnp.where(pos == 2, right, value)
    value = jnp.where(pos == 3, pltpu.roll(left, 2, 1), value)
    value = jnp.where(pos == 4, pltpu.roll(right, 1, 1), value)
    return jnp.where(pos == 5, pltpu.roll(own, 3, 1), value)


def cotangent_strip(left_ref, right_ref):
    left, right = (r[...].astype(F32) for r in (left_ref, right_ref))
    pos = lane_iota(CH) % 8
    value = jnp.where(pos == 3, pltpu.roll(left, LANES - 1, 1), 0.0)
    return jnp.where(pos == 2, pltpu.roll(right, LANES - 3, 1), value)


def neighbours(v, strip, rr, first, last):
    edge = pltpu.roll(strip, (LANES - 8 * rr - 3) % LANES, 1)
    left = jnp.where(first, edge, pltpu.roll(v, 1, 1))
    right = jnp.where(last, edge, pltpu.roll(v, LANES - 1, 1))
    return left, right


def spread_gain(gain_ref):
    return jnp.broadcast_to(gain_ref[...], (LANES, CH)).T


def spread_taps(taps_ref, out_s):
    for n in range(EB // LANES):
        rows = slice(n * LANES, (n + 1) * LANES)
        block = jnp.concatenate([taps_ref[:, rows], jnp.zeros((7, LANES), F32)], axis=0).T
        for t in range(9):
            out_s[rows, slab(t)] = jnp.broadcast_to(block[:, t : t + 1], (LANES, LANES))


def forward_kernel(
    x_ref, c_ref, top_ref, bot_ref, own_ref, left_ref, right_ref, gain_ref, wexp_ref, taps_ref,
    wprojt_ref, pre_out, conv_out, sums_out, scaled_s, cot_s, pre_s, gg_s, taps_s, acc_s,
):
    step = pl.program_id(0)

    @pl.when(step == 0)
    def _():
        gain = spread_gain(gain_ref)
        for s in range(XS):
            if s < 2:
                x = top_ref[s].astype(F32)
            elif s < ROWS + 2:
                x = x_ref[s - 2].astype(F32)
            elif s < ROWS + 4:
                x = bot_ref[s - ROWS - 2].astype(F32)
            else:
                x = input_strip(own_ref, left_ref, right_ref)
            inverse = lax.rsqrt(jnp.sum(x * x, axis=0, keepdims=True) / CH + EPS)
            scaled_s[:, slab(s)] = (x * inverse * gain).astype(BF16)
        for r in range(ROWS):
            cot_s[:, slab(r)] = c_ref[r]
        pre_s[...] = tn_dot(wexp_ref[...], scaled_s[...])
        gg_s[...] = tn_dot(wprojt_ref[...], cot_s[...])
        sums_out[...] = jnp.zeros_like(sums_out)

    spread_taps(taps_ref, taps_s)
    base = step * EB
    lane = lane_iota(SUB)
    first, last = lane == 0, lane == LANES - 1

    def body(i, carry):
        ds = pl.ds(pl.multiple_of(i * SUB, SUB), SUB)
        whole = pl.ds(pl.multiple_of(base + i * SUB, SUB), SUB)
        k = [taps_s[ds, slab(t)] for t in range(9)]

        def hidden(s):
            v = pre_s[whole, slab(s)]
            if 2 <= s < ROWS + 2:
                pre_out[ds, slab(s - 2)] = v
            v = 0.5 * v
            return rounded(v + v * jnp.tanh(v))

        strip = hidden(XS - 1)
        acc = [None] * (ROWS + 4)
        for rr in range(ROWS + 4):
            h = hidden(rr)
            hl, hr = neighbours(h, strip, rr, first, last)
            for a in (-1, 0, 1):
                o = rr - a
                if 1 <= o <= ROWS + 2:
                    t = 3 * (a + 1)
                    term = k[t] * hl + k[t + 1] * h + k[t + 2] * hr
                    acc[o] = term if acc[o] is None else acc[o] + term
        pooled = jnp.zeros((SUB, LANES), F32)
        gexc = jnp.zeros((SUB, LANES), F32)
        for o in range(1, ROWS + 3):
            v = acc[o]
            conv_out[ds, slab(o - 1)] = v
            if 2 <= o <= ROWS + 1:
                half = 0.5 * v
                act = half + half * jnp.tanh(half)
                pooled = pooled + act
                gexc = gexc + act * gg_s[whole, slab(o - 2)]
        edge = None
        for a in (-1, 0, 1):
            for c in (-1, 0, 1):
                shift = (-(8 * a + 2 * c)) % LANES
                term = k[3 * (a + 1) + c + 1] * (pltpu.roll(strip, shift, 1) if shift else strip)
                edge = term if edge is None else edge + term
        conv_out[ds, slab(CS - 1)] = edge
        acc_s[ds, :] = jnp.where(first, lane_sum(pooled), lane_sum(gexc))
        return carry

    lax.fori_loop(0, EB // SUB, body, 0)
    for n in range(EB // LANES):
        sums_out[pl.ds(2 * (step * (EB // LANES) + n), 2), :] = (
            acc_s[n * LANES : (n + 1) * LANES, :].T[:2]
        )


def squeeze_excite(parts_ref, wsq_ref, wexc_ref, exc_s, gp_s, vec_out):
    pixels = 32768.0
    total = jnp.sum(parts_ref[...], axis=0)
    pooled = jnp.concatenate([total[2 * j : 2 * j + 1] for j in range(BLOCKS)], axis=1) / pixels
    gexc = jnp.concatenate([total[2 * j + 1 : 2 * j + 2] for j in range(BLOCKS)], axis=1)
    pooled = jnp.broadcast_to(pooled, (8, EX))
    gexc = jnp.broadcast_to(gexc, (8, EX))
    wsq, wexc = wsq_ref[...], wexc_ref[...]
    spre = lax.dot_general(pooled, wsq, NT, precision=HIGH, preferred_element_type=F32)
    sig = jax.nn.sigmoid(spre)
    squeezed = spre * sig
    epre = jnp.dot(squeezed, wexc, precision=HIGH, preferred_element_type=F32)
    excite = jax.nn.sigmoid(epre)
    gepre = gexc * excite * (1.0 - excite)
    gspre = lax.dot_general(gepre, wexc, NT, precision=HIGH, preferred_element_type=F32)
    gspre = gspre * (sig * (1.0 + spre * (1.0 - sig)))
    gpool = jnp.dot(gspre, wsq, precision=HIGH, preferred_element_type=F32)
    gpool = gpool / pixels
    vec_out[...] = jnp.zeros((16, LANES), F32)
    for j in range(BLOCKS):
        cols = slice(j * LANES, (j + 1) * LANES)
        exc_s[cols, :] = jnp.broadcast_to(excite[:1, cols], (LANES, LANES)).T
        gp_s[cols, :] = jnp.broadcast_to(gpool[:1, cols], (LANES, LANES)).T
        vec_out[j : j + 1, :] = pooled[:1, cols]
        vec_out[BLOCKS + j : BLOCKS + j + 1, :] = gepre[:1, cols]
    vec_out[12:13, :SQ] = squeezed[:1]
    vec_out[13:14, :SQ] = gspre[:1]


def backward_kernel(
    core_ref, parts_ref, wsq_ref, wexc_ref, x_ref, c_ref, top_ref, bot_ref, left_ref, right_ref,
    gain_ref, mask_ref, pre_ref, conv_ref, taps_ref, wexp_ref, wprojt_ref,
    out_out, gin_out, keep_out, send_out, vec_out,
    packed_s, exc_s, gp_s, scaled_s, cot_s, inv_s, gg_s, gated_s, gpre_s, taps_s, acc_s, tsum_s,
):
    step = pl.program_id(0)

    @pl.when(step == 0)
    def _():
        squeeze_excite(parts_ref, wsq_ref, wexc_ref, exc_s, gp_s, vec_out)
        gain = spread_gain(gain_ref)
        for r in range(ROWS):
            x = x_ref[r].astype(F32)
            inverse = lax.rsqrt(jnp.sum(x * x, axis=0, keepdims=True) / CH + EPS)
            inv_s[r : r + 1, :] = inverse
            scaled_s[:, slab(r)] = (x * inverse * gain).astype(BF16)
            cot_s[:, slab(r + 1)] = c_ref[r]
        cot_s[:, slab(0)] = top_ref[2]
        cot_s[:, slab(ROWS + 1)] = bot_ref[2]
        cot_s[:, slab(CS - 1)] = cotangent_strip(left_ref, right_ref).astype(BF16)
        gg_s[...] = tn_dot(wprojt_ref[...], cot_s[...])

    spread_taps(taps_ref, taps_s)
    base = step * EB
    lane = lane_iota(SUB)
    first, last = lane == 0, lane == LANES - 1

    def body(i, carry):
        ds = pl.ds(pl.multiple_of(i * SUB, SUB), SUB)
        whole = pl.ds(pl.multiple_of(base + i * SUB, SUB), SUB)
        k = [taps_s[ds, slab(t)] for t in range(9)]
        exc, gp = exc_s[whole, :], gp_s[whole, :]

        def grad_conv(s, mask):
            half = 0.5 * conv_ref[ds, slab(s)]
            t = jnp.tanh(half)
            act = half + half * t
            if 1 <= s <= ROWS:
                gated_s[whole, slab(s - 1)] = (act * exc).astype(BF16)
            sig = 0.5 + 0.5 * t
            g = (gg_s[whole, slab(s)] * exc + gp) * (sig + act * (1.0 - sig))
            if mask is not None:
                g = jnp.where(mask_ref[mask : mask + 1, :] > 0.5, g, 0.0)
            return rounded(g)

        def hidden(r):
            half = 0.5 * pre_ref[ds, slab(r)]
            t = jnp.tanh(half)
            act = half + half * t
            sig = 0.5 + 0.5 * t
            return rounded(act), sig + act * (1.0 - sig)

        strip = grad_conv(CS - 1, 2)
        tap = [None] * 9
        state = {}
        gh = {}
        for s in range(ROWS + 2):
            g = grad_conv(s, 0 if s == 0 else 1 if s == ROWS + 1 else None)
            gl, gr = neighbours(g, strip, s + 1, first, last)
            for a in (-1, 0, 1):
                r = s + a - 1
                if 0 <= r < ROWS:
                    if r not in state:
                        state[r] = hidden(r)
                    h = state[r][0]
                    t = 3 * (a + 1)
                    term = k[t] * gr + k[t + 1] * g + k[t + 2] * gl
                    gh[r] = term if r not in gh else gh[r] + term
                    for c, v in enumerate((gr, g, gl)):
                        tap[t + c] = h * v if tap[t + c] is None else tap[t + c] + h * v
            r = s - 2
            if 0 <= r:
                gpre_s[whole, slab(r)] = (gh.pop(r) * state.pop(r)[1]).astype(BF16)
        total = jnp.zeros((SUB, LANES), F32)
        for t in range(9):
            total = jnp.where(lane == t, lane_sum(tap[t]), total)
        acc_s[ds, :] = total
        return carry

    lax.fori_loop(0, EB // SUB, body, 0)
    for n in range(EB // LANES):
        taps = acc_s[n * LANES : (n + 1) * LANES, :].T
        block = step * (EB // LANES) + n
        for t in range(9):
            tsum_s[pl.ds(BLOCKS * t + block, 1), :] = taps[t : t + 1]

    @pl.when(step == STEPS - 1)
    def _():
        gated, gpre = gated_s[...], gpre_s[...]
        for which, w in enumerate(
            (
                lax.dot_general(scaled_s[...], gpre, NT, preferred_element_type=F32),
                lax.dot_general(cot_s[:, slab(1, ROWS)], gated, NT, preferred_element_type=F32),
            )
        ):
            for n in range(BLOCKS):
                for i in range(CH // 24):
                    group = (which * BLOCKS + n) * (CH // 24) + i
                    row = PACK * (group // 3) + 24 * (group % 3)
                    packed_s[row : row + 24, :] = w[24 * i : 24 * i + 24, slab(n)]
        proj = jnp.dot(wprojt_ref[...], gated, preferred_element_type=F32)
        gs_all = jnp.dot(wexp_ref[...], gpre, preferred_element_type=F32)
        gain = spread_gain(gain_ref)
        ggain = jnp.zeros((CH, LANES), F32)
        for r in range(ROWS):
            x = x_ref[r].astype(F32)
            out_out[r] = (x + proj[:, r * LANES : (r + 1) * LANES]).astype(BF16)
            normed = x * inv_s[r : r + 1, :]
            gs = gs_all[:, r * LANES : (r + 1) * LANES]
            prod = gs * normed
            ggain = ggain + prod
            mean = jnp.sum(prod * gain, axis=0, keepdims=True) / CH
            gin = inv_s[r : r + 1, :] * (gs * gain - normed * mean) + c_ref[r].astype(F32)
            gin_out[r] = gin.astype(BF16)
        sums = jnp.broadcast_to(lane_sum(ggain), (CH, LANES)).T[:1]
        tsum_s[54:55, :] = sums[:, :LANES]
        tsum_s[55:56, :] = jnp.zeros((1, LANES), F32)
        tsum_s[55:56, : CH - LANES] = sums[:, LANES:]
        for d in range(PARTS):
            packed_s[d * PACK + 72 : (d + 1) * PACK, :] = jnp.zeros((8, LANES), F32)
            if d < 28:
                packed_s[d * PACK + 72 : d * PACK + 74, :] = tsum_s[2 * d : 2 * d + 2, :]
        core = core_ref[0]
        for q in range(PARTS // 2):
            keep_out[q] = packed_s[pl.ds(pl.multiple_of(PACK * (2 * q + core), 8), PACK), :]
            send_out[q] = packed_s[pl.ds(pl.multiple_of(PACK * (2 * q + 1 - core), 8), PACK), :]


def scale_kernel(x_ref, out_ref):
    x = x_ref[...]

    def exponent(v):
        top = jnp.max(jnp.max(jnp.abs(v), axis=1, keepdims=True), axis=0, keepdims=True)
        return jnp.ceil(jnp.log2(jnp.maximum(top, 1e-30)))

    row = lax.broadcasted_iota(jnp.int32, (8, LANES), 0)
    rest = x[72:80]
    e_big = exponent(x[:72])
    e_small = exponent(jnp.where(row < 2, rest, 0.0))
    out_ref[:72] = x[:72] * jnp.exp2(-e_big)
    rest = jnp.where(row < 5, jnp.broadcast_to(e_big, (8, LANES)), jnp.broadcast_to(e_small, (8, LANES)))
    out_ref[72:] = jnp.where(row < 2, x[72:80] * jnp.exp2(-e_small), rest)


def shape(*dims, dtype=F32):
    return jax.ShapeDtypeStruct(dims, dtype)


def full(*dims):
    return pl.BlockSpec(dims, lambda j: (0,) * len(dims))


def params(grid=True):
    return pltpu.CompilerParams(
        dimension_semantics=("arbitrary",) if grid else None, vmem_limit_bytes=VMEM
    )


def gathered(block):
    wide = jnp.broadcast_to(block[None], (PARTS // 2,) + block.shape)
    return lax.all_to_all(wide, RC, 0, 0, tiled=True, axis_index_groups=CHIPS)


def partner(block):
    return lax.ppermute(block, "col", [(i, i ^ 1) for i in range(4)])


def local(inputs, norm_gain, w_expand, kernel, w_squeeze, w_excite, w_project, cotangent):
    nrow, ncol = lax.axis_size("row"), lax.axis_size("col")
    row, col = lax.axis_index("row"), lax.axis_index("col")
    x = inputs[0].transpose(1, 0, 2)
    c = cotangent[0].transpose(1, 0, 2)
    fwd_row = [(i, i + 1) for i in range(nrow - 1)]
    bwd_row = [(i + 1, i) for i in range(nrow - 1)]
    fwd_col = [(i, i + 1) for i in range(ncol - 1)]
    bwd_col = [(i + 1, i) for i in range(ncol - 1)]
    top = lax.ppermute(jnp.concatenate([x[6:8], c[7:8]], axis=0), "row", fwd_row)
    bot = lax.ppermute(jnp.concatenate([x[0:2], c[0:1]], axis=0), "row", bwd_row)
    own = pl.pallas_call(
        strip_kernel,
        out_shape=shape(CH, LANES, dtype=BF16),
        compiler_params=params(False),
        name="strip",
    )(x, c, top, bot)
    left = lax.ppermute(own, "col", fwd_col)
    right = lax.ppermute(own, "col", bwd_col)

    line = lax.broadcasted_iota(jnp.int32, (8, LANES), 1) // 8
    pos = lax.broadcasted_iota(jnp.int32, (8, LANES), 1) % 8
    kind = lax.broadcasted_iota(jnp.int32, (8, LANES), 0)
    top_ok, bot_ok = row > 0, row < nrow - 1
    strip_ok = ((pos == 3) & (col > 0)) | ((pos == 2) & (col < ncol - 1))
    strip_ok &= ((line > 1) | top_ok) & ((line < ROWS + 2) | bot_ok)
    mask = ((kind == 0) & top_ok) | ((kind == 1) & bot_ok) | ((kind == 2) & strip_ok)
    mask = mask.astype(F32)
    gain = norm_gain[None, :]
    wprojt, taps = w_project.T, kernel.T
    halo = full(3, CH, LANES)
    tile = full(ROWS, CH, LANES)
    edge = full(CH, LANES)
    weight = full(CH, EX)
    chunk_rows = lambda width: pl.BlockSpec((EB, width), lambda j: (j, 0))
    chunk_taps = pl.BlockSpec((9, EB), lambda j: (0, j))
    pre, conv, sums = pl.pallas_call(
        forward_kernel,
        grid=(STEPS,),
        in_specs=[tile, tile, halo, halo, edge, edge, edge, full(1, CH), weight, chunk_taps,
                  weight],
        out_specs=[chunk_rows(ROWS * LANES), chunk_rows(CS * LANES), full(16, LANES)],
        out_shape=[shape(EX, ROWS * LANES), shape(EX, CS * LANES), shape(16, LANES)],
        scratch_shapes=[
            pltpu.VMEM((CH, XS * LANES), BF16),
            pltpu.VMEM((CH, ROWS * LANES), BF16),
            pltpu.VMEM((EX, XS * LANES), F32),
            pltpu.VMEM((EX, ROWS * LANES), F32),
            pltpu.VMEM((EB, 9 * LANES), F32),
            pltpu.VMEM((EB, LANES), F32),
        ],
        compiler_params=params(),
        name="forward",
    )(x, c, top, bot, own, left, right, gain, w_expand, taps, wprojt)

    sums = gathered(sums + partner(sums))
    core = (col % 2).astype(jnp.int32).reshape(1)
    out, gin, keep, send, vec = pl.pallas_call(
        backward_kernel,
        grid=(STEPS,),
        in_specs=[pl.BlockSpec(memory_space=pltpu.SMEM), full(PARTS // 2, 16, LANES),
                  full(SQ, EX), full(SQ, EX), tile, tile, halo, halo, edge, edge, full(1, CH),
                  full(8, LANES), chunk_rows(ROWS * LANES), chunk_rows(CS * LANES), chunk_taps,
                  weight, weight],
        out_specs=[tile, tile, full(PARTS // 2, PACK, LANES), full(PARTS // 2, PACK, LANES),
                   full(16, LANES)],
        out_shape=[shape(ROWS, CH, LANES, dtype=BF16), shape(ROWS, CH, LANES, dtype=BF16),
                   shape(PARTS // 2, PACK, LANES), shape(PARTS // 2, PACK, LANES),
                   shape(16, LANES)],
        scratch_shapes=[
            pltpu.VMEM((PARTS * PACK, LANES), F32),
            pltpu.VMEM((EX, LANES), F32),
            pltpu.VMEM((EX, LANES), F32),
            pltpu.VMEM((CH, ROWS * LANES), BF16),
            pltpu.VMEM((CH, CS * LANES), BF16),
            pltpu.VMEM((ROWS, LANES), F32),
            pltpu.VMEM((EX, CS * LANES), F32),
            pltpu.VMEM((EX, ROWS * LANES), BF16),
            pltpu.VMEM((EX, ROWS * LANES), BF16),
            pltpu.VMEM((EB, 9 * LANES), F32),
            pltpu.VMEM((EB, LANES), F32),
            pltpu.VMEM((56, LANES), F32),
        ],
        compiler_params=params(),
        name="backward",
    )(core, sums, w_squeeze.T, w_excite, x, c, top, bot, left, right, gain, mask, pre, conv, taps,
      w_expand, wprojt)

    mine = lax.all_to_all(
        keep + partner(send), RC, 0, 0, tiled=True, axis_index_groups=CHIPS
    )
    total = jnp.sum(mine, axis=0)
    vecs = vec[None]
    sample = lax.axis_index("dp")
    for bit in (1, 2, 4):
        both = lax.ppermute(
            jnp.concatenate([total, vecs.reshape(16 * bit, LANES)], axis=0),
            "dp",
            [(i, i ^ bit) for i in range(8)],
        )
        total = total + both[:PACK]
        theirs = both[PACK:].reshape(bit, 16, LANES)
        ahead = (sample & bit) == 0
        vecs = jnp.concatenate(
            [jnp.where(ahead, vecs, theirs), jnp.where(ahead, theirs, vecs)], axis=0
        )
    vecs = vecs.reshape(8, 2048)
    grad_wexc = jnp.einsum("bs,be->se", vecs[:, 1536:1584], vecs[:, 768:1536], precision=HIGH)
    grad_wsq = jnp.einsum("be,bs->es", vecs[:, :768], vecs[:, 1664:1712], precision=HIGH)
    scaled = pl.pallas_call(
        scale_kernel, out_shape=shape(PACK, LANES), compiler_params=params(False), name="scale"
    )(total)
    same = gathered(scaled.astype(jnp.float16))
    other = partner(same)
    even = core[0] == 0
    every = jnp.stack(
        [jnp.where(even, same, other), jnp.where(even, other, same)], axis=1
    ).reshape(PARTS, PACK, LANES).astype(F32)
    big = (every[:, :72] * jnp.exp2(every[:, 74:75])).reshape(2, BLOCKS, CH, LANES)
    small = (every[:, 72:74] * jnp.exp2(every[:, 77:78])).reshape(8192)
    return (
        out.transpose(1, 0, 2)[None],
        gin.transpose(1, 0, 2)[None],
        small[6912:7104],
        big[0].transpose(1, 0, 2).reshape(CH, EX),
        small[:6912].reshape(9, 768).T,
        grad_wsq,
        grad_wexc,
        big[1].transpose(0, 2, 1).reshape(EX, CH),
    )


def solution(mesh):
    placed = (
        P("dp", None, "row", "col"),
        P(),
        P(),
        P(),
        P(),
        P(),
        P(),
        P("dp", None, "row", "col"),
    )
    return jax.shard_map(
        local,
        mesh=mesh,
        in_specs=placed,
        out_specs=(
            P("dp", None, "row", "col"),
            P("dp", None, "row", "col"),
            P(),
            P(),
            P(),
            P(),
            P(),
            P(),
        ),
        check_vma=False,
    )
```

```python
import jax
import jax.numpy as jnp
from jax import lax
from jax.experimental import pallas as pl
from jax.experimental.pallas import tpu as pltpu
from jax.sharding import PartitionSpec as P

EPS = 1e-06
HIGH = lax.Precision.HIGHEST
RC = ("row", "col")
F32, BF16 = jnp.float32, jnp.bfloat16
CH, EX, SQ = 192, 768, 48
ROWS, LANES = 8, 128
EB = 256
SUB = 16
STEPS = EX // EB
BLOCKS = EX // LANES
PARTS, PACK = 32, 80
VMEM = 60 * 1024 * 1024
CHIPS = [[2 * q + core for q in range(PARTS // 2)] for core in range(2)]
XS = ROWS + 5
CS = ROWS + 3
NT = (((1,), (1,)), ((), ()))
TN = (((0,), (0,)), ((), ()))


def lane_iota(rows):
    return lax.broadcasted_iota(jnp.int32, (rows, LANES), 1)


def rounded(v):
    return v.astype(BF16).astype(F32)


def tn_dot(a, b):
    return lax.dot_general(a, b, TN, preferred_element_type=F32)


def lane_sum(v):
    return jnp.sum(v, axis=1, keepdims=True)


def silu_twice_slope(half):
    t = jnp.tanh(half)
    act = half * (1.0 + t)
    return act, (1.0 + t) + act * (1.0 - t)


def slab(s, n=1):
    return pl.ds(s * LANES, n * LANES)


def strip_kernel(x_ref, c_ref, out_ref):
    lane = lane_iota(CH)
    total = jnp.zeros((CH, LANES), F32)
    for rr in range(2, ROWS + 2):
        v = pltpu.roll(x_ref[rr - 2].astype(F32), (8 * rr + 2) % LANES, 1)
        total = jnp.where((lane >= 8 * rr) & (lane < 8 * rr + 4), v, total)
        v = pltpu.roll(c_ref[rr - 2].astype(F32), (8 * rr + 5) % LANES, 1)
        total = jnp.where((lane >= 8 * rr + 4) & (lane < 8 * rr + 6), v, total)
    out_ref[...] = total.astype(BF16)


def extend_kernel(own_ref, above_ref, below_ref, out_ref):
    lane = lane_iota(CH)
    shift = 8 * ROWS
    value = jnp.where(lane < 16, pltpu.roll(above_ref[...].astype(F32), LANES - shift, 1), own_ref[...].astype(F32))
    value = jnp.where(lane >= 16 + shift, pltpu.roll(below_ref[...].astype(F32), shift, 1), value)
    out_ref[...] = value.astype(BF16)


def input_strip(own_ref, left_ref, right_ref):
    own, left, right = (r[...].astype(F32) for r in (own_ref, left_ref, right_ref))
    pos = lane_iota(CH) % 8
    value = jnp.where(pos == 0, pltpu.roll(own, LANES - 1, 1), 0.0)
    value = jnp.where(pos == 1, pltpu.roll(left, 1, 1), value)
    value = jnp.where(pos == 2, right, value)
    value = jnp.where(pos == 3, pltpu.roll(left, 2, 1), value)
    value = jnp.where(pos == 4, pltpu.roll(right, 1, 1), value)
    return jnp.where(pos == 5, pltpu.roll(own, 3, 1), value)


def cotangent_strip(left_ref, right_ref):
    left, right = (r[...].astype(F32) for r in (left_ref, right_ref))
    pos = lane_iota(CH) % 8
    value = jnp.where(pos == 3, pltpu.roll(left, LANES - 1, 1), 0.0)
    return jnp.where(pos == 2, pltpu.roll(right, LANES - 3, 1), value)


def neighbours(v, strip, rr, first, last):
    edge = pltpu.roll(strip, (LANES - 8 * rr - 3) % LANES, 1)
    left = jnp.where(first, edge, pltpu.roll(v, 1, 1))
    right = jnp.where(last, edge, pltpu.roll(v, LANES - 1, 1))
    return left, right


def spread_gain(gain_ref):
    return jnp.broadcast_to(gain_ref[...], (LANES, CH)).T


def spread_taps(taps_ref, out_s):
    for n in range(EB // LANES):
        rows = slice(n * LANES, (n + 1) * LANES)
        block = jnp.concatenate([taps_ref[:, rows], jnp.zeros((7, LANES), F32)], axis=0).T
        block = 0.5 * block
        for t in range(9):
            out_s[rows, slab(t)] = jnp.broadcast_to(block[:, t : t + 1], (LANES, LANES))


def forward_kernel(
    x_ref, c_ref, top_ref, bot_ref, own_ref, left_ref, right_ref, gain_ref, wexp_ref, taps_ref,
    wprojt_ref, pre_out, conv_out, sums_out, scaled_s, cot_s, pre_s, gg_s, taps_s, acc_s,
):
    step = pl.program_id(0)

    @pl.when(step == 0)
    def _():
        gain = 0.5 * spread_gain(gain_ref)
        for s in range(XS):
            if s < 2:
                x = top_ref[s].astype(F32)
            elif s < ROWS + 2:
                x = x_ref[s - 2].astype(F32)
            elif s < ROWS + 4:
                x = bot_ref[s - ROWS - 2].astype(F32)
            else:
                x = input_strip(own_ref, left_ref, right_ref)
            inverse = lax.rsqrt(jnp.sum(x * x, axis=0, keepdims=True) / CH + EPS)
            scaled_s[:, slab(s)] = (x * inverse * gain).astype(BF16)
        for r in range(ROWS):
            cot_s[:, slab(r)] = c_ref[r]
        pre_s[...] = tn_dot(wexp_ref[...], scaled_s[...])
        gg_s[...] = tn_dot(wprojt_ref[...], cot_s[...])
        sums_out[...] = jnp.zeros_like(sums_out)

    spread_taps(taps_ref, taps_s)
    base = step * EB
    lane = lane_iota(SUB)
    first, last = lane == 0, lane == LANES - 1

    def body(i, carry):
        ds = pl.ds(pl.multiple_of(i * SUB, SUB), SUB)
        whole = pl.ds(pl.multiple_of(base + i * SUB, SUB), SUB)
        k = [taps_s[ds, slab(t)] for t in range(9)]

        def hidden(s):
            v = pre_s[whole, slab(s)]
            if 2 <= s < ROWS + 2:
                pre_out[ds, slab(s - 2)] = v
            return rounded(v * (1.0 + jnp.tanh(v)))

        strip = hidden(XS - 1)
        acc = [None] * (ROWS + 4)
        for rr in range(ROWS + 4):
            h = hidden(rr)
            hl, hr = neighbours(h, strip, rr, first, last)
            for a in (-1, 0, 1):
                o = rr - a
                if 1 <= o <= ROWS + 2:
                    t = 3 * (a + 1)
                    term = k[t] * hl + k[t + 1] * h + k[t + 2] * hr
                    acc[o] = term if acc[o] is None else acc[o] + term
        pooled = jnp.zeros((SUB, LANES), F32)
        gexc = jnp.zeros((SUB, LANES), F32)
        for o in range(1, ROWS + 3):
            v = acc[o]
            conv_out[ds, slab(o - 1)] = v
            if 2 <= o <= ROWS + 1:
                act = v * (1.0 + jnp.tanh(v))
                pooled = pooled + act
                gexc = gexc + act * gg_s[whole, slab(o - 2)]
        edge = None
        for a in (-1, 0, 1):
            for c in (-1, 0, 1):
                shift = (-(8 * a + 2 * c)) % LANES
                term = k[3 * (a + 1) + c + 1] * (pltpu.roll(strip, shift, 1) if shift else strip)
                edge = term if edge is None else edge + term
        conv_out[ds, slab(CS - 1)] = edge
        acc_s[ds, :] = jnp.where(first, lane_sum(pooled), lane_sum(gexc))
        return carry

    lax.fori_loop(0, EB // SUB, body, 0)
    for n in range(EB // LANES):
        sums_out[pl.ds(2 * (step * (EB // LANES) + n), 2), :] = (
            acc_s[n * LANES : (n + 1) * LANES, :].T[:2]
        )


def squeeze_excite(parts_ref, wsq_ref, wexc_ref, exc_s, gp_s, vec_out):
    pixels = 32768.0
    total = jnp.sum(parts_ref[...], axis=0)
    pooled = jnp.concatenate([total[2 * j : 2 * j + 1] for j in range(BLOCKS)], axis=1) / pixels
    gexc = jnp.concatenate([total[2 * j + 1 : 2 * j + 2] for j in range(BLOCKS)], axis=1)
    pooled = jnp.broadcast_to(pooled, (8, EX))
    gexc = jnp.broadcast_to(gexc, (8, EX))
    wsq, wexc = wsq_ref[...], wexc_ref[...]
    spre = lax.dot_general(pooled, wsq, NT, precision=HIGH, preferred_element_type=F32)
    sig = jax.nn.sigmoid(spre)
    squeezed = spre * sig
    epre = jnp.dot(squeezed, wexc, precision=HIGH, preferred_element_type=F32)
    excite = jax.nn.sigmoid(epre)
    gepre = gexc * excite * (1.0 - excite)
    gspre = lax.dot_general(gepre, wexc, NT, precision=HIGH, preferred_element_type=F32)
    gspre = gspre * (sig * (1.0 + spre * (1.0 - sig)))
    gpool = jnp.dot(gspre, wsq, precision=HIGH, preferred_element_type=F32)
    gpool = gpool / pixels
    vec_out[...] = jnp.zeros((16, LANES), F32)
    for j in range(BLOCKS):
        cols = slice(j * LANES, (j + 1) * LANES)
        exc_s[cols, :] = jnp.broadcast_to(excite[:1, cols], (LANES, LANES)).T
        gp_s[cols, :] = jnp.broadcast_to(gpool[:1, cols], (LANES, LANES)).T
        vec_out[j : j + 1, :] = pooled[:1, cols]
        vec_out[BLOCKS + j : BLOCKS + j + 1, :] = gepre[:1, cols]
    vec_out[12:13, :SQ] = squeezed[:1]
    vec_out[13:14, :SQ] = gspre[:1]


def backward_kernel(
    core_ref, parts_ref, wsq_ref, wexc_ref, x_ref, c_ref, top_ref, bot_ref, left_ref, right_ref,
    gain_ref, mask_ref, pre_ref, conv_ref, taps_ref, wexp_ref, wprojt_ref,
    out_out, gin_out, keep_out, send_out, vec_out,
    packed_s, exc_s, gp_s, scaled_s, cot_s, inv_s, gg_s, gated_s, gpre_s, taps_s, acc_s, tsum_s,
):
    step = pl.program_id(0)

    @pl.when(step == 0)
    def _():
        squeeze_excite(parts_ref, wsq_ref, wexc_ref, exc_s, gp_s, vec_out)
        gain = spread_gain(gain_ref)
        for r in range(ROWS):
            x = x_ref[r].astype(F32)
            inverse = lax.rsqrt(jnp.sum(x * x, axis=0, keepdims=True) / CH + EPS)
            inv_s[r : r + 1, :] = inverse
            scaled_s[:, slab(r)] = (x * inverse * gain).astype(BF16)
            cot_s[:, slab(r + 1)] = c_ref[r]
        cot_s[:, slab(0)] = top_ref[2]
        cot_s[:, slab(ROWS + 1)] = bot_ref[2]
        cot_s[:, slab(CS - 1)] = cotangent_strip(left_ref, right_ref).astype(BF16)
        gg_s[...] = tn_dot(wprojt_ref[...], cot_s[...])

    spread_taps(taps_ref, taps_s)
    base = step * EB
    lane = lane_iota(SUB)
    first, last = lane == 0, lane == LANES - 1

    def body(i, carry):
        ds = pl.ds(pl.multiple_of(i * SUB, SUB), SUB)
        whole = pl.ds(pl.multiple_of(base + i * SUB, SUB), SUB)
        k = [taps_s[ds, slab(t)] for t in range(9)]
        exc, gp = exc_s[whole, :], 0.5 * gp_s[whole, :]
        half = 0.5 * exc

        def grad_conv(s, mask):
            act, slope = silu_twice_slope(conv_ref[ds, slab(s)])
            if 1 <= s <= ROWS:
                gated_s[whole, slab(s - 1)] = (act * exc).astype(BF16)
            g = (gg_s[whole, slab(s)] * half + gp) * slope
            if mask is not None:
                g = jnp.where(mask_ref[mask : mask + 1, :] > 0.5, g, 0.0)
            return rounded(g)

        def hidden(r):
            act, slope = silu_twice_slope(pre_ref[ds, slab(r)])
            return rounded(act), slope

        strip = grad_conv(CS - 1, 2)
        tap = [None] * 9
        state = {}
        gh = {}
        for s in range(ROWS + 2):
            g = grad_conv(s, 0 if s == 0 else 1 if s == ROWS + 1 else None)
            gl, gr = neighbours(g, strip, s + 1, first, last)
            for a in (-1, 0, 1):
                r = s + a - 1
                if 0 <= r < ROWS:
                    if r not in state:
                        state[r] = hidden(r)
                    h = state[r][0]
                    t = 3 * (a + 1)
                    term = k[t] * gr + k[t + 1] * g + k[t + 2] * gl
                    gh[r] = term if r not in gh else gh[r] + term
                    for c, v in enumerate((gr, g, gl)):
                        tap[t + c] = h * v if tap[t + c] is None else tap[t + c] + h * v
            r = s - 2
            if 0 <= r:
                gpre_s[whole, slab(r)] = (gh.pop(r) * state.pop(r)[1]).astype(BF16)
        total = jnp.zeros((SUB, LANES), F32)
        for t in range(9):
            total = jnp.where(lane == t, lane_sum(tap[t]), total)
        acc_s[ds, :] = total
        return carry

    lax.fori_loop(0, EB // SUB, body, 0)
    for n in range(EB // LANES):
        taps = acc_s[n * LANES : (n + 1) * LANES, :].T
        block = step * (EB // LANES) + n
        for t in range(9):
            tsum_s[pl.ds(BLOCKS * t + block, 1), :] = taps[t : t + 1]

    @pl.when(step == STEPS - 1)
    def _():
        gated, gpre = gated_s[...], gpre_s[...]
        for which, w in enumerate(
            (
                lax.dot_general(scaled_s[...], gpre, NT, preferred_element_type=F32),
                lax.dot_general(cot_s[:, slab(1, ROWS)], gated, NT, preferred_element_type=F32),
            )
        ):
            for n in range(BLOCKS):
                for i in range(CH // 24):
                    group = (which * BLOCKS + n) * (CH // 24) + i
                    row = PACK * (group // 3) + 24 * (group % 3)
                    packed_s[row : row + 24, :] = w[24 * i : 24 * i + 24, slab(n)]
        proj = jnp.dot(wprojt_ref[...], gated, preferred_element_type=F32)
        gs_all = jnp.dot(wexp_ref[...], gpre, preferred_element_type=F32)
        gain = spread_gain(gain_ref)
        ggain = jnp.zeros((CH, LANES), F32)
        for r in range(ROWS):
            x = x_ref[r].astype(F32)
            out_out[r] = (x + proj[:, r * LANES : (r + 1) * LANES]).astype(BF16)
            normed = x * inv_s[r : r + 1, :]
            gs = gs_all[:, r * LANES : (r + 1) * LANES]
            prod = gs * normed
            ggain = ggain + prod
            mean = jnp.sum(prod * gain, axis=0, keepdims=True) / CH
            gin = inv_s[r : r + 1, :] * (gs * gain - normed * mean) + c_ref[r].astype(F32)
            gin_out[r] = gin.astype(BF16)
        sums = jnp.broadcast_to(lane_sum(ggain), (CH, LANES)).T[:1]
        tsum_s[54:55, :] = sums[:, :LANES]
        tsum_s[55:56, :] = jnp.zeros((1, LANES), F32)
        tsum_s[55:56, : CH - LANES] = sums[:, LANES:]
        for d in range(PARTS):
            packed_s[d * PACK + 72 : (d + 1) * PACK, :] = jnp.zeros((8, LANES), F32)
            if d < 28:
                packed_s[d * PACK + 72 : d * PACK + 74, :] = tsum_s[2 * d : 2 * d + 2, :]
        core = core_ref[0]
        for q in range(PARTS // 2):
            keep_out[q] = packed_s[pl.ds(pl.multiple_of(PACK * (2 * q + core), 8), PACK), :]
            send_out[q] = packed_s[pl.ds(pl.multiple_of(PACK * (2 * q + 1 - core), 8), PACK), :]


def scale_kernel(x_ref, out_ref):
    x = x_ref[...]

    def exponent(v):
        top = jnp.max(jnp.max(jnp.abs(v), axis=1, keepdims=True), axis=0, keepdims=True)
        return jnp.ceil(jnp.log2(jnp.maximum(top, 1e-30)))

    row = lax.broadcasted_iota(jnp.int32, (8, LANES), 0)
    rest = x[72:80]
    e_big = exponent(x[:72])
    e_small = exponent(jnp.where(row < 2, rest, 0.0))
    out_ref[:72] = x[:72] * jnp.exp2(-e_big)
    rest = jnp.where(row < 5, jnp.broadcast_to(e_big, (8, LANES)), jnp.broadcast_to(e_small, (8, LANES)))
    out_ref[72:] = jnp.where(row < 2, x[72:80] * jnp.exp2(-e_small), rest)


def shape(*dims, dtype=F32):
    return jax.ShapeDtypeStruct(dims, dtype)


def full(*dims):
    return pl.BlockSpec(dims, lambda j: (0,) * len(dims))


def params(grid=True):
    return pltpu.CompilerParams(
        dimension_semantics=("arbitrary",) if grid else None, vmem_limit_bytes=VMEM
    )


def gathered(block):
    wide = jnp.broadcast_to(block[None], (PARTS // 2,) + block.shape)
    return lax.all_to_all(wide, RC, 0, 0, tiled=True, axis_index_groups=CHIPS)


def partner(block):
    return lax.ppermute(block, "col", [(i, i ^ 1) for i in range(4)])


def local(inputs, norm_gain, w_expand, kernel, w_squeeze, w_excite, w_project, cotangent):
    nrow, ncol = lax.axis_size("row"), lax.axis_size("col")
    row, col = lax.axis_index("row"), lax.axis_index("col")
    x = inputs[0].transpose(1, 0, 2)
    c = cotangent[0].transpose(1, 0, 2)
    fwd_row = [(i, i + 1) for i in range(nrow - 1)]
    bwd_row = [(i + 1, i) for i in range(nrow - 1)]
    fwd_col = [(i, i + 1) for i in range(ncol - 1)]
    bwd_col = [(i + 1, i) for i in range(ncol - 1)]
    own = pl.pallas_call(
        strip_kernel,
        out_shape=shape(CH, LANES, dtype=BF16),
        compiler_params=params(False),
        name="strip",
    )(x, c)
    above = lax.ppermute(own, "row", fwd_row)
    below = lax.ppermute(own, "row", bwd_row)
    top = lax.ppermute(jnp.concatenate([x[6:8], c[7:8]], axis=0), "row", fwd_row)
    bot = lax.ppermute(jnp.concatenate([x[0:2], c[0:1]], axis=0), "row", bwd_row)
    own = pl.pallas_call(
        extend_kernel,
        out_shape=shape(CH, LANES, dtype=BF16),
        compiler_params=params(False),
        name="extend",
    )(own, above, below)
    left = lax.ppermute(own, "col", fwd_col)
    right = lax.ppermute(own, "col", bwd_col)

    line = lax.broadcasted_iota(jnp.int32, (8, LANES), 1) // 8
    pos = lax.broadcasted_iota(jnp.int32, (8, LANES), 1) % 8
    kind = lax.broadcasted_iota(jnp.int32, (8, LANES), 0)
    top_ok, bot_ok = row > 0, row < nrow - 1
    strip_ok = ((pos == 3) & (col > 0)) | ((pos == 2) & (col < ncol - 1))
    strip_ok &= ((line > 1) | top_ok) & ((line < ROWS + 2) | bot_ok)
    mask = ((kind == 0) & top_ok) | ((kind == 1) & bot_ok) | ((kind == 2) & strip_ok)
    mask = mask.astype(F32)
    gain = norm_gain[None, :]
    wprojt, taps = w_project.T, kernel.T
    halo = full(3, CH, LANES)
    tile = full(ROWS, CH, LANES)
    edge = full(CH, LANES)
    weight = full(CH, EX)
    chunk_rows = lambda width: pl.BlockSpec((EB, width), lambda j: (j, 0))
    chunk_taps = pl.BlockSpec((9, EB), lambda j: (0, j))
    pre, conv, sums = pl.pallas_call(
        forward_kernel,
        grid=(STEPS,),
        in_specs=[tile, tile, halo, halo, edge, edge, edge, full(1, CH), weight, chunk_taps,
                  weight],
        out_specs=[chunk_rows(ROWS * LANES), chunk_rows(CS * LANES), full(16, LANES)],
        out_shape=[shape(EX, ROWS * LANES), shape(EX, CS * LANES), shape(16, LANES)],
        scratch_shapes=[
            pltpu.VMEM((CH, XS * LANES), BF16),
            pltpu.VMEM((CH, ROWS * LANES), BF16),
            pltpu.VMEM((EX, XS * LANES), F32),
            pltpu.VMEM((EX, ROWS * LANES), F32),
            pltpu.VMEM((EB, 9 * LANES), F32),
            pltpu.VMEM((EB, LANES), F32),
        ],
        compiler_params=params(),
        name="forward",
    )(x, c, top, bot, own, left, right, gain, w_expand, taps, wprojt)

    sums = gathered(sums + partner(sums))
    core = (col % 2).astype(jnp.int32).reshape(1)
    out, gin, keep, send, vec = pl.pallas_call(
        backward_kernel,
        grid=(STEPS,),
        in_specs=[pl.BlockSpec(memory_space=pltpu.SMEM), full(PARTS // 2, 16, LANES),
                  full(SQ, EX), full(SQ, EX), tile, tile, halo, halo, edge, edge, full(1, CH),
                  full(8, LANES), chunk_rows(ROWS * LANES), chunk_rows(CS * LANES), chunk_taps,
                  weight, weight],
        out_specs=[tile, tile, full(PARTS // 2, PACK, LANES), full(PARTS // 2, PACK, LANES),
                   full(16, LANES)],
        out_shape=[shape(ROWS, CH, LANES, dtype=BF16), shape(ROWS, CH, LANES, dtype=BF16),
                   shape(PARTS // 2, PACK, LANES), shape(PARTS // 2, PACK, LANES),
                   shape(16, LANES)],
        scratch_shapes=[
            pltpu.VMEM((PARTS * PACK, LANES), F32),
            pltpu.VMEM((EX, LANES), F32),
            pltpu.VMEM((EX, LANES), F32),
            pltpu.VMEM((CH, ROWS * LANES), BF16),
            pltpu.VMEM((CH, CS * LANES), BF16),
            pltpu.VMEM((ROWS, LANES), F32),
            pltpu.VMEM((EX, CS * LANES), F32),
            pltpu.VMEM((EX, ROWS * LANES), BF16),
            pltpu.VMEM((EX, ROWS * LANES), BF16),
            pltpu.VMEM((EB, 9 * LANES), F32),
            pltpu.VMEM((EB, LANES), F32),
            pltpu.VMEM((56, LANES), F32),
        ],
        compiler_params=params(),
        name="backward",
    )(core, sums, w_squeeze.T, w_excite, x, c, top, bot, left, right, gain, mask, pre, conv, taps,
      w_expand, wprojt)

    mine = lax.all_to_all(
        keep + partner(send), RC, 0, 0, tiled=True, axis_index_groups=CHIPS
    )
    total = jnp.sum(mine, axis=0)
    vecs = vec[None]
    sample = lax.axis_index("dp")
    for bit in (1, 2, 4):
        both = lax.ppermute(
            jnp.concatenate([total, vecs.reshape(16 * bit, LANES)], axis=0),
            "dp",
            [(i, i ^ bit) for i in range(8)],
        )
        total = total + both[:PACK]
        theirs = both[PACK:].reshape(bit, 16, LANES)
        ahead = (sample & bit) == 0
        vecs = jnp.concatenate(
            [jnp.where(ahead, vecs, theirs), jnp.where(ahead, theirs, vecs)], axis=0
        )
    vecs = vecs.reshape(8, 2048)
    grad_wexc = jnp.einsum("bs,be->se", vecs[:, 1536:1584], vecs[:, 768:1536], precision=HIGH)
    grad_wsq = jnp.einsum("be,bs->es", vecs[:, :768], vecs[:, 1664:1712], precision=HIGH)
    scaled = pl.pallas_call(
        scale_kernel, out_shape=shape(PACK, LANES), compiler_params=params(False), name="scale"
    )(total)
    same = gathered(scaled.astype(jnp.float16))
    other = partner(same)
    even = core[0] == 0
    every = jnp.stack(
        [jnp.where(even, same, other), jnp.where(even, other, same)], axis=1
    ).reshape(PARTS, PACK, LANES).astype(F32)
    big = (every[:, :72] * jnp.exp2(every[:, 74:75])).reshape(2, BLOCKS, CH, LANES)
    small = (every[:, 72:74] * jnp.exp2(every[:, 77:78])).reshape(8192)
    return (
        out.transpose(1, 0, 2)[None],
        gin.transpose(1, 0, 2)[None],
        small[6912:7104],
        big[0].transpose(1, 0, 2).reshape(CH, EX),
        small[:6912].reshape(9, 768).T,
        grad_wsq,
        grad_wexc,
        big[1].transpose(0, 2, 1).reshape(EX, CH),
    )


def solution(mesh):
    placed = (
        P("dp", None, "row", "col"),
        P(),
        P(),
        P(),
        P(),
        P(),
        P(),
        P("dp", None, "row", "col"),
    )
    return jax.shard_map(
        local,
        mesh=mesh,
        in_specs=placed,
        out_specs=(
            P("dp", None, "row", "col"),
            P("dp", None, "row", "col"),
            P(),
            P(),
            P(),
            P(),
            P(),
            P(),
        ),
        check_vma=False,
    )
```

```python
import jax
import jax.numpy as jnp
from jax import lax
from jax.experimental import pallas as pl
from jax.experimental.pallas import tpu as pltpu
from jax.sharding import PartitionSpec as P

EPS = 1e-06
HIGH = lax.Precision.HIGHEST
RC = ("row", "col")
F32, BF16 = jnp.float32, jnp.bfloat16
CH, EX, SQ = 192, 768, 48
ROWS, LANES = 8, 128
EB = 256
SUB = 16
STEPS = EX // EB
BLOCKS = EX // LANES
PARTS, PACK = 32, 80
VMEM = 60 * 1024 * 1024
CHIPS = [[2 * q + core for q in range(PARTS // 2)] for core in range(2)]
XS = ROWS + 5
CS = ROWS + 3
NT = (((1,), (1,)), ((), ()))
TN = (((0,), (0,)), ((), ()))


def lane_iota(rows):
    return lax.broadcasted_iota(jnp.int32, (rows, LANES), 1)


def rounded(v):
    return v.astype(BF16).astype(F32)


def tn_dot(a, b):
    return lax.dot_general(a, b, TN, preferred_element_type=F32)


def lane_sum(v):
    return jnp.sum(v, axis=1, keepdims=True)


def silu_twice_slope(half):
    t = jnp.tanh(half)
    act = half * (1.0 + t)
    return act, (1.0 + t) + act * (1.0 - t)


def slab(s, n=1):
    return pl.ds(s * LANES, n * LANES)


def strip_kernel(x_ref, c_ref, top_ref, bot_ref, after_ref, out_ref):
    lane = lane_iota(CH)
    total = jnp.zeros((CH, LANES), F32)
    for rr in range(ROWS + 4):
        if rr < 2:
            v = top_ref[rr]
        elif rr < ROWS + 2:
            v = x_ref[rr - 2]
        else:
            v = bot_ref[rr - ROWS - 2]
        v = pltpu.roll(v.astype(F32), (8 * rr + 2) % LANES, 1)
        total = jnp.where((lane >= 8 * rr) & (lane < 8 * rr + 4), v, total)
        if 1 <= rr <= ROWS + 2:
            if rr == 1:
                v = top_ref[2]
            elif rr == ROWS + 2:
                v = bot_ref[2]
            else:
                v = c_ref[rr - 2]
            v = pltpu.roll(v.astype(F32), (8 * rr + 5) % LANES, 1)
            total = jnp.where((lane >= 8 * rr + 4) & (lane < 8 * rr + 6), v, total)
    out_ref[...] = total.astype(BF16)


def input_strip(own_ref, left_ref, right_ref):
    own, left, right = (r[...].astype(F32) for r in (own_ref, left_ref, right_ref))
    pos = lane_iota(CH) % 8
    value = jnp.where(pos == 0, pltpu.roll(own, LANES - 1, 1), 0.0)
    value = jnp.where(pos == 1, pltpu.roll(left, 1, 1), value)
    value = jnp.where(pos == 2, right, value)
    value = jnp.where(pos == 3, pltpu.roll(left, 2, 1), value)
    value = jnp.where(pos == 4, pltpu.roll(right, 1, 1), value)
    return jnp.where(pos == 5, pltpu.roll(own, 3, 1), value)


def cotangent_strip(left_ref, right_ref):
    left, right = (r[...].astype(F32) for r in (left_ref, right_ref))
    pos = lane_iota(CH) % 8
    value = jnp.where(pos == 3, pltpu.roll(left, LANES - 1, 1), 0.0)
    return jnp.where(pos == 2, pltpu.roll(right, LANES - 3, 1), value)


def neighbours(v, strip, rr, first, last):
    edge = pltpu.roll(strip, (LANES - 8 * rr - 3) % LANES, 1)
    left = jnp.where(first, edge, pltpu.roll(v, 1, 1))
    right = jnp.where(last, edge, pltpu.roll(v, LANES - 1, 1))
    return left, right


def spread_gain(gain_ref):
    return jnp.broadcast_to(gain_ref[...], (LANES, CH)).T


def spread_taps(taps_ref, out_s):
    for n in range(EB // LANES):
        rows = slice(n * LANES, (n + 1) * LANES)
        block = jnp.concatenate([taps_ref[:, rows], jnp.zeros((7, LANES), F32)], axis=0).T
        block = 0.5 * block
        for t in range(9):
            out_s[rows, slab(t)] = jnp.broadcast_to(block[:, t : t + 1], (LANES, LANES))


def expand_kernel(
    x_ref, c_ref, gain_ref, wexp_ref, wprojt_ref, scaled_out, inv_out, pre_out, hid_out, gg_out, cot_s
):
    @pl.when(pl.program_id(0) == 0)
    def _():
        gain = spread_gain(gain_ref)
        for r in range(ROWS):
            x = x_ref[r].astype(F32)
            inverse = lax.rsqrt(jnp.sum(x * x, axis=0, keepdims=True) / CH + EPS)
            inv_out[r : r + 1, :] = inverse
            scaled_out[:, slab(r)] = (x * inverse * gain).astype(BF16)
            cot_s[:, slab(r)] = c_ref[r]

    pre_out[...] = tn_dot(wexp_ref[...] * 0.5, scaled_out[...])
    gg_out[...] = tn_dot(wprojt_ref[...], cot_s[...])

    def body(i, carry):
        ds = pl.ds(pl.multiple_of(i * SUB, SUB), SUB)
        v = pre_out[ds, :]
        hid_out[ds, :] = (v * (1.0 + jnp.tanh(v))).astype(BF16)
        return carry

    lax.fori_loop(0, EB // SUB, body, 0)


def forward_kernel(
    top_ref, bot_ref, own_ref, left_ref, right_ref, gain_ref, wexp_ref, taps_ref, hid_ref, gg_ref,
    conv_out, sums_out, scaled_s, pre_s, taps_s, acc_s,
):
    step = pl.program_id(0)

    @pl.when(step == 0)
    def _():
        gain = 0.5 * spread_gain(gain_ref)
        for s in range(XS - ROWS):
            if s < 2:
                x = top_ref[s].astype(F32)
            elif s < 4:
                x = bot_ref[s - 2].astype(F32)
            else:
                x = input_strip(own_ref, left_ref, right_ref)
            inverse = lax.rsqrt(jnp.sum(x * x, axis=0, keepdims=True) / CH + EPS)
            scaled_s[:, slab(s)] = (x * inverse * gain).astype(BF16)
        sums_out[...] = jnp.zeros_like(sums_out)

    pre_s[...] = tn_dot(wexp_ref[...], scaled_s[...])
    spread_taps(taps_ref, taps_s)
    lane = lane_iota(SUB)
    first, last = lane == 0, lane == LANES - 1

    def body(i, carry):
        ds = pl.ds(pl.multiple_of(i * SUB, SUB), SUB)
        k = [taps_s[ds, slab(t)] for t in range(9)]

        def hidden(s):
            if 2 <= s < ROWS + 2:
                return hid_ref[ds, slab(s - 2)].astype(F32)
            v = pre_s[ds, slab(s if s < 2 else s - ROWS)]
            return rounded(v * (1.0 + jnp.tanh(v)))

        strip = hidden(XS - 1)
        acc = [None] * (ROWS + 4)
        for rr in range(ROWS + 4):
            h = hidden(rr)
            hl, hr = neighbours(h, strip, rr, first, last)
            for a in (-1, 0, 1):
                o = rr - a
                if 1 <= o <= ROWS + 2:
                    t = 3 * (a + 1)
                    term = k[t] * hl + k[t + 1] * h + k[t + 2] * hr
                    acc[o] = term if acc[o] is None else acc[o] + term
        pooled = jnp.zeros((SUB, LANES), F32)
        gexc = jnp.zeros((SUB, LANES), F32)
        for o in range(1, ROWS + 3):
            v = acc[o]
            conv_out[ds, slab(o - 1)] = v
            if 2 <= o <= ROWS + 1:
                act = v * (1.0 + jnp.tanh(v))
                pooled = pooled + act
                gexc = gexc + act * gg_ref[ds, slab(o - 2)]
        edge = None
        for a in (-1, 0, 1):
            for c in (-1, 0, 1):
                shift = (-(8 * a + 2 * c)) % LANES
                term = k[3 * (a + 1) + c + 1] * (pltpu.roll(strip, shift, 1) if shift else strip)
                edge = term if edge is None else edge + term
        conv_out[ds, slab(CS - 1)] = edge
        acc_s[ds, :] = jnp.where(first, lane_sum(pooled), lane_sum(gexc))
        return carry

    lax.fori_loop(0, EB // SUB, body, 0)
    for n in range(EB // LANES):
        sums_out[pl.ds(2 * (step * (EB // LANES) + n), 2), :] = (
            acc_s[n * LANES : (n + 1) * LANES, :].T[:2]
        )


def squeeze_excite(parts_ref, wsq_ref, wexc_ref, exc_s, gp_s, vec_out):
    pixels = 32768.0
    total = jnp.sum(parts_ref[...], axis=0)
    pooled = jnp.concatenate([total[2 * j : 2 * j + 1] for j in range(BLOCKS)], axis=1) / pixels
    gexc = jnp.concatenate([total[2 * j + 1 : 2 * j + 2] for j in range(BLOCKS)], axis=1)
    pooled = jnp.broadcast_to(pooled, (8, EX))
    gexc = jnp.broadcast_to(gexc, (8, EX))
    wsq, wexc = wsq_ref[...], wexc_ref[...]
    spre = lax.dot_general(pooled, wsq, NT, precision=HIGH, preferred_element_type=F32)
    sig = jax.nn.sigmoid(spre)
    squeezed = spre * sig
    epre = jnp.dot(squeezed, wexc, precision=HIGH, preferred_element_type=F32)
    excite = jax.nn.sigmoid(epre)
    gepre = gexc * excite * (1.0 - excite)
    gspre = lax.dot_general(gepre, wexc, NT, precision=HIGH, preferred_element_type=F32)
    gspre = gspre * (sig * (1.0 + spre * (1.0 - sig)))
    gpool = jnp.dot(gspre, wsq, precision=HIGH, preferred_element_type=F32)
    gpool = gpool / pixels
    vec_out[...] = jnp.zeros((16, LANES), F32)
    for j in range(BLOCKS):
        cols = slice(j * LANES, (j + 1) * LANES)
        exc_s[cols, :] = jnp.broadcast_to(excite[:1, cols], (LANES, LANES)).T
        gp_s[cols, :] = jnp.broadcast_to(gpool[:1, cols], (LANES, LANES)).T
        vec_out[j : j + 1, :] = pooled[:1, cols]
        vec_out[BLOCKS + j : BLOCKS + j + 1, :] = gepre[:1, cols]
    vec_out[12:13, :SQ] = squeezed[:1]
    vec_out[13:14, :SQ] = gspre[:1]


def backward_kernel(
    core_ref, parts_ref, wsq_ref, wexc_ref, x_ref, c_ref, top_ref, bot_ref, left_ref, right_ref,
    gain_ref, mask_ref, scaled_ref, inv_ref, gg_ref, pre_ref, conv_ref, taps_ref, wexp_ref, wprojt_ref,
    out_out, gin_out, keep_out, send_out, vec_out,
    packed_s, exc_s, gp_s, rim_s, cot_s, gg_s, gated_s, gpre_s, taps_s, acc_s, tsum_s,
):
    step = pl.program_id(0)

    @pl.when(step == 0)
    def _():
        squeeze_excite(parts_ref, wsq_ref, wexc_ref, exc_s, gp_s, vec_out)
        for r in range(ROWS):
            cot_s[:, slab(r)] = c_ref[r]
        rim_s[:, slab(0)] = top_ref[2]
        rim_s[:, slab(1)] = bot_ref[2]
        rim_s[:, slab(2)] = cotangent_strip(left_ref, right_ref).astype(BF16)
        gg_s[...] = tn_dot(wprojt_ref[...], rim_s[...])

    spread_taps(taps_ref, taps_s)
    base = step * EB
    lane = lane_iota(SUB)
    first, last = lane == 0, lane == LANES - 1

    def body(i, carry):
        ds = pl.ds(pl.multiple_of(i * SUB, SUB), SUB)
        whole = pl.ds(pl.multiple_of(base + i * SUB, SUB), SUB)
        k = [taps_s[ds, slab(t)] for t in range(9)]
        exc, gp = exc_s[whole, :], 0.5 * gp_s[whole, :]
        half = 0.5 * exc

        def grad_conv(s, mask):
            act, slope = silu_twice_slope(conv_ref[ds, slab(s)])
            if 1 <= s <= ROWS:
                gated_s[whole, slab(s - 1)] = (act * exc).astype(BF16)
            if 1 <= s <= ROWS:
                g = gg_ref[ds, slab(s - 1)]
            else:
                g = gg_s[whole, slab(0 if s == 0 else s - ROWS)]
            g = (g * half + gp) * slope
            if mask is not None:
                g = jnp.where(mask_ref[mask : mask + 1, :] > 0.5, g, 0.0)
            return rounded(g)

        def hidden(r):
            act, slope = silu_twice_slope(pre_ref[ds, slab(r)])
            return rounded(act), slope

        strip = grad_conv(CS - 1, 2)
        tap = [None] * 9
        state = {}
        gh = {}
        for s in range(ROWS + 2):
            g = grad_conv(s, 0 if s == 0 else 1 if s == ROWS + 1 else None)
            gl, gr = neighbours(g, strip, s + 1, first, last)
            for a in (-1, 0, 1):
                r = s + a - 1
                if 0 <= r < ROWS:
                    if r not in state:
                        state[r] = hidden(r)
                    h = state[r][0]
                    t = 3 * (a + 1)
                    term = k[t] * gr + k[t + 1] * g + k[t + 2] * gl
                    gh[r] = term if r not in gh else gh[r] + term
                    for c, v in enumerate((gr, g, gl)):
                        tap[t + c] = h * v if tap[t + c] is None else tap[t + c] + h * v
            r = s - 2
            if 0 <= r:
                gpre_s[whole, slab(r)] = (gh.pop(r) * state.pop(r)[1]).astype(BF16)
        total = jnp.zeros((SUB, LANES), F32)
        for t in range(9):
            total = jnp.where(lane == t, lane_sum(tap[t]), total)
        acc_s[ds, :] = total
        return carry

    lax.fori_loop(0, EB // SUB, body, 0)
    for n in range(EB // LANES):
        taps = acc_s[n * LANES : (n + 1) * LANES, :].T
        block = step * (EB // LANES) + n
        for t in range(9):
            tsum_s[pl.ds(BLOCKS * t + block, 1), :] = taps[t : t + 1]

    @pl.when(step == STEPS - 1)
    def _():
        gated, gpre = gated_s[...], gpre_s[...]
        for which, w in enumerate(
            (
                lax.dot_general(scaled_ref[...], gpre, NT, preferred_element_type=F32),
                lax.dot_general(cot_s[...], gated, NT, preferred_element_type=F32),
            )
        ):
            for n in range(BLOCKS):
                for i in range(CH // 24):
                    group = (which * BLOCKS + n) * (CH // 24) + i
                    row = PACK * (group // 3) + 24 * (group % 3)
                    packed_s[row : row + 24, :] = w[24 * i : 24 * i + 24, slab(n)]
        proj = jnp.dot(wprojt_ref[...], gated, preferred_element_type=F32)
        gs_all = jnp.dot(wexp_ref[...], gpre, preferred_element_type=F32)
        gain = spread_gain(gain_ref)
        ggain = jnp.zeros((CH, LANES), F32)
        for r in range(ROWS):
            x = x_ref[r].astype(F32)
            out_out[r] = (x + proj[:, r * LANES : (r + 1) * LANES]).astype(BF16)
            normed = x * inv_ref[r : r + 1, :]
            gs = gs_all[:, r * LANES : (r + 1) * LANES]
            prod = gs * normed
            ggain = ggain + prod
            mean = jnp.sum(prod * gain, axis=0, keepdims=True) / CH
            gin = inv_ref[r : r + 1, :] * (gs * gain - normed * mean) + c_ref[r].astype(F32)
            gin_out[r] = gin.astype(BF16)
        sums = jnp.broadcast_to(lane_sum(ggain), (CH, LANES)).T[:1]
        tsum_s[54:55, :] = sums[:, :LANES]
        tsum_s[55:56, :] = jnp.zeros((1, LANES), F32)
        tsum_s[55:56, : CH - LANES] = sums[:, LANES:]
        for d in range(PARTS):
            packed_s[d * PACK + 72 : (d + 1) * PACK, :] = jnp.zeros((8, LANES), F32)
            if d < 28:
                packed_s[d * PACK + 72 : d * PACK + 74, :] = tsum_s[2 * d : 2 * d + 2, :]
        core = core_ref[0]
        for q in range(PARTS // 2):
            keep_out[q] = packed_s[pl.ds(pl.multiple_of(PACK * (2 * q + core), 8), PACK), :]
            send_out[q] = packed_s[pl.ds(pl.multiple_of(PACK * (2 * q + 1 - core), 8), PACK), :]


def scale_kernel(x_ref, out_ref):
    x = x_ref[...]

    def exponent(v):
        top = jnp.max(jnp.max(jnp.abs(v), axis=1, keepdims=True), axis=0, keepdims=True)
        return jnp.ceil(jnp.log2(jnp.maximum(top, 1e-30)))

    row = lax.broadcasted_iota(jnp.int32, (8, LANES), 0)
    rest = x[72:80]
    e_big = exponent(x[:72])
    e_small = exponent(jnp.where(row < 2, rest, 0.0))
    out_ref[:72] = x[:72] * jnp.exp2(-e_big)
    rest = jnp.where(row < 5, jnp.broadcast_to(e_big, (8, LANES)), jnp.broadcast_to(e_small, (8, LANES)))
    out_ref[72:] = jnp.where(row < 2, x[72:80] * jnp.exp2(-e_small), rest)


def shape(*dims, dtype=F32):
    return jax.ShapeDtypeStruct(dims, dtype)


def full(*dims):
    return pl.BlockSpec(dims, lambda j: (0,) * len(dims))


def params(grid=True):
    return pltpu.CompilerParams(
        dimension_semantics=("arbitrary",) if grid else None, vmem_limit_bytes=VMEM
    )


def cost(flops, moved):
    return pl.CostEstimate(flops=int(flops), bytes_accessed=int(moved), transcendentals=0)


def gathered(block):
    wide = jnp.broadcast_to(block[None], (PARTS // 2,) + block.shape)
    return lax.all_to_all(wide, RC, 0, 0, tiled=True, axis_index_groups=CHIPS)


def partner(block):
    return lax.ppermute(block, "col", [(i, i ^ 1) for i in range(4)])


def local(inputs, norm_gain, w_expand, kernel, w_squeeze, w_excite, w_project, cotangent):
    nrow, ncol = lax.axis_size("row"), lax.axis_size("col")
    row, col = lax.axis_index("row"), lax.axis_index("col")
    x = inputs[0].transpose(1, 0, 2)
    c = cotangent[0].transpose(1, 0, 2)
    fwd_row = [(i, i + 1) for i in range(nrow - 1)]
    bwd_row = [(i + 1, i) for i in range(nrow - 1)]
    fwd_col = [(i, i + 1) for i in range(ncol - 1)]
    bwd_col = [(i + 1, i) for i in range(ncol - 1)]
    top = lax.ppermute(jnp.concatenate([x[6:8], c[7:8]], axis=0), "row", fwd_row)
    bot = lax.ppermute(jnp.concatenate([x[0:2], c[0:1]], axis=0), "row", bwd_row)
    gain = norm_gain[None, :]
    wprojt, taps = w_project.T, kernel.T
    halo = full(3, CH, LANES)
    tile = full(ROWS, CH, LANES)
    edge = full(CH, LANES)
    weight = full(CH, EX)
    chunk_rows = lambda width: pl.BlockSpec((EB, width), lambda j: (j, 0))
    chunk_cols = pl.BlockSpec((CH, EB), lambda j: (0, j))
    chunk_taps = pl.BlockSpec((9, EB), lambda j: (0, j))
    scaled, inv, pre, hid, gg = pl.pallas_call(
        expand_kernel,
        grid=(STEPS,),
        in_specs=[tile, tile, full(1, CH), chunk_cols, chunk_cols],
        out_specs=[full(CH, ROWS * LANES), full(ROWS, LANES), chunk_rows(ROWS * LANES),
                   chunk_rows(ROWS * LANES), chunk_rows(ROWS * LANES)],
        out_shape=[shape(CH, ROWS * LANES, dtype=BF16), shape(ROWS, LANES),
                   shape(EX, ROWS * LANES), shape(EX, ROWS * LANES, dtype=BF16),
                   shape(EX, ROWS * LANES)],
        scratch_shapes=[pltpu.VMEM((CH, ROWS * LANES), BF16)],
        compiler_params=params(),
        cost_estimate=cost(600e6, 10e6),
        name="expand",
    )(x, c, gain, w_expand, wprojt)
    own = pl.pallas_call(
        strip_kernel,
        out_shape=shape(CH, LANES, dtype=BF16),
        compiler_params=params(False),
        cost_estimate=cost(1e6, 1e6),
        name="strip",
    )(x, c, top, bot, inv)
    left = lax.ppermute(own, "col", fwd_col)
    right = lax.ppermute(own, "col", bwd_col)

    line = lax.broadcasted_iota(jnp.int32, (8, LANES), 1) // 8
    pos = lax.broadcasted_iota(jnp.int32, (8, LANES), 1) % 8
    kind = lax.broadcasted_iota(jnp.int32, (8, LANES), 0)
    top_ok, bot_ok = row > 0, row < nrow - 1
    strip_ok = ((pos == 3) & (col > 0)) | ((pos == 2) & (col < ncol - 1))
    strip_ok &= ((line > 1) | top_ok) & ((line < ROWS + 2) | bot_ok)
    mask = ((kind == 0) & top_ok) | ((kind == 1) & bot_ok) | ((kind == 2) & strip_ok)
    mask = mask.astype(F32)
    conv, sums = pl.pallas_call(
        forward_kernel,
        grid=(STEPS,),
        in_specs=[halo, halo, edge, edge, edge, full(1, CH), chunk_cols, chunk_taps,
                  chunk_rows(ROWS * LANES), chunk_rows(ROWS * LANES)],
        out_specs=[chunk_rows(CS * LANES), full(16, LANES)],
        out_shape=[shape(EX, CS * LANES), shape(16, LANES)],
        scratch_shapes=[
            pltpu.VMEM((CH, (XS - ROWS) * LANES), BF16),
            pltpu.VMEM((EB, (XS - ROWS) * LANES), F32),
            pltpu.VMEM((EB, 9 * LANES), F32),
            pltpu.VMEM((EB, LANES), F32),
        ],
        compiler_params=params(),
        cost_estimate=cost(200e6, 12e6),
        name="forward",
    )(top, bot, own, left, right, gain, w_expand, taps, hid, gg)

    sums = gathered(sums + partner(sums))
    core = (col % 2).astype(jnp.int32).reshape(1)
    out, gin, keep, send, vec = pl.pallas_call(
        backward_kernel,
        grid=(STEPS,),
        in_specs=[pl.BlockSpec(memory_space=pltpu.SMEM), full(PARTS // 2, 16, LANES),
                  full(SQ, EX), full(SQ, EX), tile, tile, halo, halo, edge, edge, full(1, CH),
                  full(8, LANES), full(CH, ROWS * LANES), full(ROWS, LANES),
                  chunk_rows(ROWS * LANES), chunk_rows(ROWS * LANES), chunk_rows(CS * LANES), chunk_taps,
                  weight, weight],
        out_specs=[tile, tile, full(PARTS // 2, PACK, LANES), full(PARTS // 2, PACK, LANES),
                   full(16, LANES)],
        out_shape=[shape(ROWS, CH, LANES, dtype=BF16), shape(ROWS, CH, LANES, dtype=BF16),
                   shape(PARTS // 2, PACK, LANES), shape(PARTS // 2, PACK, LANES),
                   shape(16, LANES)],
        scratch_shapes=[
            pltpu.VMEM((PARTS * PACK, LANES), F32),
            pltpu.VMEM((EX, LANES), F32),
            pltpu.VMEM((EX, LANES), F32),
            pltpu.VMEM((CH, 3 * LANES), BF16),
            pltpu.VMEM((CH, ROWS * LANES), BF16),
            pltpu.VMEM((EX, 3 * LANES), F32),
            pltpu.VMEM((EX, ROWS * LANES), BF16),
            pltpu.VMEM((EX, ROWS * LANES), BF16),
            pltpu.VMEM((EB, 9 * LANES), F32),
            pltpu.VMEM((EB, LANES), F32),
            pltpu.VMEM((56, LANES), F32),
        ],
        compiler_params=params(),
        cost_estimate=cost(1500e6, 16e6),
        name="backward",
    )(core, sums, w_squeeze.T, w_excite, x, c, top, bot, left, right, gain, mask, scaled, inv, gg, pre, conv, taps,
      w_expand, wprojt)

    mine = lax.all_to_all(
        keep + partner(send), RC, 0, 0, tiled=True, axis_index_groups=CHIPS
    )
    total = jnp.sum(mine, axis=0)
    vecs = vec[None]
    sample = lax.axis_index("dp")
    for bit in (1, 2, 4):
        both = lax.ppermute(
            jnp.concatenate([total, vecs.reshape(16 * bit, LANES)], axis=0),
            "dp",
            [(i, i ^ bit) for i in range(8)],
        )
        total = total + both[:PACK]
        theirs = both[PACK:].reshape(bit, 16, LANES)
        ahead = (sample & bit) == 0
        vecs = jnp.concatenate(
            [jnp.where(ahead, vecs, theirs), jnp.where(ahead, theirs, vecs)], axis=0
        )
    vecs = vecs.reshape(8, 2048)
    grad_wexc = jnp.einsum("bs,be->se", vecs[:, 1536:1584], vecs[:, 768:1536], precision=HIGH)
    grad_wsq = jnp.einsum("be,bs->es", vecs[:, :768], vecs[:, 1664:1712], precision=HIGH)
    scaled = pl.pallas_call(
        scale_kernel, out_shape=shape(PACK, LANES), compiler_params=params(False), name="scale"
    )(total)
    same = gathered(scaled.astype(jnp.float16))
    other = partner(same)
    even = core[0] == 0
    every = jnp.stack(
        [jnp.where(even, same, other), jnp.where(even, other, same)], axis=1
    ).reshape(PARTS, PACK, LANES).astype(F32)
    big = (every[:, :72] * jnp.exp2(every[:, 74:75])).reshape(2, BLOCKS, CH, LANES)
    small = (every[:, 72:74] * jnp.exp2(every[:, 77:78])).reshape(8192)
    return (
        out.transpose(1, 0, 2)[None],
        gin.transpose(1, 0, 2)[None],
        small[6912:7104],
        big[0].transpose(1, 0, 2).reshape(CH, EX),
        small[:6912].reshape(9, 768).T,
        grad_wsq,
        grad_wexc,
        big[1].transpose(0, 2, 1).reshape(EX, CH),
    )


def solution(mesh):
    placed = (
        P("dp", None, "row", "col"),
        P(),
        P(),
        P(),
        P(),
        P(),
        P(),
        P("dp", None, "row", "col"),
    )
    return jax.shard_map(
        local,
        mesh=mesh,
        in_specs=placed,
        out_specs=(
            P("dp", None, "row", "col"),
            P("dp", None, "row", "col"),
            P(),
            P(),
            P(),
            P(),
            P(),
            P(),
        ),
        check_vma=False,
    )
```

```python
import jax
import jax.numpy as jnp
from jax import lax
from jax.experimental import pallas as pl
from jax.experimental.pallas import tpu as pltpu
from jax.sharding import PartitionSpec as P

EPS = 1e-06
HIGH = lax.Precision.HIGHEST
RC = ("row", "col")
F32, BF16 = jnp.float32, jnp.bfloat16
CH, EX, SQ = 192, 768, 48
ROWS, LANES = 8, 128
EB = 256
SUB = 16
STEPS = EX // EB
BLOCKS = EX // LANES
PARTS, PACK = 32, 80
VMEM = 60 * 1024 * 1024
CHIPS = [[2 * q + core for q in range(PARTS // 2)] for core in range(2)]
XS = ROWS + 5
CS = ROWS + 3
NT = (((1,), (1,)), ((), ()))
TN = (((0,), (0,)), ((), ()))


def lane_iota(rows):
    return lax.broadcasted_iota(jnp.int32, (rows, LANES), 1)


def rounded(v):
    return v.astype(BF16).astype(F32)


def tn_dot(a, b):
    return lax.dot_general(a, b, TN, preferred_element_type=F32)


def lane_sum(v):
    return jnp.sum(v, axis=1, keepdims=True)


def silu_twice_slope(half):
    t = jnp.tanh(half)
    act = half * (1.0 + t)
    return act, (1.0 + t) + act * (1.0 - t)


def slab(s, n=1):
    return pl.ds(s * LANES, n * LANES)


def strip_kernel(x_ref, c_ref, top_ref, bot_ref, after_ref, out_ref):
    lane = lane_iota(CH)
    total = jnp.zeros((CH, LANES), F32)
    for rr in range(ROWS + 4):
        if rr < 2:
            v = top_ref[rr]
        elif rr < ROWS + 2:
            v = x_ref[rr - 2]
        else:
            v = bot_ref[rr - ROWS - 2]
        v = pltpu.roll(v.astype(F32), (8 * rr + 2) % LANES, 1)
        total = jnp.where((lane >= 8 * rr) & (lane < 8 * rr + 4), v, total)
        if 1 <= rr <= ROWS + 2:
            if rr == 1:
                v = top_ref[2]
            elif rr == ROWS + 2:
                v = bot_ref[2]
            else:
                v = c_ref[rr - 2]
            v = pltpu.roll(v.astype(F32), (8 * rr + 5) % LANES, 1)
            total = jnp.where((lane >= 8 * rr + 4) & (lane < 8 * rr + 6), v, total)
    out_ref[...] = total.astype(BF16)


def input_strip(own_ref, left_ref, right_ref):
    own, left, right = (r[...].astype(F32) for r in (own_ref, left_ref, right_ref))
    pos = lane_iota(CH) % 8
    value = jnp.where(pos == 0, pltpu.roll(own, LANES - 1, 1), 0.0)
    value = jnp.where(pos == 1, pltpu.roll(left, 1, 1), value)
    value = jnp.where(pos == 2, right, value)
    value = jnp.where(pos == 3, pltpu.roll(left, 2, 1), value)
    value = jnp.where(pos == 4, pltpu.roll(right, 1, 1), value)
    return jnp.where(pos == 5, pltpu.roll(own, 3, 1), value)


def cotangent_strip(left_ref, right_ref):
    left, right = (r[...].astype(F32) for r in (left_ref, right_ref))
    pos = lane_iota(CH) % 8
    value = jnp.where(pos == 3, pltpu.roll(left, LANES - 1, 1), 0.0)
    return jnp.where(pos == 2, pltpu.roll(right, LANES - 3, 1), value)


def neighbours(v, strip, rr, first, last):
    edge = pltpu.roll(strip, (LANES - 8 * rr - 3) % LANES, 1)
    left = jnp.where(first, edge, pltpu.roll(v, 1, 1))
    right = jnp.where(last, edge, pltpu.roll(v, LANES - 1, 1))
    return left, right


def spread_gain(gain_ref):
    return jnp.broadcast_to(gain_ref[...], (LANES, CH)).T


def spread_taps(taps_ref, out_s):
    for n in range(EB // LANES):
        rows = slice(n * LANES, (n + 1) * LANES)
        block = jnp.concatenate([taps_ref[:, rows], jnp.zeros((7, LANES), F32)], axis=0).T
        block = 0.5 * block
        for t in range(9):
            out_s[rows, slab(t)] = jnp.broadcast_to(block[:, t : t + 1], (LANES, LANES))


class Chunks:
    def __init__(self, pairs, sems):
        self.pairs, self.sems = pairs, sems

    def copies(self, step):
        rows = pl.ds(pl.multiple_of(step * EB, EB), EB)
        slot = step % 2
        return [
            pltpu.make_async_copy(src.at[rows, :], dst.at[slot], self.sems.at[n, slot])
            for n, (src, dst) in enumerate(self.pairs)
        ]

    def start(self, step):
        for copy in self.copies(step):
            copy.start()

    def advance(self, step):
        for copy in self.copies(step):
            copy.wait()

        @pl.when(step < STEPS - 1)
        def _():
            self.start(step + 1)


def expand_kernel(
    x_ref, c_ref, gain_ref, wexp_ref, wprojt_ref, scaled_out, inv_out, pre_out, hid_out, gg_out, cot_s
):
    @pl.when(pl.program_id(0) == 0)
    def _():
        gain = spread_gain(gain_ref)
        for r in range(ROWS):
            x = x_ref[r].astype(F32)
            inverse = lax.rsqrt(jnp.sum(x * x, axis=0, keepdims=True) / CH + EPS)
            inv_out[r : r + 1, :] = inverse
            scaled_out[:, slab(r)] = (x * inverse * gain).astype(BF16)
            cot_s[:, slab(r)] = c_ref[r]

    pre_out[...] = tn_dot(wexp_ref[...] * 0.5, scaled_out[...])
    gg_out[...] = tn_dot(wprojt_ref[...], cot_s[...])

    def body(i, carry):
        ds = pl.ds(pl.multiple_of(i * SUB, SUB), SUB)
        v = pre_out[ds, :]
        hid_out[ds, :] = (v * (1.0 + jnp.tanh(v))).astype(BF16)
        return carry

    lax.fori_loop(0, EB // SUB, body, 0)


def forward_kernel(
    top_ref, bot_ref, own_ref, left_ref, right_ref, gain_ref, wexp_ref, taps_ref, hid_any, gg_any,
    conv_out, sums_out, scaled_s, pre_s, taps_s, acc_s, hid_s, gg_s, sems,
):
    step = pl.program_id(0)
    chunks = Chunks(((hid_any, hid_s), (gg_any, gg_s)), sems)
    hid_ref, gg_ref = hid_s.at[step % 2], gg_s.at[step % 2]

    @pl.when(step == 0)
    def _():
        chunks.start(0)
        gain = 0.5 * spread_gain(gain_ref)
        for s in range(XS - ROWS):
            if s < 2:
                x = top_ref[s].astype(F32)
            elif s < 4:
                x = bot_ref[s - 2].astype(F32)
            else:
                x = input_strip(own_ref, left_ref, right_ref)
            inverse = lax.rsqrt(jnp.sum(x * x, axis=0, keepdims=True) / CH + EPS)
            scaled_s[:, slab(s)] = (x * inverse * gain).astype(BF16)
        sums_out[...] = jnp.zeros_like(sums_out)

    pre_s[...] = tn_dot(wexp_ref[...], scaled_s[...])
    spread_taps(taps_ref, taps_s)
    chunks.advance(step)
    lane = lane_iota(SUB)
    first, last = lane == 0, lane == LANES - 1

    def body(i, carry):
        ds = pl.ds(pl.multiple_of(i * SUB, SUB), SUB)
        k = [taps_s[ds, slab(t)] for t in range(9)]

        def hidden(s):
            if 2 <= s < ROWS + 2:
                return hid_ref[ds, slab(s - 2)].astype(F32)
            v = pre_s[ds, slab(s if s < 2 else s - ROWS)]
            return rounded(v * (1.0 + jnp.tanh(v)))

        strip = hidden(XS - 1)
        acc = [None] * (ROWS + 4)
        for rr in range(ROWS + 4):
            h = hidden(rr)
            hl, hr = neighbours(h, strip, rr, first, last)
            for a in (-1, 0, 1):
                o = rr - a
                if 1 <= o <= ROWS + 2:
                    t = 3 * (a + 1)
                    term = k[t] * hl + k[t + 1] * h + k[t + 2] * hr
                    acc[o] = term if acc[o] is None else acc[o] + term
        pooled = jnp.zeros((SUB, LANES), F32)
        gexc = jnp.zeros((SUB, LANES), F32)
        for o in range(1, ROWS + 3):
            v = acc[o]
            conv_out[ds, slab(o - 1)] = v
            if 2 <= o <= ROWS + 1:
                act = v * (1.0 + jnp.tanh(v))
                pooled = pooled + act
                gexc = gexc + act * gg_ref[ds, slab(o - 2)]
        edge = None
        for a in (-1, 0, 1):
            for c in (-1, 0, 1):
                shift = (-(8 * a + 2 * c)) % LANES
                term = k[3 * (a + 1) + c + 1] * (pltpu.roll(strip, shift, 1) if shift else strip)
                edge = term if edge is None else edge + term
        conv_out[ds, slab(CS - 1)] = edge
        acc_s[0, ds, :] = pooled
        acc_s[1, ds, :] = gexc
        return carry

    lax.fori_loop(0, EB // SUB, body, 0)
    for n in range(EB // LANES):
        for kind in range(2):
            row = jnp.sum(acc_s[kind, n * LANES : (n + 1) * LANES, :].T, axis=0, keepdims=True)
            sums_out[pl.ds(2 * (step * (EB // LANES) + n) + kind, 1), :] = row


def squeeze_excite(parts_ref, wsq_ref, wexc_ref, exc_s, gp_s, vec_out):
    pixels = 32768.0
    total = jnp.sum(parts_ref[...], axis=0)
    pooled = jnp.concatenate([total[2 * j : 2 * j + 1] for j in range(BLOCKS)], axis=1) / pixels
    gexc = jnp.concatenate([total[2 * j + 1 : 2 * j + 2] for j in range(BLOCKS)], axis=1)
    pooled = jnp.broadcast_to(pooled, (8, EX))
    gexc = jnp.broadcast_to(gexc, (8, EX))
    wsq, wexc = wsq_ref[...], wexc_ref[...]
    spre = lax.dot_general(pooled, wsq, NT, precision=HIGH, preferred_element_type=F32)
    sig = jax.nn.sigmoid(spre)
    squeezed = spre * sig
    epre = jnp.dot(squeezed, wexc, precision=HIGH, preferred_element_type=F32)
    excite = jax.nn.sigmoid(epre)
    gepre = gexc * excite * (1.0 - excite)
    gspre = lax.dot_general(gepre, wexc, NT, precision=HIGH, preferred_element_type=F32)
    gspre = gspre * (sig * (1.0 + spre * (1.0 - sig)))
    gpool = jnp.dot(gspre, wsq, precision=HIGH, preferred_element_type=F32)
    gpool = gpool / pixels
    vec_out[...] = jnp.zeros((16, LANES), F32)
    for j in range(BLOCKS):
        cols = slice(j * LANES, (j + 1) * LANES)
        exc_s[cols, :] = jnp.broadcast_to(excite[:1, cols], (LANES, LANES)).T
        gp_s[cols, :] = jnp.broadcast_to(gpool[:1, cols], (LANES, LANES)).T
        vec_out[j : j + 1, :] = pooled[:1, cols]
        vec_out[BLOCKS + j : BLOCKS + j + 1, :] = gepre[:1, cols]
    vec_out[12:13, :SQ] = squeezed[:1]
    vec_out[13:14, :SQ] = gspre[:1]


def backward_kernel(
    core_ref, parts_ref, wsq_ref, wexc_ref, x_ref, c_ref, top_ref, bot_ref, left_ref, right_ref,
    gain_ref, mask_ref, scaled_ref, inv_ref, gg_any, pre_any, conv_any, taps_ref, wexp_ref, wprojt_ref,
    out_out, gin_out, keep_any, send_any, vec_out,
    packed_s, exc_s, gp_s, rim_s, cot_s, gg_s, gated_s, gpre_s, taps_s, acc_s, tsum_s,
    ggc_s, prec_s, convc_s, sems, out_sems,
):
    step = pl.program_id(0)
    chunks = Chunks(((gg_any, ggc_s), (pre_any, prec_s), (conv_any, convc_s)), sems)
    gg_ref, pre_ref, conv_ref = (r.at[step % 2] for r in (ggc_s, prec_s, convc_s))

    @pl.when(step == 0)
    def _():
        chunks.start(0)
        squeeze_excite(parts_ref, wsq_ref, wexc_ref, exc_s, gp_s, vec_out)
        for r in range(ROWS):
            cot_s[:, slab(r)] = c_ref[r]
        rim_s[:, slab(0)] = top_ref[2]
        rim_s[:, slab(1)] = bot_ref[2]
        rim_s[:, slab(2)] = cotangent_strip(left_ref, right_ref).astype(BF16)
        gg_s[...] = tn_dot(wprojt_ref[...], rim_s[...])

    spread_taps(taps_ref, taps_s)
    chunks.advance(step)
    base = step * EB
    lane = lane_iota(SUB)
    first, last = lane == 0, lane == LANES - 1

    def body(i, carry):
        ds = pl.ds(pl.multiple_of(i * SUB, SUB), SUB)
        whole = pl.ds(pl.multiple_of(base + i * SUB, SUB), SUB)
        k = [taps_s[ds, slab(t)] for t in range(9)]
        exc, gp = exc_s[whole, :], 0.5 * gp_s[whole, :]
        half = 0.5 * exc

        def grad_conv(s, mask):
            act, slope = silu_twice_slope(conv_ref[ds, slab(s)])
            if 1 <= s <= ROWS:
                gated_s[whole, slab(s - 1)] = (act * exc).astype(BF16)
            if 1 <= s <= ROWS:
                g = gg_ref[ds, slab(s - 1)]
            else:
                g = gg_s[whole, slab(0 if s == 0 else s - ROWS)]
            g = (g * half + gp) * slope
            if mask is not None:
                g = jnp.where(mask_ref[mask : mask + 1, :] > 0.5, g, 0.0)
            return rounded(g)

        def hidden(r):
            act, slope = silu_twice_slope(pre_ref[ds, slab(r)])
            return rounded(act), slope

        strip = grad_conv(CS - 1, 2)
        tap = [None] * 9
        state = {}
        gh = {}
        for s in range(ROWS + 2):
            g = grad_conv(s, 0 if s == 0 else 1 if s == ROWS + 1 else None)
            gl, gr = neighbours(g, strip, s + 1, first, last)
            for a in (-1, 0, 1):
                r = s + a - 1
                if 0 <= r < ROWS:
                    if r not in state:
                        state[r] = hidden(r)
                    h = state[r][0]
                    t = 3 * (a + 1)
                    term = k[t] * gr + k[t + 1] * g + k[t + 2] * gl
                    gh[r] = term if r not in gh else gh[r] + term
                    for c, v in enumerate((gr, g, gl)):
                        tap[t + c] = h * v if tap[t + c] is None else tap[t + c] + h * v
            r = s - 2
            if 0 <= r:
                gpre_s[whole, slab(r)] = (gh.pop(r) * state.pop(r)[1]).astype(BF16)
        total = jnp.zeros((SUB, LANES), F32)
        for t in range(9):
            total = jnp.where(lane == t, lane_sum(tap[t]), total)
        acc_s[ds, :] = total
        return carry

    lax.fori_loop(0, EB // SUB, body, 0)
    for n in range(EB // LANES):
        taps = acc_s[n * LANES : (n + 1) * LANES, :].T
        block = step * (EB // LANES) + n
        for t in range(9):
            tsum_s[pl.ds(BLOCKS * t + block, 1), :] = taps[t : t + 1]

    @pl.when(step == STEPS - 1)
    def _():
        gated, gpre = gated_s[...], gpre_s[...]
        for which, w in enumerate(
            (
                lax.dot_general(scaled_ref[...], gpre, NT, preferred_element_type=F32),
                lax.dot_general(cot_s[...], gated, NT, preferred_element_type=F32),
            )
        ):
            for n in range(BLOCKS):
                for i in range(CH // 24):
                    group = (which * BLOCKS + n) * (CH // 24) + i
                    part = group // 3
                    row = PACK * (part % 2 * PARTS // 2 + part // 2) + 24 * (group % 3)
                    packed_s[row : row + 24, :] = w[24 * i : 24 * i + 24, slab(n)]
        gs_all = jnp.dot(wexp_ref[...], gpre, preferred_element_type=F32)
        ggain = jnp.zeros((CH, LANES), F32)
        for r in range(ROWS):
            normed = x_ref[r].astype(F32) * inv_ref[r : r + 1, :]
            ggain = ggain + gs_all[:, r * LANES : (r + 1) * LANES] * normed
        sums = jnp.broadcast_to(lane_sum(ggain), (CH, LANES)).T[:1]
        tsum_s[54:55, :] = sums[:, :LANES]
        tsum_s[55:56, :] = jnp.zeros((1, LANES), F32)
        tsum_s[55:56, : CH - LANES] = sums[:, LANES:]
        for d in range(PARTS):
            rows = slice((d % 2 * PARTS // 2 + d // 2) * PACK + 72, (d % 2 * PARTS // 2 + d // 2 + 1) * PACK)
            packed_s[rows, :] = jnp.zeros((8, LANES), F32)
            if d < 28:
                packed_s[rows.start : rows.start + 2, :] = tsum_s[2 * d : 2 * d + 2, :]
        core, half = core_ref[0], PARTS // 2 * PACK
        sends = [
            pltpu.make_async_copy(
                packed_s.at[pl.ds(pl.multiple_of(half * which, 8), half), :], dst, out_sems.at[n]
            )
            for n, (which, dst) in enumerate(((core, keep_any), (1 - core, send_any)))
        ]
        for copy in sends:
            copy.start()
        proj = jnp.dot(wprojt_ref[...], gated, preferred_element_type=F32)
        gain = spread_gain(gain_ref)
        for r in range(ROWS):
            x = x_ref[r].astype(F32)
            out_out[r] = (x + proj[:, r * LANES : (r + 1) * LANES]).astype(BF16)
            inverse = inv_ref[r : r + 1, :]
            normed = x * inverse
            gnormed = gs_all[:, r * LANES : (r + 1) * LANES] * gain
            mean = jnp.sum(gnormed * normed, axis=0, keepdims=True) / CH
            gin_out[r] = (inverse * (gnormed - normed * mean) + c_ref[r].astype(F32)).astype(BF16)
        for copy in sends:
            copy.wait()


def scale_kernel(x_ref, out_ref):
    x = x_ref[...]

    def exponent(v):
        top = jnp.max(jnp.max(jnp.abs(v), axis=1, keepdims=True), axis=0, keepdims=True)
        return jnp.ceil(jnp.log2(jnp.maximum(top, 1e-30)))

    row = lax.broadcasted_iota(jnp.int32, (8, LANES), 0)
    rest = x[72:80]
    e_big = exponent(x[:72])
    e_small = exponent(jnp.where(row < 2, rest, 0.0))
    big = x[:72] * jnp.exp2(-e_big)
    tail = jnp.where(row < 5, jnp.broadcast_to(e_big, (8, LANES)), jnp.broadcast_to(e_small, (8, LANES)))
    tail = jnp.where(row < 2, rest * jnp.exp2(-e_small), tail)
    for q in range(PARTS // 2):
        out_ref[q, :72] = big
        out_ref[q, 72:] = tail


def to_half(v):
    row = lax.broadcasted_iota(jnp.int32, (1, PACK, 1), 1)
    size = jnp.abs(v)

    def exponent(where):
        top = jnp.max(jnp.where(where, size, 0.0), axis=(1, 2), keepdims=True)
        return jnp.ceil(jnp.log2(jnp.maximum(top, 1e-30)))

    e_big, e_small = exponent(row < 72), exponent((row >= 72) & (row < 74))
    scaled = v * jnp.where(row < 72, jnp.exp2(-e_big), jnp.exp2(-e_small))
    return jnp.where(row < 74, scaled, jnp.where(row < 77, e_big, e_small)).astype(jnp.float16)


def from_half(h):
    v = h.astype(F32)
    row = lax.broadcasted_iota(jnp.int32, (1, PACK, 1), 1)
    scale = jnp.where(row < 72, jnp.exp2(v[:, 74:75]), jnp.exp2(v[:, 77:78]))
    return jnp.where(row < 74, v * scale, 0.0)


def shape(*dims, dtype=F32):
    return jax.ShapeDtypeStruct(dims, dtype)


def full(*dims):
    return pl.BlockSpec(dims, lambda j: (0,) * len(dims))


def params(grid=True):
    return pltpu.CompilerParams(
        dimension_semantics=("arbitrary",) if grid else None, vmem_limit_bytes=VMEM
    )


def cost(flops, moved):
    return pl.CostEstimate(flops=int(flops), bytes_accessed=int(moved), transcendentals=0)


def exchanged(blocks):
    return lax.all_to_all(blocks, RC, 0, 0, tiled=True, axis_index_groups=CHIPS)


def gathered(block):
    return exchanged(jnp.broadcast_to(block[None], (PARTS // 2,) + block.shape))


def partner(block):
    return lax.ppermute(block, "col", [(i, i ^ 1) for i in range(4)])


def local(inputs, norm_gain, w_expand, kernel, w_squeeze, w_excite, w_project, cotangent):
    nrow, ncol = lax.axis_size("row"), lax.axis_size("col")
    row, col = lax.axis_index("row"), lax.axis_index("col")
    x = inputs[0].transpose(1, 0, 2)
    c = cotangent[0].transpose(1, 0, 2)
    fwd_row = [(i, i + 1) for i in range(nrow - 1)]
    bwd_row = [(i + 1, i) for i in range(nrow - 1)]
    fwd_col = [(i, i + 1) for i in range(ncol - 1)]
    bwd_col = [(i + 1, i) for i in range(ncol - 1)]
    top = lax.ppermute(jnp.concatenate([x[6:8], c[7:8]], axis=0), "row", fwd_row)
    bot = lax.ppermute(jnp.concatenate([x[0:2], c[0:1]], axis=0), "row", bwd_row)
    gain = norm_gain[None, :]
    wprojt, taps = w_project.T, kernel.T
    halo = full(3, CH, LANES)
    tile = full(ROWS, CH, LANES)
    edge = full(CH, LANES)
    weight = full(CH, EX)
    anywhere = pl.BlockSpec(memory_space=pl.ANY)
    chunk_rows = lambda width: pl.BlockSpec((EB, width), lambda j: (j, 0))
    chunk_cols = pl.BlockSpec((CH, EB), lambda j: (0, j))
    chunk_taps = pl.BlockSpec((9, EB), lambda j: (0, j))
    scaled, inv, pre, hid, gg = pl.pallas_call(
        expand_kernel,
        grid=(STEPS,),
        in_specs=[tile, tile, full(1, CH), chunk_cols, chunk_cols],
        out_specs=[full(CH, ROWS * LANES), full(ROWS, LANES), chunk_rows(ROWS * LANES),
                   chunk_rows(ROWS * LANES), chunk_rows(ROWS * LANES)],
        out_shape=[shape(CH, ROWS * LANES, dtype=BF16), shape(ROWS, LANES),
                   shape(EX, ROWS * LANES), shape(EX, ROWS * LANES, dtype=BF16),
                   shape(EX, ROWS * LANES)],
        scratch_shapes=[pltpu.VMEM((CH, ROWS * LANES), BF16)],
        compiler_params=params(),
        cost_estimate=cost(600e6, 10e6),
        name="expand",
    )(x, c, gain, w_expand, wprojt)
    own = pl.pallas_call(
        strip_kernel,
        out_shape=shape(CH, LANES, dtype=BF16),
        compiler_params=params(False),
        cost_estimate=cost(1e6, 1e6),
        name="strip",
    )(x, c, top, bot, inv)
    left = lax.ppermute(own, "col", fwd_col)
    right = lax.ppermute(own, "col", bwd_col)

    line = lax.broadcasted_iota(jnp.int32, (8, LANES), 1) // 8
    pos = lax.broadcasted_iota(jnp.int32, (8, LANES), 1) % 8
    kind = lax.broadcasted_iota(jnp.int32, (8, LANES), 0)
    top_ok, bot_ok = row > 0, row < nrow - 1
    strip_ok = ((pos == 3) & (col > 0)) | ((pos == 2) & (col < ncol - 1))
    strip_ok &= ((line > 1) | top_ok) & ((line < ROWS + 2) | bot_ok)
    mask = ((kind == 0) & top_ok) | ((kind == 1) & bot_ok) | ((kind == 2) & strip_ok)
    mask = mask.astype(F32)
    conv, sums = pl.pallas_call(
        forward_kernel,
        grid=(STEPS,),
        in_specs=[halo, halo, edge, edge, edge, full(1, CH), chunk_cols, chunk_taps,
                  anywhere, anywhere],
        out_specs=[chunk_rows(CS * LANES), full(16, LANES)],
        out_shape=[shape(EX, CS * LANES), shape(16, LANES)],
        scratch_shapes=[
            pltpu.VMEM((CH, (XS - ROWS) * LANES), BF16),
            pltpu.VMEM((EB, (XS - ROWS) * LANES), F32),
            pltpu.VMEM((EB, 9 * LANES), F32),
            pltpu.VMEM((2, EB, LANES), F32),
            pltpu.VMEM((2, EB, ROWS * LANES), BF16),
            pltpu.VMEM((2, EB, ROWS * LANES), F32),
            pltpu.SemaphoreType.DMA((2, 2)),
        ],
        compiler_params=params(),
        cost_estimate=cost(200e6, 12e6),
        name="forward",
    )(top, bot, own, left, right, gain, w_expand, taps, hid, gg)

    sums = gathered(sums + partner(sums))
    core = (col % 2).astype(jnp.int32).reshape(1)
    out, gin, keep, send, vec = pl.pallas_call(
        backward_kernel,
        grid=(STEPS,),
        in_specs=[pl.BlockSpec(memory_space=pltpu.SMEM), full(PARTS // 2, 16, LANES),
                  full(SQ, EX), full(SQ, EX), tile, tile, halo, halo, edge, edge, full(1, CH),
                  full(8, LANES), full(CH, ROWS * LANES), full(ROWS, LANES),
                  anywhere, anywhere, anywhere, chunk_taps,
                  weight, weight],
        out_specs=[tile, tile, anywhere, anywhere, full(16, LANES)],
        out_shape=[shape(ROWS, CH, LANES, dtype=BF16), shape(ROWS, CH, LANES, dtype=BF16),
                   shape(PARTS // 2 * PACK, LANES), shape(PARTS // 2 * PACK, LANES),
                   shape(16, LANES)],
        scratch_shapes=[
            pltpu.VMEM((PARTS * PACK, LANES), F32),
            pltpu.VMEM((EX, LANES), F32),
            pltpu.VMEM((EX, LANES), F32),
            pltpu.VMEM((CH, 3 * LANES), BF16),
            pltpu.VMEM((CH, ROWS * LANES), BF16),
            pltpu.VMEM((EX, 3 * LANES), F32),
            pltpu.VMEM((EX, ROWS * LANES), BF16),
            pltpu.VMEM((EX, ROWS * LANES), BF16),
            pltpu.VMEM((EB, 9 * LANES), F32),
            pltpu.VMEM((EB, LANES), F32),
            pltpu.VMEM((56, LANES), F32),
            pltpu.VMEM((2, EB, ROWS * LANES), F32),
            pltpu.VMEM((2, EB, ROWS * LANES), F32),
            pltpu.VMEM((2, EB, CS * LANES), F32),
            pltpu.SemaphoreType.DMA((3, 2)),
            pltpu.SemaphoreType.DMA((2,)),
        ],
        compiler_params=params(),
        cost_estimate=cost(1500e6, 16e6),
        name="backward",
    )(core, sums, w_squeeze.T, w_excite, x, c, top, bot, left, right, gain, mask, scaled, inv, gg, pre, conv, taps,
      w_expand, wprojt)

    halves = to_half((keep + partner(send)).reshape(PARTS // 2, PACK, LANES))
    mine = exchanged(halves)
    total = jnp.sum(from_half(mine), axis=0)
    vecs = vec[None]
    sample = lax.axis_index("dp")
    for bit in (1, 2, 4):
        both = lax.ppermute(
            jnp.concatenate([total, vecs.reshape(16 * bit, LANES)], axis=0),
            "dp",
            [(i, i ^ bit) for i in range(8)],
        )
        total = total + both[:PACK]
        theirs = both[PACK:].reshape(bit, 16, LANES)
        ahead = (sample & bit) == 0
        vecs = jnp.concatenate(
            [jnp.where(ahead, vecs, theirs), jnp.where(ahead, theirs, vecs)], axis=0
        )
    vecs = vecs.reshape(8, 2048)
    grad_wexc = jnp.einsum("bs,be->se", vecs[:, 1536:1584], vecs[:, 768:1536], precision=HIGH)
    grad_wsq = jnp.einsum("be,bs->es", vecs[:, :768], vecs[:, 1664:1712], precision=HIGH)
    scaled = pl.pallas_call(
        scale_kernel,
        out_shape=shape(PARTS // 2, PACK, LANES),
        compiler_params=params(False),
        name="scale",
    )(total)
    same = exchanged(scaled.astype(jnp.float16))
    other = partner(same)
    even = core[0] == 0
    every = jnp.stack(
        [jnp.where(even, same, other), jnp.where(even, other, same)], axis=1
    ).reshape(PARTS, PACK, LANES).astype(F32)
    big = (every[:, :72] * jnp.exp2(every[:, 74:75])).reshape(2, BLOCKS, CH, LANES)
    small = (every[:, 72:74] * jnp.exp2(every[:, 77:78])).reshape(8192)
    return (
        out.transpose(1, 0, 2)[None],
        gin.transpose(1, 0, 2)[None],
        small[6912:7104],
        big[0].transpose(1, 0, 2).reshape(CH, EX),
        small[:6912].reshape(9, 768).T,
        grad_wsq,
        grad_wexc,
        big[1].transpose(0, 2, 1).reshape(EX, CH),
    )


def solution(mesh):
    placed = (
        P("dp", None, "row", "col"),
        P(),
        P(),
        P(),
        P(),
        P(),
        P(),
        P("dp", None, "row", "col"),
    )
    return jax.shard_map(
        local,
        mesh=mesh,
        in_specs=placed,
        out_specs=(
            P("dp", None, "row", "col"),
            P("dp", None, "row", "col"),
            P(),
            P(),
            P(),
            P(),
            P(),
            P(),
        ),
        check_vma=False,
    )
```

```python
import jax
import jax.numpy as jnp
from jax import lax
from jax.experimental import pallas as pl
from jax.experimental.pallas import tpu as pltpu
from jax.sharding import PartitionSpec as P

EPS = 1e-06
HIGH = lax.Precision.HIGHEST
RC = ("row", "col")
F32, BF16 = jnp.float32, jnp.bfloat16
CH, EX, SQ = 192, 768, 48
ROWS, LANES = 8, 128
EB = 256
SUB = 16
STEPS = EX // EB
BLOCKS = EX // LANES
PARTS, PACK = 32, 80
VMEM = 60 * 1024 * 1024
CHIPS = [[2 * q + core for q in range(PARTS // 2)] for core in range(2)]
XS = ROWS + 5
CS = ROWS + 3
NT = (((1,), (1,)), ((), ()))
TN = (((0,), (0,)), ((), ()))


def lane_iota(rows):
    return lax.broadcasted_iota(jnp.int32, (rows, LANES), 1)


def rounded(v):
    return v.astype(BF16).astype(F32)


def tn_dot(a, b):
    return lax.dot_general(a, b, TN, preferred_element_type=F32)


def lane_sum(v):
    return jnp.sum(v, axis=1, keepdims=True)


def silu_twice_slope(half):
    t = jnp.tanh(half)
    act = half * (1.0 + t)
    return act, (1.0 + t) + act * (1.0 - t)


def slab(s, n=1):
    return pl.ds(s * LANES, n * LANES)


def strip_lines(lines, total):
    lane = lane_iota(CH)
    for rr, x, c in lines:
        if x is not None:
            v = pltpu.roll(x.astype(F32), (8 * rr + 2) % LANES, 1)
            total = jnp.where((lane >= 8 * rr) & (lane < 8 * rr + 4), v, total)
        if c is not None:
            v = pltpu.roll(c.astype(F32), (8 * rr + 5) % LANES, 1)
            total = jnp.where((lane >= 8 * rr + 4) & (lane < 8 * rr + 6), v, total)
    return total


def strip_kernel(part_ref, top_ref, bot_ref, out_ref):
    last = ROWS + 2
    lines = [
        (0, top_ref[0], None),
        (1, top_ref[1], top_ref[2]),
        (last, bot_ref[0], bot_ref[2]),
        (last + 1, bot_ref[1], None),
    ]
    out_ref[...] = strip_lines(lines, part_ref[...].astype(F32)).astype(BF16)


def input_strip(own_ref, left_ref, right_ref):
    own, left, right = (r[...].astype(F32) for r in (own_ref, left_ref, right_ref))
    pos = lane_iota(CH) % 8
    value = jnp.where(pos == 0, pltpu.roll(own, LANES - 1, 1), 0.0)
    value = jnp.where(pos == 1, pltpu.roll(left, 1, 1), value)
    value = jnp.where(pos == 2, right, value)
    value = jnp.where(pos == 3, pltpu.roll(left, 2, 1), value)
    value = jnp.where(pos == 4, pltpu.roll(right, 1, 1), value)
    return jnp.where(pos == 5, pltpu.roll(own, 3, 1), value)


def cotangent_strip(left_ref, right_ref):
    left, right = (r[...].astype(F32) for r in (left_ref, right_ref))
    pos = lane_iota(CH) % 8
    value = jnp.where(pos == 3, pltpu.roll(left, LANES - 1, 1), 0.0)
    return jnp.where(pos == 2, pltpu.roll(right, LANES - 3, 1), value)


def neighbours(v, strip, rr, first, last):
    edge = pltpu.roll(strip, (LANES - 8 * rr - 3) % LANES, 1)
    left = jnp.where(first, edge, pltpu.roll(v, 1, 1))
    right = jnp.where(last, edge, pltpu.roll(v, LANES - 1, 1))
    return left, right


def spread_gain(gain_ref):
    return jnp.broadcast_to(gain_ref[...], (LANES, CH)).T


def spread_taps(taps_ref, out_s):
    for n in range(EB // LANES):
        rows = slice(n * LANES, (n + 1) * LANES)
        block = jnp.concatenate([taps_ref[:, rows], jnp.zeros((7, LANES), F32)], axis=0).T
        block = 0.5 * block
        for t in range(9):
            out_s[rows, slab(t)] = jnp.broadcast_to(block[:, t : t + 1], (LANES, LANES))


class Chunks:
    def __init__(self, pairs, sems):
        self.pairs, self.sems = pairs, sems

    def copies(self, step):
        rows = pl.ds(pl.multiple_of(step * EB, EB), EB)
        slot = step % 2
        return [
            pltpu.make_async_copy(src.at[rows, :], dst.at[slot], self.sems.at[n, slot])
            for n, (src, dst) in enumerate(self.pairs)
        ]

    def start(self, step):
        for copy in self.copies(step):
            copy.start()

    def advance(self, step):
        for copy in self.copies(step):
            copy.wait()

        @pl.when(step < STEPS - 1)
        def _():
            self.start(step + 1)


def expand_kernel(
    x_ref, c_ref, gain_ref, wexp_ref, wprojt_ref,
    scaled_out, inv_out, part_out, pre_out, hid_out, gg_out, cot_s,
):
    @pl.when(pl.program_id(0) == 0)
    def _():
        gain = spread_gain(gain_ref)
        for r in range(ROWS):
            x = x_ref[r].astype(F32)
            inverse = lax.rsqrt(jnp.sum(x * x, axis=0, keepdims=True) / CH + EPS)
            inv_out[r : r + 1, :] = inverse
            scaled_out[:, slab(r)] = (x * inverse * gain).astype(BF16)
            cot_s[:, slab(r)] = c_ref[r]
        lines = [(r + 2, x_ref[r], c_ref[r]) for r in range(ROWS)]
        part_out[...] = strip_lines(lines, jnp.zeros((CH, LANES), F32)).astype(BF16)

    pre_out[...] = tn_dot(wexp_ref[...] * 0.5, scaled_out[...])
    gg_out[...] = tn_dot(wprojt_ref[...], cot_s[...])

    def body(i, carry):
        ds = pl.ds(pl.multiple_of(i * SUB, SUB), SUB)
        v = pre_out[ds, :]
        hid_out[ds, :] = (v * (1.0 + jnp.tanh(v))).astype(BF16)
        return carry

    lax.fori_loop(0, EB // SUB, body, 0)


def forward_kernel(
    top_ref, bot_ref, own_ref, left_ref, right_ref, gain_ref, wexp_ref, taps_ref, hid_any, gg_any,
    conv_out, sums_out, scaled_s, pre_s, taps_s, acc_s, hid_s, gg_s, sems,
):
    step = pl.program_id(0)
    chunks = Chunks(((hid_any, hid_s), (gg_any, gg_s)), sems)
    hid_ref, gg_ref = hid_s.at[step % 2], gg_s.at[step % 2]

    @pl.when(step == 0)
    def _():
        chunks.start(0)
        gain = 0.5 * spread_gain(gain_ref)
        for s in range(XS - ROWS):
            if s < 2:
                x = top_ref[s].astype(F32)
            elif s < 4:
                x = bot_ref[s - 2].astype(F32)
            else:
                x = input_strip(own_ref, left_ref, right_ref)
            inverse = lax.rsqrt(jnp.sum(x * x, axis=0, keepdims=True) / CH + EPS)
            scaled_s[:, slab(s)] = (x * inverse * gain).astype(BF16)
        sums_out[...] = jnp.zeros_like(sums_out)

    pre_s[...] = tn_dot(wexp_ref[...], scaled_s[...])
    spread_taps(taps_ref, taps_s)
    chunks.advance(step)
    lane = lane_iota(SUB)
    first, last = lane == 0, lane == LANES - 1

    def body(i, carry):
        ds = pl.ds(pl.multiple_of(i * SUB, SUB), SUB)
        k = [taps_s[ds, slab(t)] for t in range(9)]

        def hidden(s):
            if 2 <= s < ROWS + 2:
                return hid_ref[ds, slab(s - 2)].astype(F32)
            v = pre_s[ds, slab(s if s < 2 else s - ROWS)]
            return rounded(v * (1.0 + jnp.tanh(v)))

        strip = hidden(XS - 1)
        acc = [None] * (ROWS + 4)
        for rr in range(ROWS + 4):
            h = hidden(rr)
            hl, hr = neighbours(h, strip, rr, first, last)
            for a in (-1, 0, 1):
                o = rr - a
                if 1 <= o <= ROWS + 2:
                    t = 3 * (a + 1)
                    term = k[t] * hl + k[t + 1] * h + k[t + 2] * hr
                    acc[o] = term if acc[o] is None else acc[o] + term
        pooled = jnp.zeros((SUB, LANES), F32)
        gexc = jnp.zeros((SUB, LANES), F32)
        for o in range(1, ROWS + 3):
            v = acc[o]
            conv_out[ds, slab(o - 1)] = v
            if 2 <= o <= ROWS + 1:
                act = v * (1.0 + jnp.tanh(v))
                pooled = pooled + act
                gexc = gexc + act * gg_ref[ds, slab(o - 2)]
        edge = None
        for a in (-1, 0, 1):
            for c in (-1, 0, 1):
                shift = (-(8 * a + 2 * c)) % LANES
                term = k[3 * (a + 1) + c + 1] * (pltpu.roll(strip, shift, 1) if shift else strip)
                edge = term if edge is None else edge + term
        conv_out[ds, slab(CS - 1)] = edge
        acc_s[0, ds, :] = pooled
        acc_s[1, ds, :] = gexc
        return carry

    lax.fori_loop(0, EB // SUB, body, 0)
    for n in range(EB // LANES):
        for kind in range(2):
            row = jnp.sum(acc_s[kind, n * LANES : (n + 1) * LANES, :].T, axis=0, keepdims=True)
            sums_out[pl.ds(2 * (step * (EB // LANES) + n) + kind, 1), :] = row


def squeeze_excite(parts_ref, wsq_ref, wexc_ref, exc_s, gp_s, vec_out):
    pixels = 32768.0
    total = jnp.sum(parts_ref[...], axis=0)
    pooled = jnp.concatenate([total[2 * j : 2 * j + 1] for j in range(BLOCKS)], axis=1) / pixels
    gexc = jnp.concatenate([total[2 * j + 1 : 2 * j + 2] for j in range(BLOCKS)], axis=1)
    pooled = jnp.broadcast_to(pooled, (8, EX))
    gexc = jnp.broadcast_to(gexc, (8, EX))
    wsq, wexc = wsq_ref[...], wexc_ref[...]
    spre = lax.dot_general(pooled, wsq, NT, precision=HIGH, preferred_element_type=F32)
    sig = jax.nn.sigmoid(spre)
    squeezed = spre * sig
    epre = jnp.dot(squeezed, wexc, precision=HIGH, preferred_element_type=F32)
    excite = jax.nn.sigmoid(epre)
    gepre = gexc * excite * (1.0 - excite)
    gspre = lax.dot_general(gepre, wexc, NT, precision=HIGH, preferred_element_type=F32)
    gspre = gspre * (sig * (1.0 + spre * (1.0 - sig)))
    gpool = jnp.dot(gspre, wsq, precision=HIGH, preferred_element_type=F32)
    gpool = gpool / pixels
    vec_out[...] = jnp.zeros((16, LANES), F32)
    for j in range(BLOCKS):
        cols = slice(j * LANES, (j + 1) * LANES)
        exc_s[cols, :] = jnp.broadcast_to(excite[:1, cols], (LANES, LANES)).T
        gp_s[cols, :] = jnp.broadcast_to(gpool[:1, cols], (LANES, LANES)).T
        vec_out[j : j + 1, :] = pooled[:1, cols]
        vec_out[BLOCKS + j : BLOCKS + j + 1, :] = gepre[:1, cols]
    vec_out[12:13, :SQ] = squeezed[:1]
    vec_out[13:14, :SQ] = gspre[:1]


def backward_kernel(
    core_ref, parts_ref, wsq_ref, wexc_ref, x_ref, c_ref, top_ref, bot_ref, left_ref, right_ref,
    gain_ref, mask_ref, scaled_ref, inv_ref, gg_any, pre_any, conv_any, taps_ref, wexp_ref, wprojt_ref,
    out_out, gin_out, keep_any, send_any, vec_out,
    packed_s, exc_s, gp_s, rim_s, cot_s, gg_s, gated_s, gpre_s, taps_s, acc_s, tsum_s,
    ggc_s, prec_s, convc_s, sems, out_sems,
):
    step = pl.program_id(0)
    chunks = Chunks(((gg_any, ggc_s), (pre_any, prec_s), (conv_any, convc_s)), sems)
    gg_ref, pre_ref, conv_ref = (r.at[step % 2] for r in (ggc_s, prec_s, convc_s))

    @pl.when(step == 0)
    def _():
        chunks.start(0)
        squeeze_excite(parts_ref, wsq_ref, wexc_ref, exc_s, gp_s, vec_out)
        for r in range(ROWS):
            cot_s[:, slab(r)] = c_ref[r]
        rim_s[:, slab(0)] = top_ref[2]
        rim_s[:, slab(1)] = bot_ref[2]
        rim_s[:, slab(2)] = cotangent_strip(left_ref, right_ref).astype(BF16)
        gg_s[...] = tn_dot(wprojt_ref[...], rim_s[...])

    spread_taps(taps_ref, taps_s)
    chunks.advance(step)
    base = step * EB
    lane = lane_iota(SUB)
    first, last = lane == 0, lane == LANES - 1

    def body(i, carry):
        ds = pl.ds(pl.multiple_of(i * SUB, SUB), SUB)
        whole = pl.ds(pl.multiple_of(base + i * SUB, SUB), SUB)
        k = [taps_s[ds, slab(t)] for t in range(9)]
        exc, gp = exc_s[whole, :], 0.5 * gp_s[whole, :]
        half = 0.5 * exc

        def grad_conv(s, mask):
            act, slope = silu_twice_slope(conv_ref[ds, slab(s)])
            if 1 <= s <= ROWS:
                gated_s[whole, slab(s - 1)] = (act * exc).astype(BF16)
            if 1 <= s <= ROWS:
                g = gg_ref[ds, slab(s - 1)]
            else:
                g = gg_s[whole, slab(0 if s == 0 else s - ROWS)]
            g = (g * half + gp) * slope
            if mask is not None:
                g = jnp.where(mask_ref[mask : mask + 1, :] > 0.5, g, 0.0)
            return rounded(g)

        def hidden(r):
            act, slope = silu_twice_slope(pre_ref[ds, slab(r)])
            return rounded(act), slope

        strip = grad_conv(CS - 1, 2)
        tap = [None] * 9
        state = {}
        gh = {}
        for s in range(ROWS + 2):
            g = grad_conv(s, 0 if s == 0 else 1 if s == ROWS + 1 else None)
            gl, gr = neighbours(g, strip, s + 1, first, last)
            for a in (-1, 0, 1):
                r = s + a - 1
                if 0 <= r < ROWS:
                    if r not in state:
                        state[r] = hidden(r)
                    h = state[r][0]
                    t = 3 * (a + 1)
                    term = k[t] * gr + k[t + 1] * g + k[t + 2] * gl
                    gh[r] = term if r not in gh else gh[r] + term
                    for c, v in enumerate((gr, g, gl)):
                        tap[t + c] = h * v if tap[t + c] is None else tap[t + c] + h * v
            r = s - 2
            if 0 <= r:
                gpre_s[whole, slab(r)] = (gh.pop(r) * state.pop(r)[1]).astype(BF16)
        total = jnp.zeros((SUB, LANES), F32)
        for t in range(9):
            total = jnp.where(lane == t, lane_sum(tap[t]), total)
        acc_s[ds, :] = total
        return carry

    lax.fori_loop(0, EB // SUB, body, 0)
    for n in range(EB // LANES):
        taps = acc_s[n * LANES : (n + 1) * LANES, :].T
        block = step * (EB // LANES) + n
        for t in range(9):
            tsum_s[pl.ds(BLOCKS * t + block, 1), :] = taps[t : t + 1]

    @pl.when(step == STEPS - 1)
    def _():
        gated, gpre = gated_s[...], gpre_s[...]
        for which, w in enumerate(
            (
                lax.dot_general(scaled_ref[...], gpre, NT, preferred_element_type=F32),
                lax.dot_general(cot_s[...], gated, NT, preferred_element_type=F32),
            )
        ):
            for i in range(CH // 8):
                for n in range(BLOCKS):
                    group = (which * (CH // 8) + i) * BLOCKS + n
                    part = group // 9
                    row = PACK * (part % 2 * PARTS // 2 + part // 2) + 8 * (group % 9)
                    packed_s[row : row + 8, :] = w[8 * i : 8 * i + 8, slab(n)]
        gs_all = jnp.dot(wexp_ref[...], gpre, preferred_element_type=F32)
        ggain = jnp.zeros((CH, LANES), F32)
        for r in range(ROWS):
            normed = x_ref[r].astype(F32) * inv_ref[r : r + 1, :]
            ggain = ggain + gs_all[:, r * LANES : (r + 1) * LANES] * normed
        sums = jnp.broadcast_to(lane_sum(ggain), (CH, LANES)).T[:1]
        tsum_s[54:55, :] = sums[:, :LANES]
        tsum_s[55:56, :] = jnp.zeros((1, LANES), F32)
        tsum_s[55:56, : CH - LANES] = sums[:, LANES:]
        for d in range(PARTS):
            rows = slice((d % 2 * PARTS // 2 + d // 2) * PACK + 72, (d % 2 * PARTS // 2 + d // 2 + 1) * PACK)
            packed_s[rows, :] = jnp.zeros((8, LANES), F32)
            if d < 28:
                packed_s[rows.start : rows.start + 2, :] = tsum_s[2 * d : 2 * d + 2, :]
        core, half = core_ref[0], PARTS // 2 * PACK
        sends = [
            pltpu.make_async_copy(
                packed_s.at[pl.ds(pl.multiple_of(half * which, 8), half), :], dst, out_sems.at[n]
            )
            for n, (which, dst) in enumerate(((core, keep_any), (1 - core, send_any)))
        ]
        for copy in sends:
            copy.start()
        proj = jnp.dot(wprojt_ref[...], gated, preferred_element_type=F32)
        gain = spread_gain(gain_ref)
        for r in range(ROWS):
            x = x_ref[r].astype(F32)
            out_out[r] = (x + proj[:, r * LANES : (r + 1) * LANES]).astype(BF16)
            inverse = inv_ref[r : r + 1, :]
            normed = x * inverse
            gnormed = gs_all[:, r * LANES : (r + 1) * LANES] * gain
            mean = jnp.sum(gnormed * normed, axis=0, keepdims=True) / CH
            gin_out[r] = (inverse * (gnormed - normed * mean) + c_ref[r].astype(F32)).astype(BF16)
        for copy in sends:
            copy.wait()


def to_half(v):
    row = lax.broadcasted_iota(jnp.int32, (1, PACK, 1), 1)
    size = jnp.abs(v)

    def exponent(where):
        top = jnp.max(jnp.where(where, size, 0.0), axis=(1, 2), keepdims=True)
        return jnp.ceil(jnp.log2(jnp.maximum(top, 1e-30)))

    e_big, e_small = exponent(row < 72), exponent((row >= 72) & (row < 74))
    scaled = v * jnp.where(row < 72, jnp.exp2(-e_big), jnp.exp2(-e_small))
    return jnp.where(row < 74, scaled, jnp.where(row < 77, e_big, e_small)).astype(jnp.float16)


def from_half(h):
    v = h.astype(F32)
    row = lax.broadcasted_iota(jnp.int32, (1, PACK, 1), 1)
    scale = jnp.where(row < 72, jnp.exp2(v[:, 74:75]), jnp.exp2(v[:, 77:78]))
    return jnp.where(row < 74, v * scale, 0.0)


def shape(*dims, dtype=F32):
    return jax.ShapeDtypeStruct(dims, dtype)


def full(*dims):
    return pl.BlockSpec(dims, lambda j: (0,) * len(dims))


def params(grid=True):
    return pltpu.CompilerParams(
        dimension_semantics=("arbitrary",) if grid else None, vmem_limit_bytes=VMEM
    )


def cost(flops, moved):
    return pl.CostEstimate(flops=int(flops), bytes_accessed=int(moved), transcendentals=0)


def exchanged(blocks):
    return lax.all_to_all(blocks, RC, 0, 0, tiled=True, axis_index_groups=CHIPS)


def gathered(block):
    return exchanged(jnp.broadcast_to(block[None], (PARTS // 2,) + block.shape))


def partner(block):
    return lax.ppermute(block, "col", [(i, i ^ 1) for i in range(4)])


def local(inputs, norm_gain, w_expand, kernel, w_squeeze, w_excite, w_project, cotangent):
    nrow, ncol = lax.axis_size("row"), lax.axis_size("col")
    row, col = lax.axis_index("row"), lax.axis_index("col")
    x = inputs[0].transpose(1, 0, 2)
    c = cotangent[0].transpose(1, 0, 2)
    fwd_row = [(i, i + 1) for i in range(nrow - 1)]
    bwd_row = [(i + 1, i) for i in range(nrow - 1)]
    fwd_col = [(i, i + 1) for i in range(ncol - 1)]
    bwd_col = [(i + 1, i) for i in range(ncol - 1)]
    top = lax.ppermute(jnp.concatenate([x[6:8], c[7:8]], axis=0), "row", fwd_row)
    bot = lax.ppermute(jnp.concatenate([x[0:2], c[0:1]], axis=0), "row", bwd_row)
    gain = norm_gain[None, :]
    wprojt, taps = w_project.T, kernel.T
    halo = full(3, CH, LANES)
    tile = full(ROWS, CH, LANES)
    edge = full(CH, LANES)
    weight = full(CH, EX)
    anywhere = pl.BlockSpec(memory_space=pl.ANY)
    chunk_rows = lambda width: pl.BlockSpec((EB, width), lambda j: (j, 0))
    chunk_cols = pl.BlockSpec((CH, EB), lambda j: (0, j))
    chunk_taps = pl.BlockSpec((9, EB), lambda j: (0, j))
    scaled, inv, part, pre, hid, gg = pl.pallas_call(
        expand_kernel,
        grid=(STEPS,),
        in_specs=[tile, tile, full(1, CH), chunk_cols, chunk_cols],
        out_specs=[full(CH, ROWS * LANES), full(ROWS, LANES), edge, chunk_rows(ROWS * LANES),
                   chunk_rows(ROWS * LANES), chunk_rows(ROWS * LANES)],
        out_shape=[shape(CH, ROWS * LANES, dtype=BF16), shape(ROWS, LANES),
                   shape(CH, LANES, dtype=BF16),
                   shape(EX, ROWS * LANES), shape(EX, ROWS * LANES, dtype=BF16),
                   shape(EX, ROWS * LANES)],
        scratch_shapes=[pltpu.VMEM((CH, ROWS * LANES), BF16)],
        compiler_params=params(),
        cost_estimate=cost(600e6, 10e6),
        name="expand",
    )(x, c, gain, w_expand, wprojt)
    own = pl.pallas_call(
        strip_kernel,
        out_shape=shape(CH, LANES, dtype=BF16),
        compiler_params=params(False),
        cost_estimate=cost(1e6, 1e6),
        name="strip",
    )(part, top, bot)
    left = lax.ppermute(own, "col", fwd_col)
    right = lax.ppermute(own, "col", bwd_col)

    line = lax.broadcasted_iota(jnp.int32, (8, LANES), 1) // 8
    pos = lax.broadcasted_iota(jnp.int32, (8, LANES), 1) % 8
    kind = lax.broadcasted_iota(jnp.int32, (8, LANES), 0)
    top_ok, bot_ok = row > 0, row < nrow - 1
    strip_ok = ((pos == 3) & (col > 0)) | ((pos == 2) & (col < ncol - 1))
    strip_ok &= ((line > 1) | top_ok) & ((line < ROWS + 2) | bot_ok)
    mask = ((kind == 0) & top_ok) | ((kind == 1) & bot_ok) | ((kind == 2) & strip_ok)
    mask = mask.astype(F32)
    conv, sums = pl.pallas_call(
        forward_kernel,
        grid=(STEPS,),
        in_specs=[halo, halo, edge, edge, edge, full(1, CH), chunk_cols, chunk_taps,
                  anywhere, anywhere],
        out_specs=[chunk_rows(CS * LANES), full(16, LANES)],
        out_shape=[shape(EX, CS * LANES), shape(16, LANES)],
        scratch_shapes=[
            pltpu.VMEM((CH, (XS - ROWS) * LANES), BF16),
            pltpu.VMEM((EB, (XS - ROWS) * LANES), F32),
            pltpu.VMEM((EB, 9 * LANES), F32),
            pltpu.VMEM((2, EB, LANES), F32),
            pltpu.VMEM((2, EB, ROWS * LANES), BF16),
            pltpu.VMEM((2, EB, ROWS * LANES), F32),
            pltpu.SemaphoreType.DMA((2, 2)),
        ],
        compiler_params=params(),
        cost_estimate=cost(200e6, 12e6),
        name="forward",
    )(top, bot, own, left, right, gain, w_expand, taps, hid, gg)

    sums = gathered(sums + partner(sums))
    core = (col % 2).astype(jnp.int32).reshape(1)
    out, gin, keep, send, vec = pl.pallas_call(
        backward_kernel,
        grid=(STEPS,),
        in_specs=[pl.BlockSpec(memory_space=pltpu.SMEM), full(PARTS // 2, 16, LANES),
                  full(SQ, EX), full(SQ, EX), tile, tile, halo, halo, edge, edge, full(1, CH),
                  full(8, LANES), full(CH, ROWS * LANES), full(ROWS, LANES),
                  anywhere, anywhere, anywhere, chunk_taps,
                  weight, weight],
        out_specs=[tile, tile, anywhere, anywhere, full(16, LANES)],
        out_shape=[shape(ROWS, CH, LANES, dtype=BF16), shape(ROWS, CH, LANES, dtype=BF16),
                   shape(PARTS // 2 * PACK, LANES), shape(PARTS // 2 * PACK, LANES),
                   shape(16, LANES)],
        scratch_shapes=[
            pltpu.VMEM((PARTS * PACK, LANES), F32),
            pltpu.VMEM((EX, LANES), F32),
            pltpu.VMEM((EX, LANES), F32),
            pltpu.VMEM((CH, 3 * LANES), BF16),
            pltpu.VMEM((CH, ROWS * LANES), BF16),
            pltpu.VMEM((EX, 3 * LANES), F32),
            pltpu.VMEM((EX, ROWS * LANES), BF16),
            pltpu.VMEM((EX, ROWS * LANES), BF16),
            pltpu.VMEM((EB, 9 * LANES), F32),
            pltpu.VMEM((EB, LANES), F32),
            pltpu.VMEM((56, LANES), F32),
            pltpu.VMEM((2, EB, ROWS * LANES), F32),
            pltpu.VMEM((2, EB, ROWS * LANES), F32),
            pltpu.VMEM((2, EB, CS * LANES), F32),
            pltpu.SemaphoreType.DMA((3, 2)),
            pltpu.SemaphoreType.DMA((2,)),
        ],
        compiler_params=params(),
        cost_estimate=cost(1500e6, 16e6),
        name="backward",
    )(core, sums, w_squeeze.T, w_excite, x, c, top, bot, left, right, gain, mask, scaled, inv, gg, pre, conv, taps,
      w_expand, wprojt)

    halves = to_half((keep + partner(send)).reshape(PARTS // 2, PACK, LANES))
    mine = exchanged(halves)
    total = jnp.sum(from_half(mine), axis=0)
    vecs = vec[None]
    sample = lax.axis_index("dp")
    for bit in (1, 2, 4):
        both = lax.ppermute(
            jnp.concatenate([total, vecs.reshape(16 * bit, LANES)], axis=0),
            "dp",
            [(i, i ^ bit) for i in range(8)],
        )
        total = total + both[:PACK]
        theirs = both[PACK:].reshape(bit, 16, LANES)
        ahead = (sample & bit) == 0
        vecs = jnp.concatenate(
            [jnp.where(ahead, vecs, theirs), jnp.where(ahead, theirs, vecs)], axis=0
        )
    vecs = vecs.reshape(8, 2048)
    grad_wexc = jnp.einsum("bs,be->se", vecs[:, 1536:1584], vecs[:, 768:1536], precision=HIGH)
    grad_wsq = jnp.einsum("be,bs->es", vecs[:, :768], vecs[:, 1664:1712], precision=HIGH)
    same = gathered(to_half(total[None])[0])
    other = partner(same)
    even = core[0] == 0
    every = jnp.stack(
        [jnp.where(even, same, other), jnp.where(even, other, same)], axis=1
    ).reshape(PARTS, PACK, LANES).astype(F32)
    big = (every[:, :72] * jnp.exp2(every[:, 74:75])).reshape(2, CH // 8, BLOCKS, 8, LANES)
    big = big.transpose(0, 1, 3, 2, 4).reshape(2, CH, EX)
    small = (every[:, 72:74] * jnp.exp2(every[:, 77:78])).reshape(8192)
    return (
        out.transpose(1, 0, 2)[None],
        gin.transpose(1, 0, 2)[None],
        small[6912:7104],
        big[0],
        small[:6912].reshape(9, 768).T,
        grad_wsq,
        grad_wexc,
        big[1].T,
    )


def solution(mesh):
    placed = (
        P("dp", None, "row", "col"),
        P(),
        P(),
        P(),
        P(),
        P(),
        P(),
        P("dp", None, "row", "col"),
    )
    return jax.shard_map(
        local,
        mesh=mesh,
        in_specs=placed,
        out_specs=(
            P("dp", None, "row", "col"),
            P("dp", None, "row", "col"),
            P(),
            P(),
            P(),
            P(),
            P(),
            P(),
        ),
        check_vma=False,
    )
```

```python
import jax
import jax.numpy as jnp
from jax import lax
from jax.experimental import pallas as pl
from jax.experimental.pallas import tpu as pltpu
from jax.sharding import PartitionSpec as P

EPS = 1e-06
HIGH = lax.Precision.HIGHEST
RC = ("row", "col")
F32, BF16 = jnp.float32, jnp.bfloat16
CH, EX, SQ = 192, 768, 48
ROWS, LANES = 8, 128
EB = 256
SUB = 16
STEPS = EX // EB
BLOCKS = EX // LANES
PARTS, PACK = 32, 80
VMEM_KIB = 60 * 1024
CHIPS = [[2 * q + core for q in range(PARTS // 2)] for core in range(2)]
XS = ROWS + 5
CS = ROWS + 3
NT = (((1,), (1,)), ((), ()))
TN = (((0,), (0,)), ((), ()))


def lane_iota(rows):
    return lax.broadcasted_iota(jnp.int32, (rows, LANES), 1)


def rounded(v):
    return v.astype(BF16).astype(F32)


def tn_dot(a, b):
    return lax.dot_general(a, b, TN, preferred_element_type=F32)


def lane_sum(v):
    return jnp.sum(v, axis=1, keepdims=True)


def silu_twice_slope(half):
    t = jnp.tanh(half)
    act = half * (1.0 + t)
    return act, (1.0 + t) + act * (1.0 - t)


def slab(s, n=1):
    return pl.ds(s * LANES, n * LANES)


def strip_lines(lines, total):
    lane = lane_iota(CH)
    for rr, x, c in lines:
        if x is not None:
            v = pltpu.roll(x.astype(F32), (8 * rr + 2) % LANES, 1)
            total = jnp.where((lane >= 8 * rr) & (lane < 8 * rr + 4), v, total)
        if c is not None:
            v = pltpu.roll(c.astype(F32), (8 * rr + 5) % LANES, 1)
            total = jnp.where((lane >= 8 * rr + 4) & (lane < 8 * rr + 6), v, total)
    return total


def strip_kernel(part_ref, top_ref, bot_ref, out_ref):
    last = ROWS + 2
    lines = [
        (0, top_ref[0], None),
        (1, top_ref[1], top_ref[2]),
        (last, bot_ref[0], bot_ref[2]),
        (last + 1, bot_ref[1], None),
    ]
    out_ref[...] = strip_lines(lines, part_ref[...].astype(F32)).astype(BF16)


def input_strip(own_ref, left_ref, right_ref):
    own, left, right = (r[...].astype(F32) for r in (own_ref, left_ref, right_ref))
    pos = lane_iota(CH) % 8
    value = jnp.where(pos == 0, pltpu.roll(own, LANES - 1, 1), 0.0)
    value = jnp.where(pos == 1, pltpu.roll(left, 1, 1), value)
    value = jnp.where(pos == 2, right, value)
    value = jnp.where(pos == 3, pltpu.roll(left, 2, 1), value)
    value = jnp.where(pos == 4, pltpu.roll(right, 1, 1), value)
    return jnp.where(pos == 5, pltpu.roll(own, 3, 1), value)


def cotangent_strip(left_ref, right_ref):
    left, right = (r[...].astype(F32) for r in (left_ref, right_ref))
    pos = lane_iota(CH) % 8
    value = jnp.where(pos == 3, pltpu.roll(left, LANES - 1, 1), 0.0)
    return jnp.where(pos == 2, pltpu.roll(right, LANES - 3, 1), value)


def neighbours(v, strip, rr, first, last):
    edge = pltpu.roll(strip, (LANES - 8 * rr - 3) % LANES, 1)
    left = jnp.where(first, edge, pltpu.roll(v, 1, 1))
    right = jnp.where(last, edge, pltpu.roll(v, LANES - 1, 1))
    return left, right


def spread_gain(gain_ref):
    return jnp.broadcast_to(gain_ref[...], (LANES, CH)).T


def spread_taps(taps_ref, out_s):
    for n in range(EB // LANES):
        rows = slice(n * LANES, (n + 1) * LANES)
        block = jnp.concatenate([taps_ref[:, rows], jnp.zeros((7, LANES), F32)], axis=0).T
        block = 0.5 * block
        for t in range(9):
            out_s[rows, slab(t)] = jnp.broadcast_to(block[:, t : t + 1], (LANES, LANES))


class Chunks:
    def __init__(self, pairs, sems):
        self.pairs, self.sems = pairs, sems

    def copies(self, step):
        rows = pl.ds(pl.multiple_of(step * EB, EB), EB)
        slot = step % 2
        return [
            pltpu.make_async_copy(src.at[rows, :], dst.at[slot], self.sems.at[n, slot])
            for n, (src, dst) in enumerate(self.pairs)
        ]

    def start(self, step):
        for copy in self.copies(step):
            copy.start()

    def advance(self, step):
        for copy in self.copies(step):
            copy.wait()

        @pl.when(step < STEPS - 1)
        def _():
            self.start(step + 1)


def expand_kernel(
    x_ref, c_ref, gain_ref, wexp_ref, wprojt_ref,
    scaled_out, inv_out, part_out, pre_out, hid_out, gg_out, cot_s,
):
    @pl.when(pl.program_id(0) == 0)
    def _():
        gain = spread_gain(gain_ref)
        for r in range(ROWS):
            x = x_ref[r].astype(F32)
            inverse = lax.rsqrt(jnp.sum(x * x, axis=0, keepdims=True) / CH + EPS)
            inv_out[r : r + 1, :] = inverse
            scaled_out[:, slab(r)] = (x * inverse * gain).astype(BF16)
            cot_s[:, slab(r)] = c_ref[r]
        lines = [(r + 2, x_ref[r], c_ref[r]) for r in range(ROWS)]
        part_out[...] = strip_lines(lines, jnp.zeros((CH, LANES), F32)).astype(BF16)

    pre_out[...] = tn_dot(wexp_ref[...] * 0.5, scaled_out[...])
    gg_out[...] = tn_dot(wprojt_ref[...], cot_s[...])

    def body(i, carry):
        ds = pl.ds(pl.multiple_of(i * SUB, SUB), SUB)
        v = pre_out[ds, :]
        hid_out[ds, :] = (v * (1.0 + jnp.tanh(v))).astype(BF16)
        return carry

    lax.fori_loop(0, EB // SUB, body, 0, unroll=4)


def forward_kernel(
    top_ref, bot_ref, own_ref, left_ref, right_ref, gain_ref, wexp_ref, taps_ref, hid_any, gg_any,
    conv_out, sums_out, scaled_s, pre_s, taps_s, acc_s, hid_s, gg_s, sems,
):
    step = pl.program_id(0)
    chunks = Chunks(((hid_any, hid_s), (gg_any, gg_s)), sems)
    hid_ref, gg_ref = hid_s.at[step % 2], gg_s.at[step % 2]

    @pl.when(step == 0)
    def _():
        chunks.start(0)
        gain = 0.5 * spread_gain(gain_ref)
        for s in range(XS - ROWS):
            if s < 2:
                x = top_ref[s].astype(F32)
            elif s < 4:
                x = bot_ref[s - 2].astype(F32)
            else:
                x = input_strip(own_ref, left_ref, right_ref)
            inverse = lax.rsqrt(jnp.sum(x * x, axis=0, keepdims=True) / CH + EPS)
            scaled_s[:, slab(s)] = (x * inverse * gain).astype(BF16)
        sums_out[...] = jnp.zeros_like(sums_out)

    pre_s[...] = tn_dot(wexp_ref[...], scaled_s[...])
    spread_taps(taps_ref, taps_s)
    chunks.advance(step)
    lane = lane_iota(SUB)
    first, last = lane == 0, lane == LANES - 1

    def body(i, carry):
        ds = pl.ds(pl.multiple_of(i * SUB, SUB), SUB)
        k = [taps_s[ds, slab(t)] for t in range(9)]

        def hidden(s):
            if 2 <= s < ROWS + 2:
                return hid_ref[ds, slab(s - 2)].astype(F32)
            v = pre_s[ds, slab(s if s < 2 else s - ROWS)]
            return rounded(v * (1.0 + jnp.tanh(v)))

        strip = hidden(XS - 1)
        acc = [None] * (ROWS + 4)
        for rr in range(ROWS + 4):
            h = hidden(rr)
            hl, hr = neighbours(h, strip, rr, first, last)
            for a in (-1, 0, 1):
                o = rr - a
                if 1 <= o <= ROWS + 2:
                    t = 3 * (a + 1)
                    term = k[t] * hl + k[t + 1] * h + k[t + 2] * hr
                    acc[o] = term if acc[o] is None else acc[o] + term
        pooled = jnp.zeros((SUB, LANES), F32)
        gexc = jnp.zeros((SUB, LANES), F32)
        for o in range(1, ROWS + 3):
            v = acc[o]
            conv_out[ds, slab(o - 1)] = v
            if 2 <= o <= ROWS + 1:
                act = v * (1.0 + jnp.tanh(v))
                pooled = pooled + act
                gexc = gexc + act * gg_ref[ds, slab(o - 2)]
        edge = None
        for a in (-1, 0, 1):
            for c in (-1, 0, 1):
                shift = (-(8 * a + 2 * c)) % LANES
                term = k[3 * (a + 1) + c + 1] * (pltpu.roll(strip, shift, 1) if shift else strip)
                edge = term if edge is None else edge + term
        conv_out[ds, slab(CS - 1)] = edge
        acc_s[0, ds, :] = pooled
        acc_s[1, ds, :] = gexc
        return carry

    lax.fori_loop(0, EB // SUB, body, 0, unroll=8)
    for n in range(EB // LANES):
        for kind in range(2):
            row = jnp.sum(acc_s[kind, n * LANES : (n + 1) * LANES, :].T, axis=0, keepdims=True)
            sums_out[pl.ds(2 * (step * (EB // LANES) + n) + kind, 1), :] = row


def squeeze_excite(parts_ref, wsq_ref, wexc_ref, exc_s, gp_s, vec_out):
    pixels = 32768.0
    total = jnp.sum(parts_ref[...], axis=0)
    pooled = jnp.concatenate([total[2 * j : 2 * j + 1] for j in range(BLOCKS)], axis=1) / pixels
    gexc = jnp.concatenate([total[2 * j + 1 : 2 * j + 2] for j in range(BLOCKS)], axis=1)
    pooled = jnp.broadcast_to(pooled, (8, EX))
    gexc = jnp.broadcast_to(gexc, (8, EX))
    wsq, wexc = wsq_ref[...], wexc_ref[...]
    spre = lax.dot_general(pooled, wsq, NT, precision=HIGH, preferred_element_type=F32)
    sig = jax.nn.sigmoid(spre)
    squeezed = spre * sig
    epre = jnp.dot(squeezed, wexc, precision=HIGH, preferred_element_type=F32)
    excite = jax.nn.sigmoid(epre)
    gepre = gexc * excite * (1.0 - excite)
    gspre = lax.dot_general(gepre, wexc, NT, precision=HIGH, preferred_element_type=F32)
    gspre = gspre * (sig * (1.0 + spre * (1.0 - sig)))
    gpool = jnp.dot(gspre, wsq, precision=HIGH, preferred_element_type=F32)
    gpool = gpool / pixels
    vec_out[...] = jnp.zeros((16, LANES), F32)
    for j in range(BLOCKS):
        cols = slice(j * LANES, (j + 1) * LANES)
        exc_s[cols, :] = jnp.broadcast_to(excite[:1, cols], (LANES, LANES)).T
        gp_s[cols, :] = jnp.broadcast_to(gpool[:1, cols], (LANES, LANES)).T
        vec_out[j : j + 1, :] = pooled[:1, cols]
        vec_out[BLOCKS + j : BLOCKS + j + 1, :] = gepre[:1, cols]
    vec_out[12:13, :SQ] = squeezed[:1]
    vec_out[13:14, :SQ] = gspre[:1]


def backward_kernel(
    core_ref, parts_ref, wsq_ref, wexc_ref, x_ref, c_ref, top_ref, bot_ref, left_ref, right_ref,
    gain_ref, mask_ref, scaled_ref, inv_ref, gg_any, pre_any, conv_any, taps_ref, wexp_ref, wprojt_ref,
    out_out, gin_out, keep_any, send_any, vec_out,
    packed_s, exc_s, gp_s, rim_s, cot_s, gg_s, gated_s, gpre_s, taps_s, acc_s, tsum_s,
    ggc_s, prec_s, convc_s, sems, out_sems,
):
    step = pl.program_id(0)
    chunks = Chunks(((gg_any, ggc_s), (pre_any, prec_s), (conv_any, convc_s)), sems)
    gg_ref, pre_ref, conv_ref = (r.at[step % 2] for r in (ggc_s, prec_s, convc_s))

    @pl.when(step == 0)
    def _():
        chunks.start(0)
        squeeze_excite(parts_ref, wsq_ref, wexc_ref, exc_s, gp_s, vec_out)
        for r in range(ROWS):
            cot_s[:, slab(r)] = c_ref[r]
        rim_s[:, slab(0)] = top_ref[2]
        rim_s[:, slab(1)] = bot_ref[2]
        rim_s[:, slab(2)] = cotangent_strip(left_ref, right_ref).astype(BF16)
        gg_s[...] = tn_dot(wprojt_ref[...], rim_s[...])

    spread_taps(taps_ref, taps_s)
    chunks.advance(step)
    base = step * EB
    lane = lane_iota(SUB)
    first, last = lane == 0, lane == LANES - 1

    def body(i, carry):
        ds = pl.ds(pl.multiple_of(i * SUB, SUB), SUB)
        whole = pl.ds(pl.multiple_of(base + i * SUB, SUB), SUB)
        k = [taps_s[ds, slab(t)] for t in range(9)]
        exc, gp = exc_s[whole, :], 0.5 * gp_s[whole, :]
        half = 0.5 * exc

        def grad_conv(s, mask):
            act, slope = silu_twice_slope(conv_ref[ds, slab(s)])
            if 1 <= s <= ROWS:
                gated_s[whole, slab(s - 1)] = (act * exc).astype(BF16)
            if 1 <= s <= ROWS:
                g = gg_ref[ds, slab(s - 1)]
            else:
                g = gg_s[whole, slab(0 if s == 0 else s - ROWS)]
            g = (g * half + gp) * slope
            if mask is not None:
                g = jnp.where(mask_ref[mask : mask + 1, :] > 0.5, g, 0.0)
            return rounded(g)

        def hidden(r):
            act, slope = silu_twice_slope(pre_ref[ds, slab(r)])
            return rounded(act), slope

        strip = grad_conv(CS - 1, 2)
        tap = [None] * 9
        state = {}
        gh = {}
        for s in range(ROWS + 2):
            g = grad_conv(s, 0 if s == 0 else 1 if s == ROWS + 1 else None)
            gl, gr = neighbours(g, strip, s + 1, first, last)
            for a in (-1, 0, 1):
                r = s + a - 1
                if 0 <= r < ROWS:
                    if r not in state:
                        state[r] = hidden(r)
                    h = state[r][0]
                    t = 3 * (a + 1)
                    term = k[t] * gr + k[t + 1] * g + k[t + 2] * gl
                    gh[r] = term if r not in gh else gh[r] + term
                    for c, v in enumerate((gr, g, gl)):
                        tap[t + c] = h * v if tap[t + c] is None else tap[t + c] + h * v
            r = s - 2
            if 0 <= r:
                gpre_s[whole, slab(r)] = (gh.pop(r) * state.pop(r)[1]).astype(BF16)
        total = jnp.zeros((SUB, LANES), F32)
        for t in range(9):
            total = jnp.where(lane == t, lane_sum(tap[t]), total)
        acc_s[ds, :] = total
        return carry

    lax.fori_loop(0, EB // SUB, body, 0, unroll=2)
    for n in range(EB // LANES):
        taps = acc_s[n * LANES : (n + 1) * LANES, :].T
        block = step * (EB // LANES) + n
        for t in range(9):
            tsum_s[pl.ds(BLOCKS * t + block, 1), :] = taps[t : t + 1]

    @pl.when(step == STEPS - 1)
    def _():
        gated, gpre = gated_s[...], gpre_s[...]
        for which, w in enumerate(
            (
                lax.dot_general(scaled_ref[...], gpre, NT, preferred_element_type=F32),
                lax.dot_general(cot_s[...], gated, NT, preferred_element_type=F32),
            )
        ):
            for i in range(CH // 8):
                for n in range(BLOCKS):
                    group = (which * (CH // 8) + i) * BLOCKS + n
                    part = group // 9
                    row = PACK * (part % 2 * PARTS // 2 + part // 2) + 8 * (group % 9)
                    packed_s[row : row + 8, :] = w[8 * i : 8 * i + 8, slab(n)]
        gs_all = jnp.dot(wexp_ref[...], gpre, preferred_element_type=F32)
        ggain = jnp.zeros((CH, LANES), F32)
        for r in range(ROWS):
            normed = x_ref[r].astype(F32) * inv_ref[r : r + 1, :]
            ggain = ggain + gs_all[:, r * LANES : (r + 1) * LANES] * normed
        sums = jnp.broadcast_to(lane_sum(ggain), (CH, LANES)).T[:1]
        tsum_s[54:55, :] = sums[:, :LANES]
        tsum_s[55:56, :] = jnp.zeros((1, LANES), F32)
        tsum_s[55:56, : CH - LANES] = sums[:, LANES:]
        for d in range(PARTS):
            rows = slice((d % 2 * PARTS // 2 + d // 2) * PACK + 72, (d % 2 * PARTS // 2 + d // 2 + 1) * PACK)
            packed_s[rows, :] = jnp.zeros((8, LANES), F32)
            if d < 28:
                packed_s[rows.start : rows.start + 2, :] = tsum_s[2 * d : 2 * d + 2, :]
        core, half = core_ref[0], PARTS // 2 * PACK
        sends = [
            pltpu.make_async_copy(
                packed_s.at[pl.ds(pl.multiple_of(half * which, 8), half), :], dst, out_sems.at[n]
            )
            for n, (which, dst) in enumerate(((core, keep_any), (1 - core, send_any)))
        ]
        for copy in sends:
            copy.start()
        proj = jnp.dot(wprojt_ref[...], gated, preferred_element_type=F32)
        gain = spread_gain(gain_ref)
        for r in range(ROWS):
            x = x_ref[r].astype(F32)
            out_out[r] = (x + proj[:, r * LANES : (r + 1) * LANES]).astype(BF16)
            inverse = inv_ref[r : r + 1, :]
            normed = x * inverse
            gnormed = gs_all[:, r * LANES : (r + 1) * LANES] * gain
            mean = jnp.sum(gnormed * normed, axis=0, keepdims=True) / CH
            gin_out[r] = (inverse * (gnormed - normed * mean) + c_ref[r].astype(F32)).astype(BF16)
        for copy in sends:
            copy.wait()


def to_half(v):
    row = lax.broadcasted_iota(jnp.int32, (1, PACK, 1), 1)
    size = jnp.abs(v)

    def exponent(where):
        top = jnp.max(jnp.where(where, size, 0.0), axis=(1, 2), keepdims=True)
        return jnp.ceil(jnp.log2(jnp.maximum(top, 1e-30)))

    e_big, e_small = exponent(row < 72), exponent((row >= 72) & (row < 74))
    scaled = v * jnp.where(row < 72, jnp.exp2(-e_big), jnp.exp2(-e_small))
    return jnp.where(row < 74, scaled, jnp.where(row < 77, e_big, e_small)).astype(jnp.float16)


def from_half(h):
    v = h.astype(F32)
    row = lax.broadcasted_iota(jnp.int32, (1, PACK, 1), 1)
    scale = jnp.where(row < 72, jnp.exp2(v[:, 74:75]), jnp.exp2(v[:, 77:78]))
    return jnp.where(row < 74, v * scale, 0.0)


def shape(*dims, dtype=F32):
    return jax.ShapeDtypeStruct(dims, dtype)


def full(*dims):
    return pl.BlockSpec(dims, lambda j: (0,) * len(dims))


def params(grid=True, kib=VMEM_KIB):
    return pltpu.CompilerParams(
        dimension_semantics=("arbitrary",) if grid else None, vmem_limit_bytes=kib * 1024
    )


def cost(flops, moved):
    return pl.CostEstimate(flops=int(flops), bytes_accessed=int(moved), transcendentals=0)


def exchanged(blocks):
    return lax.all_to_all(blocks, RC, 0, 0, tiled=True, axis_index_groups=CHIPS)


def gathered(block):
    return exchanged(jnp.broadcast_to(block[None], (PARTS // 2,) + block.shape))


def partner(block):
    return lax.ppermute(block, "col", [(i, i ^ 1) for i in range(4)])


def local(inputs, norm_gain, w_expand, kernel, w_squeeze, w_excite, w_project, cotangent):
    nrow, ncol = lax.axis_size("row"), lax.axis_size("col")
    row, col = lax.axis_index("row"), lax.axis_index("col")
    x = inputs[0].transpose(1, 0, 2)
    c = cotangent[0].transpose(1, 0, 2)
    fwd_row = [(i, i + 1) for i in range(nrow - 1)]
    bwd_row = [(i + 1, i) for i in range(nrow - 1)]
    fwd_col = [(i, i + 1) for i in range(ncol - 1)]
    bwd_col = [(i + 1, i) for i in range(ncol - 1)]
    top = lax.ppermute(jnp.concatenate([x[6:8], c[7:8]], axis=0), "row", fwd_row)
    bot = lax.ppermute(jnp.concatenate([x[0:2], c[0:1]], axis=0), "row", bwd_row)
    gain = norm_gain[None, :]
    wprojt, taps = w_project.T, kernel.T
    halo = full(3, CH, LANES)
    tile = full(ROWS, CH, LANES)
    edge = full(CH, LANES)
    weight = full(CH, EX)
    anywhere = pl.BlockSpec(memory_space=pl.ANY)
    chunk_rows = lambda width: pl.BlockSpec((EB, width), lambda j: (j, 0))
    chunk_cols = pl.BlockSpec((CH, EB), lambda j: (0, j))
    chunk_taps = pl.BlockSpec((9, EB), lambda j: (0, j))
    scaled, inv, part, pre, hid, gg = pl.pallas_call(
        expand_kernel,
        grid=(STEPS,),
        in_specs=[tile, tile, full(1, CH), chunk_cols, chunk_cols],
        out_specs=[full(CH, ROWS * LANES), full(ROWS, LANES), edge, chunk_rows(ROWS * LANES),
                   chunk_rows(ROWS * LANES), chunk_rows(ROWS * LANES)],
        out_shape=[shape(CH, ROWS * LANES, dtype=BF16), shape(ROWS, LANES),
                   shape(CH, LANES, dtype=BF16),
                   shape(EX, ROWS * LANES), shape(EX, ROWS * LANES, dtype=BF16),
                   shape(EX, ROWS * LANES)],
        scratch_shapes=[pltpu.VMEM((CH, ROWS * LANES), BF16)],
        compiler_params=params(),
        cost_estimate=cost(600e6, 10e6),
        name="expand",
    )(x, c, gain, w_expand, wprojt)
    own = pl.pallas_call(
        strip_kernel,
        out_shape=shape(CH, LANES, dtype=BF16),
        compiler_params=params(False, 4096),
        cost_estimate=cost(1e6, 1e6),
        name="strip",
    )(part, top, bot)
    left = lax.ppermute(own, "col", fwd_col)
    right = lax.ppermute(own, "col", bwd_col)

    line = lax.broadcasted_iota(jnp.int32, (8, LANES), 1) // 8
    pos = lax.broadcasted_iota(jnp.int32, (8, LANES), 1) % 8
    kind = lax.broadcasted_iota(jnp.int32, (8, LANES), 0)
    top_ok, bot_ok = row > 0, row < nrow - 1
    strip_ok = ((pos == 3) & (col > 0)) | ((pos == 2) & (col < ncol - 1))
    strip_ok &= ((line > 1) | top_ok) & ((line < ROWS + 2) | bot_ok)
    mask = ((kind == 0) & top_ok) | ((kind == 1) & bot_ok) | ((kind == 2) & strip_ok)
    mask = mask.astype(F32)
    conv, sums = pl.pallas_call(
        forward_kernel,
        grid=(STEPS,),
        in_specs=[halo, halo, edge, edge, edge, full(1, CH), chunk_cols, chunk_taps,
                  anywhere, anywhere],
        out_specs=[chunk_rows(CS * LANES), full(16, LANES)],
        out_shape=[shape(EX, CS * LANES), shape(16, LANES)],
        scratch_shapes=[
            pltpu.VMEM((CH, (XS - ROWS) * LANES), BF16),
            pltpu.VMEM((EB, (XS - ROWS) * LANES), F32),
            pltpu.VMEM((EB, 9 * LANES), F32),
            pltpu.VMEM((2, EB, LANES), F32),
            pltpu.VMEM((2, EB, ROWS * LANES), BF16),
            pltpu.VMEM((2, EB, ROWS * LANES), F32),
            pltpu.SemaphoreType.DMA((2, 2)),
        ],
        compiler_params=params(),
        cost_estimate=cost(200e6, 12e6),
        name="forward",
    )(top, bot, own, left, right, gain, w_expand, taps, hid, gg)

    sums = gathered(sums + partner(sums))
    core = (col % 2).astype(jnp.int32).reshape(1)
    out, gin, keep, send, vec = pl.pallas_call(
        backward_kernel,
        grid=(STEPS,),
        in_specs=[pl.BlockSpec(memory_space=pltpu.SMEM), full(PARTS // 2, 16, LANES),
                  full(SQ, EX), full(SQ, EX), tile, tile, halo, halo, edge, edge, full(1, CH),
                  full(8, LANES), full(CH, ROWS * LANES), full(ROWS, LANES),
                  anywhere, anywhere, anywhere, chunk_taps,
                  weight, weight],
        out_specs=[tile, tile, anywhere, anywhere, full(16, LANES)],
        out_shape=[shape(ROWS, CH, LANES, dtype=BF16), shape(ROWS, CH, LANES, dtype=BF16),
                   shape(PARTS // 2 * PACK, LANES), shape(PARTS // 2 * PACK, LANES),
                   shape(16, LANES)],
        scratch_shapes=[
            pltpu.VMEM((PARTS * PACK, LANES), F32),
            pltpu.VMEM((EX, LANES), F32),
            pltpu.VMEM((EX, LANES), F32),
            pltpu.VMEM((CH, 3 * LANES), BF16),
            pltpu.VMEM((CH, ROWS * LANES), BF16),
            pltpu.VMEM((EX, 3 * LANES), F32),
            pltpu.VMEM((EX, ROWS * LANES), BF16),
            pltpu.VMEM((EX, ROWS * LANES), BF16),
            pltpu.VMEM((EB, 9 * LANES), F32),
            pltpu.VMEM((EB, LANES), F32),
            pltpu.VMEM((56, LANES), F32),
            pltpu.VMEM((2, EB, ROWS * LANES), F32),
            pltpu.VMEM((2, EB, ROWS * LANES), F32),
            pltpu.VMEM((2, EB, CS * LANES), F32),
            pltpu.SemaphoreType.DMA((3, 2)),
            pltpu.SemaphoreType.DMA((2,)),
        ],
        compiler_params=params(),
        cost_estimate=cost(1500e6, 16e6),
        name="backward",
    )(core, sums, w_squeeze.T, w_excite, x, c, top, bot, left, right, gain, mask, scaled, inv, gg, pre, conv, taps,
      w_expand, wprojt)

    halves = to_half((keep + partner(send)).reshape(PARTS // 2, PACK, LANES))
    mine = exchanged(halves)
    total = jnp.sum(from_half(mine), axis=0)
    vecs = vec[None]
    sample = lax.axis_index("dp")
    for bit in (1, 2, 4):
        both = lax.ppermute(
            jnp.concatenate([total, vecs.reshape(16 * bit, LANES)], axis=0),
            "dp",
            [(i, i ^ bit) for i in range(8)],
        )
        total = total + both[:PACK]
        theirs = both[PACK:].reshape(bit, 16, LANES)
        ahead = (sample & bit) == 0
        vecs = jnp.concatenate(
            [jnp.where(ahead, vecs, theirs), jnp.where(ahead, theirs, vecs)], axis=0
        )
    vecs = vecs.reshape(8, 2048)
    grad_wexc = jnp.einsum("bs,be->se", vecs[:, 1536:1584], vecs[:, 768:1536], precision=HIGH)
    grad_wsq = jnp.einsum("be,bs->es", vecs[:, :768], vecs[:, 1664:1712], precision=HIGH)
    same = gathered(to_half(total[None])[0])
    other = partner(same)
    even = core[0] == 0
    every = jnp.stack(
        [jnp.where(even, same, other), jnp.where(even, other, same)], axis=1
    ).reshape(PARTS, PACK, LANES).astype(F32)
    big = (every[:, :72] * jnp.exp2(every[:, 74:75])).reshape(2, CH // 8, BLOCKS, 8, LANES)
    big = big.transpose(0, 1, 3, 2, 4).reshape(2, CH, EX)
    small = (every[:, 72:74] * jnp.exp2(every[:, 77:78])).reshape(8192)
    return (
        out.transpose(1, 0, 2)[None],
        gin.transpose(1, 0, 2)[None],
        small[6912:7104],
        big[0],
        small[:6912].reshape(9, 768).T,
        grad_wsq,
        grad_wexc,
        big[1].T,
    )


def solution(mesh):
    placed = (
        P("dp", None, "row", "col"),
        P(),
        P(),
        P(),
        P(),
        P(),
        P(),
        P("dp", None, "row", "col"),
    )
    return jax.shard_map(
        local,
        mesh=mesh,
        in_specs=placed,
        out_specs=(
            P("dp", None, "row", "col"),
            P("dp", None, "row", "col"),
            P(),
            P(),
            P(),
            P(),
            P(),
            P(),
        ),
        check_vma=False,
    )
```

```python
import jax
import jax.numpy as jnp
from jax import lax
from jax.experimental import pallas as pl
from jax.experimental.pallas import tpu as pltpu
from jax.sharding import PartitionSpec as P

EPS = 1e-06
HIGH = lax.Precision.HIGHEST
RC = ("row", "col")
F32, BF16 = jnp.float32, jnp.bfloat16
CH, EX, SQ = 192, 768, 48
ROWS, LANES = 8, 128
EB = 256
SUB = 16
STEPS = EX // EB
BLOCKS = EX // LANES
PARTS, PACK = 32, 80
VMEM_KIB = 60 * 1024
CHIPS = [[2 * q + core for q in range(PARTS // 2)] for core in range(2)]
XS = ROWS + 5
CS = ROWS + 3
NT = (((1,), (1,)), ((), ()))
TN = (((0,), (0,)), ((), ()))


def lane_iota(rows):
    return lax.broadcasted_iota(jnp.int32, (rows, LANES), 1)


def rounded(v):
    return v.astype(BF16).astype(F32)


def tn_dot(a, b):
    return lax.dot_general(a, b, TN, preferred_element_type=F32)


def lane_sum(v):
    return jnp.sum(v, axis=1, keepdims=True)


def silu_twice_slope(half):
    t = jnp.tanh(half)
    act = half * (1.0 + t)
    return act, (1.0 + t) + act * (1.0 - t)


def slab(s, n=1):
    return pl.ds(s * LANES, n * LANES)


def strip_lines(lines, total):
    lane = lane_iota(CH)
    for rr, x, c in lines:
        if x is not None:
            v = pltpu.roll(x.astype(F32), (8 * rr + 2) % LANES, 1)
            total = jnp.where((lane >= 8 * rr) & (lane < 8 * rr + 4), v, total)
        if c is not None:
            v = pltpu.roll(c.astype(F32), (8 * rr + 5) % LANES, 1)
            total = jnp.where((lane >= 8 * rr + 4) & (lane < 8 * rr + 6), v, total)
    return total


def strip_kernel(part_ref, top_ref, bot_ref, out_ref):
    last = ROWS + 2
    lines = [
        (0, top_ref[0], None),
        (1, top_ref[1], top_ref[2]),
        (last, bot_ref[0], bot_ref[2]),
        (last + 1, bot_ref[1], None),
    ]
    out_ref[...] = strip_lines(lines, part_ref[...].astype(F32)).astype(BF16)


def input_strip(own_ref, left_ref, right_ref):
    own, left, right = (r[...].astype(F32) for r in (own_ref, left_ref, right_ref))
    pos = lane_iota(CH) % 8
    value = jnp.where(pos == 0, pltpu.roll(own, LANES - 1, 1), 0.0)
    value = jnp.where(pos == 1, pltpu.roll(left, 1, 1), value)
    value = jnp.where(pos == 2, right, value)
    value = jnp.where(pos == 3, pltpu.roll(left, 2, 1), value)
    value = jnp.where(pos == 4, pltpu.roll(right, 1, 1), value)
    return jnp.where(pos == 5, pltpu.roll(own, 3, 1), value)


def cotangent_strip(left_ref, right_ref):
    left, right = (r[...].astype(F32) for r in (left_ref, right_ref))
    pos = lane_iota(CH) % 8
    value = jnp.where(pos == 3, pltpu.roll(left, LANES - 1, 1), 0.0)
    return jnp.where(pos == 2, pltpu.roll(right, LANES - 3, 1), value)


def neighbours(v, strip, rr, first, last):
    edge = pltpu.roll(strip, (LANES - 8 * rr - 3) % LANES, 1)
    left = jnp.where(first, edge, pltpu.roll(v, 1, 1))
    right = jnp.where(last, edge, pltpu.roll(v, LANES - 1, 1))
    return left, right


def spread_gain(gain_ref):
    return jnp.broadcast_to(gain_ref[...], (LANES, CH)).T


def spread_taps(taps_ref, out_s):
    for n in range(EB // LANES):
        rows = slice(n * LANES, (n + 1) * LANES)
        block = jnp.concatenate([taps_ref[:, rows], jnp.zeros((7, LANES), F32)], axis=0).T
        block = 0.5 * block
        for t in range(9):
            out_s[rows, slab(t)] = jnp.broadcast_to(block[:, t : t + 1], (LANES, LANES))


class Chunks:
    def __init__(self, pairs, sems):
        self.pairs, self.sems = pairs, sems

    def copies(self, step):
        rows = pl.ds(pl.multiple_of(step * EB, EB), EB)
        slot = step % 2
        return [
            pltpu.make_async_copy(src.at[rows, :], dst.at[slot], self.sems.at[n, slot])
            for n, (src, dst) in enumerate(self.pairs)
        ]

    def start(self, step):
        for copy in self.copies(step):
            copy.start()

    def advance(self, step):
        for copy in self.copies(step):
            copy.wait()

        @pl.when(step < STEPS - 1)
        def _():
            self.start(step + 1)


def expand_kernel(
    x_ref, c_ref, gain_ref, wexp_ref, wprojt_ref,
    scaled_out, inv_out, part_out, pre_out, hid_out, gg_out, cot_s,
):
    @pl.when(pl.program_id(0) == 0)
    def _():
        gain = spread_gain(gain_ref)
        for r in range(ROWS):
            x = x_ref[r].astype(F32)
            inverse = lax.rsqrt(jnp.sum(x * x, axis=0, keepdims=True) / CH + EPS)
            inv_out[r : r + 1, :] = inverse
            scaled_out[:, slab(r)] = (x * inverse * gain).astype(BF16)
            cot_s[:, slab(r)] = c_ref[r]
        lines = [(r + 2, x_ref[r], c_ref[r]) for r in range(ROWS)]
        part_out[...] = strip_lines(lines, jnp.zeros((CH, LANES), F32)).astype(BF16)

    pre_out[...] = tn_dot(wexp_ref[...] * 0.5, scaled_out[...])
    gg_out[...] = tn_dot(wprojt_ref[...], cot_s[...])

    def body(i, carry):
        ds = pl.ds(pl.multiple_of(i * SUB, SUB), SUB)
        v = pre_out[ds, :]
        hid_out[ds, :] = (v * (1.0 + jnp.tanh(v))).astype(BF16)
        return carry

    lax.fori_loop(0, EB // SUB, body, 0, unroll=4)


def forward_kernel(
    top_ref, bot_ref, own_ref, left_ref, right_ref, gain_ref, wexp_ref, taps_ref, hid_any, gg_any,
    conv_out, sums_out, scaled_s, pre_s, taps_s, acc_s, hid_s, gg_s, sems,
):
    step = pl.program_id(0)
    chunks = Chunks(((hid_any, hid_s), (gg_any, gg_s)), sems)
    hid_ref, gg_ref = hid_s.at[step % 2], gg_s.at[step % 2]

    @pl.when(step == 0)
    def _():
        chunks.start(0)
        gain = 0.5 * spread_gain(gain_ref)
        for s in range(XS - ROWS):
            if s < 2:
                x = top_ref[s].astype(F32)
            elif s < 4:
                x = bot_ref[s - 2].astype(F32)
            else:
                x = input_strip(own_ref, left_ref, right_ref)
            inverse = lax.rsqrt(jnp.sum(x * x, axis=0, keepdims=True) / CH + EPS)
            scaled_s[:, slab(s)] = (x * inverse * gain).astype(BF16)
        sums_out[...] = jnp.zeros_like(sums_out)

    pre_s[...] = tn_dot(wexp_ref[...], scaled_s[...])
    spread_taps(taps_ref, taps_s)
    chunks.advance(step)
    lane = lane_iota(SUB)
    first, last = lane == 0, lane == LANES - 1

    def body(i, carry):
        ds = pl.ds(pl.multiple_of(i * SUB, SUB), SUB)
        k = [taps_s[ds, slab(t)] for t in range(9)]

        def hidden(s):
            if 2 <= s < ROWS + 2:
                return hid_ref[ds, slab(s - 2)].astype(F32)
            v = pre_s[ds, slab(s if s < 2 else s - ROWS)]
            return rounded(v * (1.0 + jnp.tanh(v)))

        strip = hidden(XS - 1)
        acc = [None] * (ROWS + 4)
        for rr in range(ROWS + 4):
            h = hidden(rr)
            hl, hr = neighbours(h, strip, rr, first, last)
            for a in (-1, 0, 1):
                o = rr - a
                if 1 <= o <= ROWS + 2:
                    t = 3 * (a + 1)
                    term = k[t] * hl + k[t + 1] * h + k[t + 2] * hr
                    acc[o] = term if acc[o] is None else acc[o] + term
        pooled = jnp.zeros((SUB, LANES), F32)
        gexc = jnp.zeros((SUB, LANES), F32)
        for o in range(1, ROWS + 3):
            v = acc[o]
            conv_out[ds, slab(o - 1)] = v
            if 2 <= o <= ROWS + 1:
                act = v * (1.0 + jnp.tanh(v))
                pooled = pooled + act
                gexc = gexc + act * gg_ref[ds, slab(o - 2)]
        edge = None
        for a in (-1, 0, 1):
            for c in (-1, 0, 1):
                shift = (-(8 * a + 2 * c)) % LANES
                term = k[3 * (a + 1) + c + 1] * (pltpu.roll(strip, shift, 1) if shift else strip)
                edge = term if edge is None else edge + term
        conv_out[ds, slab(CS - 1)] = edge
        acc_s[0, ds, :] = pooled
        acc_s[1, ds, :] = gexc
        return carry

    lax.fori_loop(0, EB // SUB, body, 0, unroll=8)
    for n in range(EB // LANES):
        for kind in range(2):
            row = jnp.sum(acc_s[kind, n * LANES : (n + 1) * LANES, :].T, axis=0, keepdims=True)
            sums_out[pl.ds(2 * (step * (EB // LANES) + n) + kind, 1), :] = row


def squeeze_excite(parts_ref, wsq_ref, wexc_ref, exc_s, gp_s, vec_out):
    pixels = 32768.0
    total = jnp.sum(parts_ref[...], axis=0)
    pooled = jnp.concatenate([total[2 * j : 2 * j + 1] for j in range(BLOCKS)], axis=1) / pixels
    gexc = jnp.concatenate([total[2 * j + 1 : 2 * j + 2] for j in range(BLOCKS)], axis=1)
    pooled = jnp.broadcast_to(pooled, (8, EX))
    gexc = jnp.broadcast_to(gexc, (8, EX))
    wsq, wexc = wsq_ref[...], wexc_ref[...]
    spre = lax.dot_general(pooled, wsq, NT, precision=HIGH, preferred_element_type=F32)
    sig = jax.nn.sigmoid(spre)
    squeezed = spre * sig
    epre = jnp.dot(squeezed, wexc, precision=HIGH, preferred_element_type=F32)
    excite = jax.nn.sigmoid(epre)
    gepre = gexc * excite * (1.0 - excite)
    gspre = lax.dot_general(gepre, wexc, NT, precision=HIGH, preferred_element_type=F32)
    gspre = gspre * (sig * (1.0 + spre * (1.0 - sig)))
    gpool = jnp.dot(gspre, wsq, precision=HIGH, preferred_element_type=F32)
    gpool = gpool / pixels
    vec_out[...] = jnp.zeros((16, LANES), F32)
    for j in range(BLOCKS):
        cols = slice(j * LANES, (j + 1) * LANES)
        exc_s[cols, :] = jnp.broadcast_to(excite[:1, cols], (LANES, LANES)).T
        gp_s[cols, :] = jnp.broadcast_to(gpool[:1, cols], (LANES, LANES)).T
        vec_out[j : j + 1, :] = pooled[:1, cols]
        vec_out[BLOCKS + j : BLOCKS + j + 1, :] = gepre[:1, cols]
    vec_out[12:13, :SQ] = squeezed[:1]
    vec_out[13:14, :SQ] = gspre[:1]


def backward_kernel(
    core_ref, parts_ref, wsq_ref, wexc_ref, x_ref, c_ref, top_ref, bot_ref, left_ref, right_ref,
    gain_ref, mask_ref, scaled_ref, inv_ref, gg_any, pre_any, conv_any, taps_ref, wexp_ref, wprojt_ref,
    out_out, gin_out, keep_any, send_any, vec_out,
    packed_s, exc_s, gp_s, rim_s, cot_s, gg_s, gated_s, gpre_s, taps_s, acc_s, tsum_s,
    ggc_s, prec_s, convc_s, sems, out_sems,
):
    step = pl.program_id(0)
    chunks = Chunks(((gg_any, ggc_s), (pre_any, prec_s), (conv_any, convc_s)), sems)
    gg_ref, pre_ref, conv_ref = (r.at[step % 2] for r in (ggc_s, prec_s, convc_s))

    @pl.when(step == 0)
    def _():
        chunks.start(0)
        squeeze_excite(parts_ref, wsq_ref, wexc_ref, exc_s, gp_s, vec_out)
        for r in range(ROWS):
            cot_s[:, slab(r)] = c_ref[r]
        rim_s[:, slab(0)] = top_ref[2]
        rim_s[:, slab(1)] = bot_ref[2]
        rim_s[:, slab(2)] = cotangent_strip(left_ref, right_ref).astype(BF16)
        gg_s[...] = tn_dot(wprojt_ref[...], rim_s[...])

    spread_taps(taps_ref, taps_s)
    chunks.advance(step)
    base = step * EB
    lane = lane_iota(SUB)
    first, last = lane == 0, lane == LANES - 1

    def body(i, carry):
        ds = pl.ds(pl.multiple_of(i * SUB, SUB), SUB)
        whole = pl.ds(pl.multiple_of(base + i * SUB, SUB), SUB)
        k = [taps_s[ds, slab(t)] for t in range(9)]
        exc, gp = exc_s[whole, :], 0.5 * gp_s[whole, :]
        half = 0.5 * exc

        def grad_conv(s, mask):
            act, slope = silu_twice_slope(conv_ref[ds, slab(s)])
            if 1 <= s <= ROWS:
                gated_s[whole, slab(s - 1)] = (act * exc).astype(BF16)
            if 1 <= s <= ROWS:
                g = gg_ref[ds, slab(s - 1)]
            else:
                g = gg_s[whole, slab(0 if s == 0 else s - ROWS)]
            g = (g * half + gp) * slope
            if mask is not None:
                g = jnp.where(mask_ref[mask : mask + 1, :] > 0.5, g, 0.0)
            return rounded(g)

        def hidden(r):
            act, slope = silu_twice_slope(pre_ref[ds, slab(r)])
            return rounded(act), slope

        strip = grad_conv(CS - 1, 2)
        tap = [None] * 9
        state = {}
        gh = {}
        for s in range(ROWS + 2):
            g = grad_conv(s, 0 if s == 0 else 1 if s == ROWS + 1 else None)
            gl, gr = neighbours(g, strip, s + 1, first, last)
            for a in (-1, 0, 1):
                r = s + a - 1
                if 0 <= r < ROWS:
                    if r not in state:
                        state[r] = hidden(r)
                    h = state[r][0]
                    t = 3 * (a + 1)
                    term = k[t] * gr + k[t + 1] * g + k[t + 2] * gl
                    gh[r] = term if r not in gh else gh[r] + term
                    for c, v in enumerate((gr, g, gl)):
                        tap[t + c] = h * v if tap[t + c] is None else tap[t + c] + h * v
            r = s - 2
            if 0 <= r:
                gpre_s[whole, slab(r)] = (gh.pop(r) * state.pop(r)[1]).astype(BF16)
        total = jnp.zeros((SUB, LANES), F32)
        for t in range(9):
            total = jnp.where(lane == t, lane_sum(tap[t]), total)
        acc_s[ds, :] = total
        return carry

    lax.fori_loop(0, EB // SUB, body, 0, unroll=2)
    for n in range(EB // LANES):
        taps = acc_s[n * LANES : (n + 1) * LANES, :].T
        block = step * (EB // LANES) + n
        for t in range(9):
            tsum_s[pl.ds(BLOCKS * t + block, 1), :] = taps[t : t + 1]

    @pl.when(step == STEPS - 1)
    def _():
        gated, gpre = gated_s[...], gpre_s[...]
        for which, w in enumerate(
            (
                lax.dot_general(scaled_ref[...], gpre, NT, preferred_element_type=F32),
                lax.dot_general(cot_s[...], gated, NT, preferred_element_type=F32),
            )
        ):
            for i in range(CH // 8):
                for n in range(BLOCKS):
                    group = (which * (CH // 8) + i) * BLOCKS + n
                    part = group // 9
                    row = PACK * (part % 2 * PARTS // 2 + part // 2) + 8 * (group % 9)
                    packed_s[row : row + 8, :] = w[8 * i : 8 * i + 8, slab(n)]
        gs_all = jnp.dot(wexp_ref[...], gpre, preferred_element_type=F32)
        ggain = jnp.zeros((CH, LANES), F32)
        for r in range(ROWS):
            normed = x_ref[r].astype(F32) * inv_ref[r : r + 1, :]
            ggain = ggain + gs_all[:, r * LANES : (r + 1) * LANES] * normed
        sums = jnp.broadcast_to(lane_sum(ggain), (CH, LANES)).T[:1]
        tsum_s[54:55, :] = sums[:, :LANES]
        tsum_s[55:56, :] = jnp.zeros((1, LANES), F32)
        tsum_s[55:56, : CH - LANES] = sums[:, LANES:]
        spare = lax.broadcasted_iota(jnp.int32, (8, LANES), 0)
        for d in range(PARTS):
            base = (d % 2 * PARTS // 2 + d // 2) * PACK
            packed_s[base + 72 : base + PACK, :] = jnp.zeros((8, LANES), F32)
            if d < 28:
                packed_s[base + 72 : base + 74, :] = tsum_s[2 * d : 2 * d + 2, :]
            tail = packed_s[base + 72 : base + PACK, :]
            big = jnp.max(jnp.abs(packed_s[base : base + 72, :]), axis=0, keepdims=True)
            tail = jnp.where(spare == 2, big, tail)
            small = jnp.max(jnp.where(spare < 2, jnp.abs(tail), 0.0), axis=0, keepdims=True)
            packed_s[base + 72 : base + PACK, :] = jnp.where(spare == 3, small, tail)
        core, half = core_ref[0], PARTS // 2 * PACK
        sends = [
            pltpu.make_async_copy(
                packed_s.at[pl.ds(pl.multiple_of(half * which, 8), half), :], dst, out_sems.at[n]
            )
            for n, (which, dst) in enumerate(((core, keep_any), (1 - core, send_any)))
        ]
        for copy in sends:
            copy.start()
        proj = jnp.dot(wprojt_ref[...], gated, preferred_element_type=F32)
        gain = spread_gain(gain_ref)
        for r in range(ROWS):
            x = x_ref[r].astype(F32)
            out_out[r] = (x + proj[:, r * LANES : (r + 1) * LANES]).astype(BF16)
            inverse = inv_ref[r : r + 1, :]
            normed = x * inverse
            gnormed = gs_all[:, r * LANES : (r + 1) * LANES] * gain
            mean = jnp.sum(gnormed * normed, axis=0, keepdims=True) / CH
            gin_out[r] = (inverse * (gnormed - normed * mean) + c_ref[r].astype(F32)).astype(BF16)
        for copy in sends:
            copy.wait()


def to_half(v, big, small):
    row = lax.broadcasted_iota(jnp.int32, (1, PACK, 1), 1)
    e_big, e_small = (
        jnp.ceil(jnp.log2(jnp.maximum(jnp.max(m, axis=(1, 2), keepdims=True), 1e-30)))
        for m in (big, small)
    )
    scaled = v * jnp.where(row < 72, jnp.exp2(-e_big), jnp.exp2(-e_small))
    return jnp.where(row < 74, scaled, jnp.where(row < 77, e_big, e_small)).astype(jnp.float16)


def from_half(h):
    v = h.astype(F32)
    row = lax.broadcasted_iota(jnp.int32, (1, PACK, 1), 1)
    scale = jnp.where(row < 72, jnp.exp2(v[:, 74:75]), jnp.exp2(v[:, 77:78]))
    return jnp.where(row < 74, v * scale, 0.0)


def shape(*dims, dtype=F32):
    return jax.ShapeDtypeStruct(dims, dtype)


def full(*dims):
    return pl.BlockSpec(dims, lambda j: (0,) * len(dims))


def params(grid=True, kib=VMEM_KIB):
    return pltpu.CompilerParams(
        dimension_semantics=("arbitrary",) if grid else None, vmem_limit_bytes=kib * 1024
    )


def cost(flops, moved):
    return pl.CostEstimate(flops=int(flops), bytes_accessed=int(moved), transcendentals=0)


def exchanged(blocks):
    return lax.all_to_all(blocks, RC, 0, 0, tiled=True, axis_index_groups=CHIPS)


def gathered(block):
    return exchanged(jnp.broadcast_to(block[None], (PARTS // 2,) + block.shape))


def partner(block):
    return lax.ppermute(block, "col", [(i, i ^ 1) for i in range(4)])


def local(inputs, norm_gain, w_expand, kernel, w_squeeze, w_excite, w_project, cotangent):
    nrow, ncol = lax.axis_size("row"), lax.axis_size("col")
    row, col = lax.axis_index("row"), lax.axis_index("col")
    x = inputs[0].transpose(1, 0, 2)
    c = cotangent[0].transpose(1, 0, 2)
    fwd_row = [(i, i + 1) for i in range(nrow - 1)]
    bwd_row = [(i + 1, i) for i in range(nrow - 1)]
    fwd_col = [(i, i + 1) for i in range(ncol - 1)]
    bwd_col = [(i + 1, i) for i in range(ncol - 1)]
    top = lax.ppermute(jnp.concatenate([x[6:8], c[7:8]], axis=0), "row", fwd_row)
    bot = lax.ppermute(jnp.concatenate([x[0:2], c[0:1]], axis=0), "row", bwd_row)
    gain = norm_gain[None, :]
    wprojt, taps = w_project.T, kernel.T
    halo = full(3, CH, LANES)
    tile = full(ROWS, CH, LANES)
    edge = full(CH, LANES)
    weight = full(CH, EX)
    anywhere = pl.BlockSpec(memory_space=pl.ANY)
    chunk_rows = lambda width: pl.BlockSpec((EB, width), lambda j: (j, 0))
    chunk_cols = pl.BlockSpec((CH, EB), lambda j: (0, j))
    chunk_taps = pl.BlockSpec((9, EB), lambda j: (0, j))
    scaled, inv, part, pre, hid, gg = pl.pallas_call(
        expand_kernel,
        grid=(STEPS,),
        in_specs=[tile, tile, full(1, CH), chunk_cols, chunk_cols],
        out_specs=[full(CH, ROWS * LANES), full(ROWS, LANES), edge, chunk_rows(ROWS * LANES),
                   chunk_rows(ROWS * LANES), chunk_rows(ROWS * LANES)],
        out_shape=[shape(CH, ROWS * LANES, dtype=BF16), shape(ROWS, LANES),
                   shape(CH, LANES, dtype=BF16),
                   shape(EX, ROWS * LANES), shape(EX, ROWS * LANES, dtype=BF16),
                   shape(EX, ROWS * LANES)],
        scratch_shapes=[pltpu.VMEM((CH, ROWS * LANES), BF16)],
        compiler_params=params(),
        cost_estimate=cost(600e6, 10e6),
        name="expand",
    )(x, c, gain, w_expand, wprojt)
    own = pl.pallas_call(
        strip_kernel,
        out_shape=shape(CH, LANES, dtype=BF16),
        compiler_params=params(False, 4096),
        cost_estimate=cost(1e6, 1e6),
        name="strip",
    )(part, top, bot)
    left = lax.ppermute(own, "col", fwd_col)
    right = lax.ppermute(own, "col", bwd_col)

    line = lax.broadcasted_iota(jnp.int32, (8, LANES), 1) // 8
    pos = lax.broadcasted_iota(jnp.int32, (8, LANES), 1) % 8
    kind = lax.broadcasted_iota(jnp.int32, (8, LANES), 0)
    top_ok, bot_ok = row > 0, row < nrow - 1
    strip_ok = ((pos == 3) & (col > 0)) | ((pos == 2) & (col < ncol - 1))
    strip_ok &= ((line > 1) | top_ok) & ((line < ROWS + 2) | bot_ok)
    mask = ((kind == 0) & top_ok) | ((kind == 1) & bot_ok) | ((kind == 2) & strip_ok)
    mask = mask.astype(F32)
    conv, sums = pl.pallas_call(
        forward_kernel,
        grid=(STEPS,),
        in_specs=[halo, halo, edge, edge, edge, full(1, CH), chunk_cols, chunk_taps,
                  anywhere, anywhere],
        out_specs=[chunk_rows(CS * LANES), full(16, LANES)],
        out_shape=[shape(EX, CS * LANES), shape(16, LANES)],
        scratch_shapes=[
            pltpu.VMEM((CH, (XS - ROWS) * LANES), BF16),
            pltpu.VMEM((EB, (XS - ROWS) * LANES), F32),
            pltpu.VMEM((EB, 9 * LANES), F32),
            pltpu.VMEM((2, EB, LANES), F32),
            pltpu.VMEM((2, EB, ROWS * LANES), BF16),
            pltpu.VMEM((2, EB, ROWS * LANES), F32),
            pltpu.SemaphoreType.DMA((2, 2)),
        ],
        compiler_params=params(),
        cost_estimate=cost(200e6, 12e6),
        name="forward",
    )(top, bot, own, left, right, gain, w_expand, taps, hid, gg)

    sums = gathered(sums + partner(sums))
    core = (col % 2).astype(jnp.int32).reshape(1)
    out, gin, keep, send, vec = pl.pallas_call(
        backward_kernel,
        grid=(STEPS,),
        in_specs=[pl.BlockSpec(memory_space=pltpu.SMEM), full(PARTS // 2, 16, LANES),
                  full(SQ, EX), full(SQ, EX), tile, tile, halo, halo, edge, edge, full(1, CH),
                  full(8, LANES), full(CH, ROWS * LANES), full(ROWS, LANES),
                  anywhere, anywhere, anywhere, chunk_taps,
                  weight, weight],
        out_specs=[tile, tile, anywhere, anywhere, full(16, LANES)],
        out_shape=[shape(ROWS, CH, LANES, dtype=BF16), shape(ROWS, CH, LANES, dtype=BF16),
                   shape(PARTS // 2 * PACK, LANES), shape(PARTS // 2 * PACK, LANES),
                   shape(16, LANES)],
        scratch_shapes=[
            pltpu.VMEM((PARTS * PACK, LANES), F32),
            pltpu.VMEM((EX, LANES), F32),
            pltpu.VMEM((EX, LANES), F32),
            pltpu.VMEM((CH, 3 * LANES), BF16),
            pltpu.VMEM((CH, ROWS * LANES), BF16),
            pltpu.VMEM((EX, 3 * LANES), F32),
            pltpu.VMEM((EX, ROWS * LANES), BF16),
            pltpu.VMEM((EX, ROWS * LANES), BF16),
            pltpu.VMEM((EB, 9 * LANES), F32),
            pltpu.VMEM((EB, LANES), F32),
            pltpu.VMEM((56, LANES), F32),
            pltpu.VMEM((2, EB, ROWS * LANES), F32),
            pltpu.VMEM((2, EB, ROWS * LANES), F32),
            pltpu.VMEM((2, EB, CS * LANES), F32),
            pltpu.SemaphoreType.DMA((3, 2)),
            pltpu.SemaphoreType.DMA((2,)),
        ],
        compiler_params=params(),
        cost_estimate=cost(1500e6, 16e6),
        name="backward",
    )(core, sums, w_squeeze.T, w_excite, x, c, top, bot, left, right, gain, mask, scaled, inv, gg, pre, conv, taps,
      w_expand, wprojt)

    pair = (keep + partner(send)).reshape(PARTS // 2, PACK, LANES)
    halves = to_half(pair, pair[:, 74:75], pair[:, 75:76])
    mine = exchanged(halves)
    total = jnp.sum(from_half(mine), axis=0)
    vecs = vec[None]
    sample = lax.axis_index("dp")
    members = 1
    for bit in (4, 2, 1):
        both = lax.ppermute(
            jnp.concatenate([total, vecs.reshape(16 * members, LANES)], axis=0),
            "dp",
            [(i, i ^ bit) for i in range(8)],
        )
        total = total + both[:PACK]
        theirs = both[PACK:].reshape(members, 16, LANES)
        ahead = (sample & bit) == 0
        vecs = jnp.concatenate(
            [jnp.where(ahead, vecs, theirs), jnp.where(ahead, theirs, vecs)], axis=0
        )
        members *= 2
    vecs = vecs.reshape(8, 2048)
    grad_wexc = jnp.einsum("bs,be->se", vecs[:, 1536:1584], vecs[:, 768:1536], precision=HIGH)
    grad_wsq = jnp.einsum("be,bs->es", vecs[:, :768], vecs[:, 1664:1712], precision=HIGH)
    same = gathered(to_half(total[None], jnp.abs(total[None, :72]), jnp.abs(total[None, 72:74]))[0])
    other = partner(same)
    even = core[0] == 0
    every = jnp.stack(
        [jnp.where(even, same, other), jnp.where(even, other, same)], axis=1
    ).reshape(PARTS, PACK, LANES).astype(F32)
    big = (every[:, :72] * jnp.exp2(every[:, 74:75])).reshape(2, CH // 8, BLOCKS, 8, LANES)
    big = big.transpose(0, 1, 3, 2, 4).reshape(2, CH, EX)
    small = (every[:, 72:74] * jnp.exp2(every[:, 77:78])).reshape(8192)
    return (
        out.transpose(1, 0, 2)[None],
        gin.transpose(1, 0, 2)[None],
        small[6912:7104],
        big[0],
        small[:6912].reshape(9, 768).T,
        grad_wsq,
        grad_wexc,
        big[1].T,
    )


def solution(mesh):
    placed = (
        P("dp", None, "row", "col"),
        P(),
        P(),
        P(),
        P(),
        P(),
        P(),
        P("dp", None, "row", "col"),
    )
    return jax.shard_map(
        local,
        mesh=mesh,
        in_specs=placed,
        out_specs=(
            P("dp", None, "row", "col"),
            P("dp", None, "row", "col"),
            P(),
            P(),
            P(),
            P(),
            P(),
            P(),
        ),
        check_vma=False,
    )
```

```python
import jax
import jax.numpy as jnp
from jax import lax
from jax.experimental import pallas as pl
from jax.experimental.pallas import tpu as pltpu
from jax.sharding import PartitionSpec as P

EPS = 1e-06
HIGH = lax.Precision.HIGHEST
RC = ("row", "col")
F32, BF16 = jnp.float32, jnp.bfloat16
CH, EX, SQ = 192, 768, 48
ROWS, LANES = 8, 128
EB = 256
SUB = 16
STEPS = EX // EB
BLOCKS = EX // LANES
PARTS, PACK = 32, 80
VMEM_KIB = 60 * 1024
CHIPS = [[2 * q + core for q in range(PARTS // 2)] for core in range(2)]
XS = ROWS + 5
CS = ROWS + 3
NT = (((1,), (1,)), ((), ()))
TN = (((0,), (0,)), ((), ()))


def lane_iota(rows):
    return lax.broadcasted_iota(jnp.int32, (rows, LANES), 1)


def rounded(v):
    return v.astype(BF16).astype(F32)


def tn_dot(a, b):
    return lax.dot_general(a, b, TN, preferred_element_type=F32)


def lane_sum(v):
    return jnp.sum(v, axis=1, keepdims=True)


def silu_twice_slope(half):
    t = jnp.tanh(half)
    act = half * (1.0 + t)
    return act, (1.0 + t) + act * (1.0 - t)


def slab(s, n=1):
    return pl.ds(s * LANES, n * LANES)


def strip_lines(lines, total):
    lane = lane_iota(CH)
    for rr, x, c in lines:
        if x is not None:
            v = pltpu.roll(x.astype(F32), (8 * rr + 2) % LANES, 1)
            total = jnp.where((lane >= 8 * rr) & (lane < 8 * rr + 4), v, total)
        if c is not None:
            v = pltpu.roll(c.astype(F32), (8 * rr + 5) % LANES, 1)
            total = jnp.where((lane >= 8 * rr + 4) & (lane < 8 * rr + 6), v, total)
    return total


def strip_kernel(part_ref, top_ref, bot_ref, out_ref):
    last = ROWS + 2
    lines = [
        (0, top_ref[0], None),
        (1, top_ref[1], top_ref[2]),
        (last, bot_ref[0], bot_ref[2]),
        (last + 1, bot_ref[1], None),
    ]
    out_ref[...] = strip_lines(lines, part_ref[...].astype(F32)).astype(BF16)


def input_strip(own_ref, left_ref, right_ref):
    own, left, right = (r[...].astype(F32) for r in (own_ref, left_ref, right_ref))
    pos = lane_iota(CH) % 8
    value = jnp.where(pos == 0, pltpu.roll(own, LANES - 1, 1), 0.0)
    value = jnp.where(pos == 1, pltpu.roll(left, 1, 1), value)
    value = jnp.where(pos == 2, right, value)
    value = jnp.where(pos == 3, pltpu.roll(left, 2, 1), value)
    value = jnp.where(pos == 4, pltpu.roll(right, 1, 1), value)
    return jnp.where(pos == 5, pltpu.roll(own, 3, 1), value)


def cotangent_strip(left_ref, right_ref):
    left, right = (r[...].astype(F32) for r in (left_ref, right_ref))
    pos = lane_iota(CH) % 8
    value = jnp.where(pos == 3, pltpu.roll(left, LANES - 1, 1), 0.0)
    return jnp.where(pos == 2, pltpu.roll(right, LANES - 3, 1), value)


def neighbours(v, strip, rr, first, last):
    edge = pltpu.roll(strip, (LANES - 8 * rr - 3) % LANES, 1)
    left = jnp.where(first, edge, pltpu.roll(v, 1, 1))
    right = jnp.where(last, edge, pltpu.roll(v, LANES - 1, 1))
    return left, right


def spread_gain(gain_ref):
    return jnp.broadcast_to(gain_ref[...], (LANES, CH)).T


def spread_taps(taps_ref, out_s):
    for n in range(EB // LANES):
        rows = slice(n * LANES, (n + 1) * LANES)
        block = jnp.concatenate([taps_ref[:, rows], jnp.zeros((7, LANES), F32)], axis=0).T
        block = 0.5 * block
        for t in range(9):
            out_s[rows, slab(t)] = jnp.broadcast_to(block[:, t : t + 1], (LANES, LANES))


class Chunks:
    def __init__(self, pairs, sems):
        self.pairs, self.sems = pairs, sems

    def copies(self, step):
        rows = pl.ds(pl.multiple_of(step * EB, EB), EB)
        slot = step % 2
        return [
            pltpu.make_async_copy(src.at[rows, :], dst.at[slot], self.sems.at[n, slot])
            for n, (src, dst) in enumerate(self.pairs)
        ]

    def start(self, step):
        for copy in self.copies(step):
            copy.start()

    def advance(self, step):
        for copy in self.copies(step):
            copy.wait()

        @pl.when(step < STEPS - 1)
        def _():
            self.start(step + 1)


def expand_kernel(
    x_ref, c_ref, gain_ref, wexp_ref, wprojt_ref,
    scaled_out, inv_out, part_out, pre_out, hid_out, gg_out, cot_s,
):
    @pl.when(pl.program_id(0) == 0)
    def _():
        gain = spread_gain(gain_ref)
        for r in range(ROWS):
            x = x_ref[r].astype(F32)
            inverse = lax.rsqrt(jnp.sum(x * x, axis=0, keepdims=True) / CH + EPS)
            inv_out[r : r + 1, :] = inverse
            scaled_out[:, slab(r)] = (x * inverse * gain).astype(BF16)
            cot_s[:, slab(r)] = c_ref[r]
        lines = [(r + 2, x_ref[r], c_ref[r]) for r in range(ROWS)]
        part_out[...] = strip_lines(lines, jnp.zeros((CH, LANES), F32)).astype(BF16)

    pre_out[...] = tn_dot(wexp_ref[...] * 0.5, scaled_out[...])
    gg_out[...] = tn_dot(wprojt_ref[...], cot_s[...])

    def body(i, carry):
        ds = pl.ds(pl.multiple_of(i * SUB, SUB), SUB)
        v = pre_out[ds, :]
        hid_out[ds, :] = (v * (1.0 + jnp.tanh(v))).astype(BF16)
        return carry

    lax.fori_loop(0, EB // SUB, body, 0, unroll=4)


def forward_kernel(
    top_ref, bot_ref, own_ref, left_ref, right_ref, gain_ref, wexp_ref, taps_ref, hid_any, gg_any,
    conv_out, sums_out, scaled_s, pre_s, taps_s, acc_s, hid_s, gg_s, sems,
):
    step = pl.program_id(0)
    chunks = Chunks(((hid_any, hid_s), (gg_any, gg_s)), sems)
    hid_ref, gg_ref = hid_s.at[step % 2], gg_s.at[step % 2]

    @pl.when(step == 0)
    def _():
        chunks.start(0)
        gain = 0.5 * spread_gain(gain_ref)
        for s in range(XS - ROWS):
            if s < 2:
                x = top_ref[s].astype(F32)
            elif s < 4:
                x = bot_ref[s - 2].astype(F32)
            else:
                x = input_strip(own_ref, left_ref, right_ref)
            inverse = lax.rsqrt(jnp.sum(x * x, axis=0, keepdims=True) / CH + EPS)
            scaled_s[:, slab(s)] = (x * inverse * gain).astype(BF16)
        sums_out[...] = jnp.zeros_like(sums_out)

    pre_s[...] = tn_dot(wexp_ref[...], scaled_s[...])
    spread_taps(taps_ref, taps_s)
    chunks.advance(step)
    lane = lane_iota(SUB)
    first, last = lane == 0, lane == LANES - 1

    def body(i, carry):
        ds = pl.ds(pl.multiple_of(i * SUB, SUB), SUB)
        k = [taps_s[ds, slab(t)] for t in range(9)]

        def hidden(s):
            if 2 <= s < ROWS + 2:
                return hid_ref[ds, slab(s - 2)].astype(F32)
            v = pre_s[ds, slab(s if s < 2 else s - ROWS)]
            return rounded(v * (1.0 + jnp.tanh(v)))

        strip = hidden(XS - 1)
        acc = [None] * (ROWS + 4)
        for rr in range(ROWS + 4):
            h = hidden(rr)
            hl, hr = neighbours(h, strip, rr, first, last)
            for a in (-1, 0, 1):
                o = rr - a
                if 1 <= o <= ROWS + 2:
                    t = 3 * (a + 1)
                    term = k[t] * hl + k[t + 1] * h + k[t + 2] * hr
                    acc[o] = term if acc[o] is None else acc[o] + term
        pooled = jnp.zeros((SUB, LANES), F32)
        gexc = jnp.zeros((SUB, LANES), F32)
        for o in range(1, ROWS + 3):
            v = acc[o]
            conv_out[ds, slab(o - 1)] = v
            if 2 <= o <= ROWS + 1:
                act = v * (1.0 + jnp.tanh(v))
                pooled = pooled + act
                gexc = gexc + act * gg_ref[ds, slab(o - 2)]
        edge = None
        for a in (-1, 0, 1):
            for c in (-1, 0, 1):
                shift = (-(8 * a + 2 * c)) % LANES
                term = k[3 * (a + 1) + c + 1] * (pltpu.roll(strip, shift, 1) if shift else strip)
                edge = term if edge is None else edge + term
        conv_out[ds, slab(CS - 1)] = edge
        acc_s[0, ds, :] = pooled
        acc_s[1, ds, :] = gexc
        return carry

    lax.fori_loop(0, EB // SUB, body, 0, unroll=8)
    for n in range(EB // LANES):
        for kind in range(2):
            row = jnp.sum(acc_s[kind, n * LANES : (n + 1) * LANES, :].T, axis=0, keepdims=True)
            sums_out[pl.ds(2 * (step * (EB // LANES) + n) + kind, 1), :] = row


def squeeze_excite(parts_ref, wsq_ref, wexc_ref, exc_s, gp_s, vec_out):
    pixels = 32768.0
    total = jnp.sum(parts_ref[...], axis=0)
    pooled = jnp.concatenate([total[2 * j : 2 * j + 1] for j in range(BLOCKS)], axis=1) / pixels
    gexc = jnp.concatenate([total[2 * j + 1 : 2 * j + 2] for j in range(BLOCKS)], axis=1)
    pooled = jnp.broadcast_to(pooled, (8, EX))
    gexc = jnp.broadcast_to(gexc, (8, EX))
    wsq, wexc = wsq_ref[...], wexc_ref[...]
    spre = lax.dot_general(pooled, wsq, NT, precision=HIGH, preferred_element_type=F32)
    sig = jax.nn.sigmoid(spre)
    squeezed = spre * sig
    epre = jnp.dot(squeezed, wexc, precision=HIGH, preferred_element_type=F32)
    excite = jax.nn.sigmoid(epre)
    gepre = gexc * excite * (1.0 - excite)
    gspre = lax.dot_general(gepre, wexc, NT, precision=HIGH, preferred_element_type=F32)
    gspre = gspre * (sig * (1.0 + spre * (1.0 - sig)))
    gpool = jnp.dot(gspre, wsq, precision=HIGH, preferred_element_type=F32)
    gpool = gpool / pixels
    vec_out[...] = jnp.zeros((16, LANES), F32)
    for j in range(BLOCKS):
        cols = slice(j * LANES, (j + 1) * LANES)
        exc_s[cols, :] = jnp.broadcast_to(excite[:1, cols], (LANES, LANES)).T
        gp_s[cols, :] = jnp.broadcast_to(gpool[:1, cols], (LANES, LANES)).T
        vec_out[j : j + 1, :] = pooled[:1, cols]
        vec_out[BLOCKS + j : BLOCKS + j + 1, :] = gepre[:1, cols]
    vec_out[12:13, :SQ] = squeezed[:1]
    vec_out[13:14, :SQ] = gspre[:1]


def backward_kernel(
    core_ref, parts_ref, wsq_ref, wexc_ref, x_ref, c_ref, top_ref, bot_ref, left_ref, right_ref,
    gain_ref, mask_ref, scaled_ref, inv_ref, gg_any, pre_any, conv_any, taps_ref, wexp_ref, wprojt_ref,
    out_out, gin_out, keep_any, send_any, vec_out,
    packed_s, exc_s, gp_s, rim_s, cot_s, gg_s, gated_s, gpre_s, taps_s, acc_s, tsum_s,
    ggc_s, prec_s, convc_s, sems, out_sems,
):
    step = pl.program_id(0)
    chunks = Chunks(((gg_any, ggc_s), (pre_any, prec_s), (conv_any, convc_s)), sems)
    gg_ref, pre_ref, conv_ref = (r.at[step % 2] for r in (ggc_s, prec_s, convc_s))

    @pl.when(step == 0)
    def _():
        chunks.start(0)
        squeeze_excite(parts_ref, wsq_ref, wexc_ref, exc_s, gp_s, vec_out)
        for r in range(ROWS):
            cot_s[:, slab(r)] = c_ref[r]
        rim_s[:, slab(0)] = top_ref[2]
        rim_s[:, slab(1)] = bot_ref[2]
        rim_s[:, slab(2)] = cotangent_strip(left_ref, right_ref).astype(BF16)
        gg_s[...] = tn_dot(wprojt_ref[...], rim_s[...])

    spread_taps(taps_ref, taps_s)
    chunks.advance(step)
    base = step * EB
    lane = lane_iota(SUB)
    first, last = lane == 0, lane == LANES - 1

    def body(i, carry):
        ds = pl.ds(pl.multiple_of(i * SUB, SUB), SUB)
        whole = pl.ds(pl.multiple_of(base + i * SUB, SUB), SUB)
        k = [taps_s[ds, slab(t)] for t in range(9)]
        exc, gp = exc_s[whole, :], 0.5 * gp_s[whole, :]
        half = 0.5 * exc

        def grad_conv(s, mask):
            act, slope = silu_twice_slope(conv_ref[ds, slab(s)])
            if 1 <= s <= ROWS:
                gated_s[whole, slab(s - 1)] = (act * exc).astype(BF16)
            if 1 <= s <= ROWS:
                g = gg_ref[ds, slab(s - 1)]
            else:
                g = gg_s[whole, slab(0 if s == 0 else s - ROWS)]
            g = (g * half + gp) * slope
            if mask is not None:
                g = jnp.where(mask_ref[mask : mask + 1, :] > 0.5, g, 0.0)
            return rounded(g)

        def hidden(r):
            act, slope = silu_twice_slope(pre_ref[ds, slab(r)])
            return rounded(act), slope

        strip = grad_conv(CS - 1, 2)
        tap = [None] * 9
        state = {}
        gh = {}
        for s in range(ROWS + 2):
            g = grad_conv(s, 0 if s == 0 else 1 if s == ROWS + 1 else None)
            gl, gr = neighbours(g, strip, s + 1, first, last)
            for a in (-1, 0, 1):
                r = s + a - 1
                if 0 <= r < ROWS:
                    if r not in state:
                        state[r] = hidden(r)
                    h = state[r][0]
                    t = 3 * (a + 1)
                    term = k[t] * gr + k[t + 1] * g + k[t + 2] * gl
                    gh[r] = term if r not in gh else gh[r] + term
                    for c, v in enumerate((gr, g, gl)):
                        tap[t + c] = h * v if tap[t + c] is None else tap[t + c] + h * v
            r = s - 2
            if 0 <= r:
                gpre_s[whole, slab(r)] = (gh.pop(r) * state.pop(r)[1]).astype(BF16)
        total = jnp.zeros((SUB, LANES), F32)
        for t in range(9):
            total = jnp.where(lane == t, lane_sum(tap[t]), total)
        acc_s[ds, :] = total
        return carry

    lax.fori_loop(0, EB // SUB, body, 0, unroll=2)
    for n in range(EB // LANES):
        taps = acc_s[n * LANES : (n + 1) * LANES, :].T
        block = step * (EB // LANES) + n
        for t in range(9):
            tsum_s[pl.ds(BLOCKS * t + block, 1), :] = taps[t : t + 1]

    @pl.when(step == STEPS - 1)
    def _():
        gated, gpre = gated_s[...], gpre_s[...]
        for which, w in enumerate(
            (
                lax.dot_general(scaled_ref[...], gpre, NT, preferred_element_type=F32),
                lax.dot_general(cot_s[...], gated, NT, preferred_element_type=F32),
            )
        ):
            for i in range(CH // 8):
                for n in range(BLOCKS):
                    group = (which * (CH // 8) + i) * BLOCKS + n
                    part = group // 9
                    row = PACK * (part % 2 * PARTS // 2 + part // 2) + 8 * (group % 9)
                    packed_s[row : row + 8, :] = w[8 * i : 8 * i + 8, slab(n)]
        gs_all = jnp.dot(wexp_ref[...], gpre, preferred_element_type=F32)
        ggain = jnp.zeros((CH, LANES), F32)
        for r in range(ROWS):
            normed = x_ref[r].astype(F32) * inv_ref[r : r + 1, :]
            ggain = ggain + gs_all[:, r * LANES : (r + 1) * LANES] * normed
        sums = jnp.broadcast_to(lane_sum(ggain), (CH, LANES)).T[:1]
        tsum_s[54:55, :] = sums[:, :LANES]
        tsum_s[55:56, :] = jnp.zeros((1, LANES), F32)
        tsum_s[55:56, : CH - LANES] = sums[:, LANES:]
        spare = lax.broadcasted_iota(jnp.int32, (8, LANES), 0)
        for d in range(PARTS):
            base = (d % 2 * PARTS // 2 + d // 2) * PACK
            packed_s[base + 72 : base + PACK, :] = jnp.zeros((8, LANES), F32)
            if d < 28:
                packed_s[base + 72 : base + 74, :] = tsum_s[2 * d : 2 * d + 2, :]
            tail = packed_s[base + 72 : base + PACK, :]
            big = jnp.max(jnp.abs(packed_s[base : base + 72, :]), axis=0, keepdims=True)
            tail = jnp.where(spare == 2, big, tail)
            small = jnp.max(jnp.where(spare < 2, jnp.abs(tail), 0.0), axis=0, keepdims=True)
            packed_s[base + 72 : base + PACK, :] = jnp.where(spare == 3, small, tail)
        core, half = core_ref[0], PARTS // 2 * PACK
        sends = [
            pltpu.make_async_copy(
                packed_s.at[pl.ds(pl.multiple_of(half * which, 8), half), :], dst, out_sems.at[n]
            )
            for n, (which, dst) in enumerate(((core, keep_any), (1 - core, send_any)))
        ]
        for copy in sends:
            copy.start()
        proj = jnp.dot(wprojt_ref[...], gated, preferred_element_type=F32)
        gain = spread_gain(gain_ref)
        for r in range(ROWS):
            x = x_ref[r].astype(F32)
            out_out[r] = (x + proj[:, r * LANES : (r + 1) * LANES]).astype(BF16)
            inverse = inv_ref[r : r + 1, :]
            normed = x * inverse
            gnormed = gs_all[:, r * LANES : (r + 1) * LANES] * gain
            mean = jnp.sum(gnormed * normed, axis=0, keepdims=True) / CH
            gin_out[r] = (inverse * (gnormed - normed * mean) + c_ref[r].astype(F32)).astype(BF16)
        for copy in sends:
            copy.wait()


TOP = 15.0


def to_half(v, big, small):
    row = lax.broadcasted_iota(jnp.int32, (1, PACK, 1), 1)
    e_big, e_small = (
        jnp.ceil(jnp.log2(jnp.maximum(jnp.max(m, axis=(1, 2), keepdims=True), 1e-30))) - TOP
        for m in (big, small)
    )
    scaled = v * jnp.where(row < 72, jnp.exp2(-e_big), jnp.exp2(-e_small))
    return jnp.where(row < 74, scaled, jnp.where(row < 77, e_big, e_small)).astype(jnp.float16)


def from_half(h):
    v = h.astype(F32)
    row = lax.broadcasted_iota(jnp.int32, (1, PACK, 1), 1)
    s_big, s_small = jnp.exp2(v[:, 74:75]), jnp.exp2(v[:, 77:78])
    bounds = jnp.where(row == 74, s_big, jnp.where(row == 75, s_small, 0.0)) * 2.0**TOP
    return jnp.where(row < 74, v * jnp.where(row < 72, s_big, s_small), bounds)


def shape(*dims, dtype=F32):
    return jax.ShapeDtypeStruct(dims, dtype)


def full(*dims):
    return pl.BlockSpec(dims, lambda j: (0,) * len(dims))


def params(grid=True, kib=VMEM_KIB):
    return pltpu.CompilerParams(
        dimension_semantics=("arbitrary",) if grid else None, vmem_limit_bytes=kib * 1024
    )


def cost(flops, moved):
    return pl.CostEstimate(flops=int(flops), bytes_accessed=int(moved), transcendentals=0)


def exchanged(blocks):
    return lax.all_to_all(blocks, RC, 0, 0, tiled=True, axis_index_groups=CHIPS)


def gathered(block):
    return exchanged(jnp.broadcast_to(block[None], (PARTS // 2,) + block.shape))


def partner(block):
    return lax.ppermute(block, "col", [(i, i ^ 1) for i in range(4)])


def local(inputs, norm_gain, w_expand, kernel, w_squeeze, w_excite, w_project, cotangent):
    nrow, ncol = lax.axis_size("row"), lax.axis_size("col")
    row, col = lax.axis_index("row"), lax.axis_index("col")
    x = inputs[0].transpose(1, 0, 2)
    c = cotangent[0].transpose(1, 0, 2)
    fwd_row = [(i, i + 1) for i in range(nrow - 1)]
    bwd_row = [(i + 1, i) for i in range(nrow - 1)]
    fwd_col = [(i, i + 1) for i in range(ncol - 1)]
    bwd_col = [(i + 1, i) for i in range(ncol - 1)]
    top = lax.ppermute(jnp.concatenate([x[6:8], c[7:8]], axis=0), "row", fwd_row)
    bot = lax.ppermute(jnp.concatenate([x[0:2], c[0:1]], axis=0), "row", bwd_row)
    gain = norm_gain[None, :]
    wprojt, taps = w_project.T, kernel.T
    halo = full(3, CH, LANES)
    tile = full(ROWS, CH, LANES)
    edge = full(CH, LANES)
    weight = full(CH, EX)
    anywhere = pl.BlockSpec(memory_space=pl.ANY)
    chunk_rows = lambda width: pl.BlockSpec((EB, width), lambda j: (j, 0))
    chunk_cols = pl.BlockSpec((CH, EB), lambda j: (0, j))
    chunk_taps = pl.BlockSpec((9, EB), lambda j: (0, j))
    scaled, inv, part, pre, hid, gg = pl.pallas_call(
        expand_kernel,
        grid=(STEPS,),
        in_specs=[tile, tile, full(1, CH), chunk_cols, chunk_cols],
        out_specs=[full(CH, ROWS * LANES), full(ROWS, LANES), edge, chunk_rows(ROWS * LANES),
                   chunk_rows(ROWS * LANES), chunk_rows(ROWS * LANES)],
        out_shape=[shape(CH, ROWS * LANES, dtype=BF16), shape(ROWS, LANES),
                   shape(CH, LANES, dtype=BF16),
                   shape(EX, ROWS * LANES), shape(EX, ROWS * LANES, dtype=BF16),
                   shape(EX, ROWS * LANES)],
        scratch_shapes=[pltpu.VMEM((CH, ROWS * LANES), BF16)],
        compiler_params=params(),
        cost_estimate=cost(600e6, 10e6),
        name="expand",
    )(x, c, gain, w_expand, wprojt)
    own = pl.pallas_call(
        strip_kernel,
        out_shape=shape(CH, LANES, dtype=BF16),
        compiler_params=params(False, 4096),
        cost_estimate=cost(1e6, 1e6),
        name="strip",
    )(part, top, bot)
    left = lax.ppermute(own, "col", fwd_col)
    right = lax.ppermute(own, "col", bwd_col)

    line = lax.broadcasted_iota(jnp.int32, (8, LANES), 1) // 8
    pos = lax.broadcasted_iota(jnp.int32, (8, LANES), 1) % 8
    kind = lax.broadcasted_iota(jnp.int32, (8, LANES), 0)
    top_ok, bot_ok = row > 0, row < nrow - 1
    strip_ok = ((pos == 3) & (col > 0)) | ((pos == 2) & (col < ncol - 1))
    strip_ok &= ((line > 1) | top_ok) & ((line < ROWS + 2) | bot_ok)
    mask = ((kind == 0) & top_ok) | ((kind == 1) & bot_ok) | ((kind == 2) & strip_ok)
    mask = mask.astype(F32)
    conv, sums = pl.pallas_call(
        forward_kernel,
        grid=(STEPS,),
        in_specs=[halo, halo, edge, edge, edge, full(1, CH), chunk_cols, chunk_taps,
                  anywhere, anywhere],
        out_specs=[chunk_rows(CS * LANES), full(16, LANES)],
        out_shape=[shape(EX, CS * LANES), shape(16, LANES)],
        scratch_shapes=[
            pltpu.VMEM((CH, (XS - ROWS) * LANES), BF16),
            pltpu.VMEM((EB, (XS - ROWS) * LANES), F32),
            pltpu.VMEM((EB, 9 * LANES), F32),
            pltpu.VMEM((2, EB, LANES), F32),
            pltpu.VMEM((2, EB, ROWS * LANES), BF16),
            pltpu.VMEM((2, EB, ROWS * LANES), F32),
            pltpu.SemaphoreType.DMA((2, 2)),
        ],
        compiler_params=params(),
        cost_estimate=cost(200e6, 12e6),
        name="forward",
    )(top, bot, own, left, right, gain, w_expand, taps, hid, gg)

    sums = gathered(sums + partner(sums))
    core = (col % 2).astype(jnp.int32).reshape(1)
    out, gin, keep, send, vec = pl.pallas_call(
        backward_kernel,
        grid=(STEPS,),
        in_specs=[pl.BlockSpec(memory_space=pltpu.SMEM), full(PARTS // 2, 16, LANES),
                  full(SQ, EX), full(SQ, EX), tile, tile, halo, halo, edge, edge, full(1, CH),
                  full(8, LANES), full(CH, ROWS * LANES), full(ROWS, LANES),
                  anywhere, anywhere, anywhere, chunk_taps,
                  weight, weight],
        out_specs=[tile, tile, anywhere, anywhere, full(16, LANES)],
        out_shape=[shape(ROWS, CH, LANES, dtype=BF16), shape(ROWS, CH, LANES, dtype=BF16),
                   shape(PARTS // 2 * PACK, LANES), shape(PARTS // 2 * PACK, LANES),
                   shape(16, LANES)],
        scratch_shapes=[
            pltpu.VMEM((PARTS * PACK, LANES), F32),
            pltpu.VMEM((EX, LANES), F32),
            pltpu.VMEM((EX, LANES), F32),
            pltpu.VMEM((CH, 3 * LANES), BF16),
            pltpu.VMEM((CH, ROWS * LANES), BF16),
            pltpu.VMEM((EX, 3 * LANES), F32),
            pltpu.VMEM((EX, ROWS * LANES), BF16),
            pltpu.VMEM((EX, ROWS * LANES), BF16),
            pltpu.VMEM((EB, 9 * LANES), F32),
            pltpu.VMEM((EB, LANES), F32),
            pltpu.VMEM((56, LANES), F32),
            pltpu.VMEM((2, EB, ROWS * LANES), F32),
            pltpu.VMEM((2, EB, ROWS * LANES), F32),
            pltpu.VMEM((2, EB, CS * LANES), F32),
            pltpu.SemaphoreType.DMA((3, 2)),
            pltpu.SemaphoreType.DMA((2,)),
        ],
        compiler_params=params(),
        cost_estimate=cost(1500e6, 16e6),
        name="backward",
    )(core, sums, w_squeeze.T, w_excite, x, c, top, bot, left, right, gain, mask, scaled, inv, gg, pre, conv, taps,
      w_expand, wprojt)

    keep = keep.reshape(PARTS // 2, PACK, LANES)
    sent = partner(send).reshape(PARTS // 2, PACK, LANES)
    halves = to_half(
        keep + sent, keep[:, 74:75] + sent[:, 74:75], keep[:, 75:76] + sent[:, 75:76]
    )
    mine = exchanged(halves)
    total = jnp.sum(from_half(mine), axis=0)
    vecs = vec[None]
    sample = lax.axis_index("dp")
    members = 1
    for bit in (4, 2, 1):
        both = lax.ppermute(
            jnp.concatenate([total, vecs.reshape(16 * members, LANES)], axis=0),
            "dp",
            [(i, i ^ bit) for i in range(8)],
        )
        total = total + both[:PACK]
        theirs = both[PACK:].reshape(members, 16, LANES)
        ahead = (sample & bit) == 0
        vecs = jnp.concatenate(
            [jnp.where(ahead, vecs, theirs), jnp.where(ahead, theirs, vecs)], axis=0
        )
        members *= 2
    vecs = vecs.reshape(8, 2048)
    grad_wexc = jnp.einsum("bs,be->se", vecs[:, 1536:1584], vecs[:, 768:1536], precision=HIGH)
    grad_wsq = jnp.einsum("be,bs->es", vecs[:, :768], vecs[:, 1664:1712], precision=HIGH)
    same = gathered(to_half(total[None], total[None, 74:75], total[None, 75:76])[0])
    other = partner(same)
    even = core[0] == 0
    every = jnp.stack(
        [jnp.where(even, same, other), jnp.where(even, other, same)], axis=1
    ).reshape(PARTS, PACK, LANES).astype(F32)
    big = (every[:, :72] * jnp.exp2(every[:, 74:75])).reshape(2, CH // 8, BLOCKS, 8, LANES)
    big = big.transpose(0, 1, 3, 2, 4).reshape(2, CH, EX)
    small = (every[:, 72:74] * jnp.exp2(every[:, 77:78])).reshape(8192)
    return (
        out.transpose(1, 0, 2)[None],
        gin.transpose(1, 0, 2)[None],
        small[6912:7104],
        big[0],
        small[:6912].reshape(9, 768).T,
        grad_wsq,
        grad_wexc,
        big[1].T,
    )


def solution(mesh):
    placed = (
        P("dp", None, "row", "col"),
        P(),
        P(),
        P(),
        P(),
        P(),
        P(),
        P("dp", None, "row", "col"),
    )
    return jax.shard_map(
        local,
        mesh=mesh,
        in_specs=placed,
        out_specs=(
            P("dp", None, "row", "col"),
            P("dp", None, "row", "col"),
            P(),
            P(),
            P(),
            P(),
            P(),
            P(),
        ),
        check_vma=False,
    )
```

```python
import jax
import jax.numpy as jnp
from jax import lax
from jax.experimental import pallas as pl
from jax.experimental.pallas import tpu as pltpu
from jax.sharding import PartitionSpec as P

EPS = 1e-06
HIGH = lax.Precision.HIGHEST
RC = ("row", "col")
F32, BF16 = jnp.float32, jnp.bfloat16
CH, EX, SQ = 192, 768, 48
ROWS, LANES = 8, 128
EB = 256
SUB = 16
STEPS = EX // EB
BLOCKS = EX // LANES
PARTS, PACK = 32, 80
VMEM_KIB = 60 * 1024
CHIPS = [[2 * q + core for q in range(PARTS // 2)] for core in range(2)]
XS = ROWS + 5
CS = ROWS + 3
NT = (((1,), (1,)), ((), ()))
TN = (((0,), (0,)), ((), ()))


def lane_iota(rows):
    return lax.broadcasted_iota(jnp.int32, (rows, LANES), 1)


def rounded(v):
    return v.astype(BF16).astype(F32)


def tn_dot(a, b):
    return lax.dot_general(a, b, TN, preferred_element_type=F32)


def lane_sum(v):
    return jnp.sum(v, axis=1, keepdims=True)


def silu_twice_slope(half):
    t = jnp.tanh(half)
    act = half * (1.0 + t)
    return act, (1.0 + t) + act * (1.0 - t)


def slab(s, n=1):
    return pl.ds(s * LANES, n * LANES)


def strip_lines(lines, total):
    lane = lane_iota(CH)
    for rr, x, c in lines:
        if x is not None:
            v = pltpu.roll(x.astype(F32), (8 * rr + 2) % LANES, 1)
            total = jnp.where((lane >= 8 * rr) & (lane < 8 * rr + 4), v, total)
        if c is not None:
            v = pltpu.roll(c.astype(F32), (8 * rr + 5) % LANES, 1)
            total = jnp.where((lane >= 8 * rr + 4) & (lane < 8 * rr + 6), v, total)
    return total


def strip_kernel(part_ref, top_ref, bot_ref, out_ref):
    last = ROWS + 2
    lines = [
        (0, top_ref[0], None),
        (1, top_ref[1], top_ref[2]),
        (last, bot_ref[0], bot_ref[2]),
        (last + 1, bot_ref[1], None),
    ]
    out_ref[...] = strip_lines(lines, part_ref[...].astype(F32)).astype(BF16)


def input_strip(own_ref, left_ref, right_ref):
    own, left, right = (r[...].astype(F32) for r in (own_ref, left_ref, right_ref))
    pos = lane_iota(CH) % 8
    value = jnp.where(pos == 0, pltpu.roll(own, LANES - 1, 1), 0.0)
    value = jnp.where(pos == 1, pltpu.roll(left, 1, 1), value)
    value = jnp.where(pos == 2, right, value)
    value = jnp.where(pos == 3, pltpu.roll(left, 2, 1), value)
    value = jnp.where(pos == 4, pltpu.roll(right, 1, 1), value)
    return jnp.where(pos == 5, pltpu.roll(own, 3, 1), value)


def cotangent_strip(left_ref, right_ref):
    left, right = (r[...].astype(F32) for r in (left_ref, right_ref))
    pos = lane_iota(CH) % 8
    value = jnp.where(pos == 3, pltpu.roll(left, LANES - 1, 1), 0.0)
    return jnp.where(pos == 2, pltpu.roll(right, LANES - 3, 1), value)


def neighbours(v, strip, rr, first, last):
    edge = pltpu.roll(strip, (LANES - 8 * rr - 3) % LANES, 1)
    left = jnp.where(first, edge, pltpu.roll(v, 1, 1))
    right = jnp.where(last, edge, pltpu.roll(v, LANES - 1, 1))
    return left, right


def spread_gain(gain_ref):
    return jnp.broadcast_to(gain_ref[...], (LANES, CH)).T


def spread_taps(taps_ref, out_s):
    for n in range(EB // LANES):
        rows = slice(n * LANES, (n + 1) * LANES)
        block = jnp.concatenate([taps_ref[:, rows], jnp.zeros((7, LANES), F32)], axis=0).T
        block = 0.5 * block
        for t in range(9):
            out_s[rows, slab(t)] = jnp.broadcast_to(block[:, t : t + 1], (LANES, LANES))


class Chunks:
    def __init__(self, pairs, sems):
        self.pairs, self.sems = pairs, sems

    def copies(self, step):
        rows = pl.ds(pl.multiple_of(step * EB, EB), EB)
        slot = step % 2
        return [
            pltpu.make_async_copy(src.at[rows, :], dst.at[slot], self.sems.at[n, slot])
            for n, (src, dst) in enumerate(self.pairs)
        ]

    def start(self, step):
        for copy in self.copies(step):
            copy.start()

    def advance(self, step):
        for copy in self.copies(step):
            copy.wait()

        @pl.when(step < STEPS - 1)
        def _():
            self.start(step + 1)


def expand_kernel(
    x_ref, c_ref, gain_ref, wexp_ref, wprojt_ref,
    scaled_out, inv_out, part_out, pre_out, hid_out, gg_out, cot_s,
):
    @pl.when(pl.program_id(0) == 0)
    def _():
        gain = spread_gain(gain_ref)
        for r in range(ROWS):
            x = x_ref[r].astype(F32)
            inverse = lax.rsqrt(jnp.sum(x * x, axis=0, keepdims=True) / CH + EPS)
            inv_out[r : r + 1, :] = inverse
            scaled_out[:, slab(r)] = (x * inverse * gain).astype(BF16)
            cot_s[:, slab(r)] = c_ref[r]
        lines = [(r + 2, x_ref[r], c_ref[r]) for r in range(ROWS)]
        part_out[...] = strip_lines(lines, jnp.zeros((CH, LANES), F32)).astype(BF16)

    pre_out[...] = tn_dot(wexp_ref[...] * 0.5, scaled_out[...])
    gg_out[...] = tn_dot(wprojt_ref[...], cot_s[...])

    def body(i, carry):
        ds = pl.ds(pl.multiple_of(i * SUB, SUB), SUB)
        v = pre_out[ds, :]
        hid_out[ds, :] = (v * (1.0 + jnp.tanh(v))).astype(BF16)
        return carry

    lax.fori_loop(0, EB // SUB, body, 0, unroll=4)


def forward_kernel(
    top_ref, bot_ref, own_ref, left_ref, right_ref, gain_ref, wexp_ref, taps_ref, hid_any, gg_any,
    conv_out, sums_out, scaled_s, pre_s, taps_s, acc_s, hid_s, gg_s, sems,
):
    step = pl.program_id(0)
    chunks = Chunks(((hid_any, hid_s), (gg_any, gg_s)), sems)
    hid_ref, gg_ref = hid_s.at[step % 2], gg_s.at[step % 2]

    @pl.when(step == 0)
    def _():
        chunks.start(0)
        gain = 0.5 * spread_gain(gain_ref)
        for s in range(XS - ROWS):
            if s < 2:
                x = top_ref[s].astype(F32)
            elif s < 4:
                x = bot_ref[s - 2].astype(F32)
            else:
                x = input_strip(own_ref, left_ref, right_ref)
            inverse = lax.rsqrt(jnp.sum(x * x, axis=0, keepdims=True) / CH + EPS)
            scaled_s[:, slab(s)] = (x * inverse * gain).astype(BF16)
        sums_out[...] = jnp.zeros_like(sums_out)

    pre_s[...] = tn_dot(wexp_ref[...], scaled_s[...])
    spread_taps(taps_ref, taps_s)
    chunks.advance(step)
    lane = lane_iota(SUB)
    first, last = lane == 0, lane == LANES - 1

    def body(i, carry):
        ds = pl.ds(pl.multiple_of(i * SUB, SUB), SUB)
        k = [taps_s[ds, slab(t)] for t in range(9)]

        def hidden(s):
            if 2 <= s < ROWS + 2:
                return hid_ref[ds, slab(s - 2)].astype(F32)
            v = pre_s[ds, slab(s if s < 2 else s - ROWS)]
            return rounded(v * (1.0 + jnp.tanh(v)))

        strip = hidden(XS - 1)
        acc = [None] * (ROWS + 4)
        for rr in range(ROWS + 4):
            h = hidden(rr)
            hl, hr = neighbours(h, strip, rr, first, last)
            for a in (-1, 0, 1):
                o = rr - a
                if 1 <= o <= ROWS + 2:
                    t = 3 * (a + 1)
                    term = k[t] * hl + k[t + 1] * h + k[t + 2] * hr
                    acc[o] = term if acc[o] is None else acc[o] + term
        pooled = jnp.zeros((SUB, LANES), F32)
        gexc = jnp.zeros((SUB, LANES), F32)
        for o in range(1, ROWS + 3):
            v = acc[o]
            conv_out[ds, slab(o - 1)] = v
            if 2 <= o <= ROWS + 1:
                act = v * (1.0 + jnp.tanh(v))
                pooled = pooled + act
                gexc = gexc + act * gg_ref[ds, slab(o - 2)]
        edge = None
        for a in (-1, 0, 1):
            for c in (-1, 0, 1):
                shift = (-(8 * a + 2 * c)) % LANES
                term = k[3 * (a + 1) + c + 1] * (pltpu.roll(strip, shift, 1) if shift else strip)
                edge = term if edge is None else edge + term
        conv_out[ds, slab(CS - 1)] = edge
        acc_s[0, ds, :] = pooled
        acc_s[1, ds, :] = gexc
        return carry

    lax.fori_loop(0, EB // SUB, body, 0, unroll=8)
    for n in range(EB // LANES):
        for kind in range(2):
            row = jnp.sum(acc_s[kind, n * LANES : (n + 1) * LANES, :].T, axis=0, keepdims=True)
            sums_out[pl.ds(2 * (step * (EB // LANES) + n) + kind, 1), :] = row


def squeeze_excite(parts_ref, wsq_ref, wexc_ref, exc_s, gp_s, vec_out):
    pixels = 32768.0
    total = jnp.sum(parts_ref[...], axis=0)
    pooled = jnp.concatenate([total[2 * j : 2 * j + 1] for j in range(BLOCKS)], axis=1) / pixels
    gexc = jnp.concatenate([total[2 * j + 1 : 2 * j + 2] for j in range(BLOCKS)], axis=1)
    pooled = jnp.broadcast_to(pooled, (8, EX))
    gexc = jnp.broadcast_to(gexc, (8, EX))
    wsq, wexc = wsq_ref[...], wexc_ref[...]
    spre = lax.dot_general(pooled, wsq, NT, precision=HIGH, preferred_element_type=F32)
    sig = jax.nn.sigmoid(spre)
    squeezed = spre * sig
    epre = jnp.dot(squeezed, wexc, precision=HIGH, preferred_element_type=F32)
    excite = jax.nn.sigmoid(epre)
    gepre = gexc * excite * (1.0 - excite)
    gspre = lax.dot_general(gepre, wexc, NT, precision=HIGH, preferred_element_type=F32)
    gspre = gspre * (sig * (1.0 + spre * (1.0 - sig)))
    gpool = jnp.dot(gspre, wsq, precision=HIGH, preferred_element_type=F32)
    gpool = gpool / pixels
    vec_out[...] = jnp.zeros((16, LANES), F32)
    for j in range(BLOCKS):
        cols = slice(j * LANES, (j + 1) * LANES)
        exc_s[cols, :] = jnp.broadcast_to(excite[:1, cols], (LANES, LANES)).T
        gp_s[cols, :] = jnp.broadcast_to(gpool[:1, cols], (LANES, LANES)).T
        vec_out[j : j + 1, :] = pooled[:1, cols]
        vec_out[BLOCKS + j : BLOCKS + j + 1, :] = gepre[:1, cols]
    vec_out[12:13, :SQ] = squeezed[:1]
    vec_out[13:14, :SQ] = gspre[:1]


def backward_kernel(
    core_ref, parts_ref, wsq_ref, wexc_ref, x_ref, c_ref, top_ref, bot_ref, left_ref, right_ref,
    gain_ref, mask_ref, scaled_ref, inv_ref, gg_any, pre_any, conv_any, taps_ref, wexp_ref, wprojt_ref,
    out_out, gin_out, keep_any, send_any, vec_out,
    packed_s, exc_s, gp_s, rim_s, cot_s, gg_s, gated_s, gpre_s, taps_s, acc_s, tsum_s,
    ggc_s, prec_s, convc_s, sems, out_sems,
):
    step = pl.program_id(0)
    chunks = Chunks(((gg_any, ggc_s), (pre_any, prec_s), (conv_any, convc_s)), sems)
    gg_ref, pre_ref, conv_ref = (r.at[step % 2] for r in (ggc_s, prec_s, convc_s))

    @pl.when(step == 0)
    def _():
        chunks.start(0)
        squeeze_excite(parts_ref, wsq_ref, wexc_ref, exc_s, gp_s, vec_out)
        for r in range(ROWS):
            cot_s[:, slab(r)] = c_ref[r]
        rim_s[:, slab(0)] = top_ref[2]
        rim_s[:, slab(1)] = bot_ref[2]
        rim_s[:, slab(2)] = cotangent_strip(left_ref, right_ref).astype(BF16)
        gg_s[...] = tn_dot(wprojt_ref[...], rim_s[...])

    spread_taps(taps_ref, taps_s)
    chunks.advance(step)
    base = step * EB
    lane = lane_iota(SUB)
    first, last = lane == 0, lane == LANES - 1

    def body(i, carry):
        ds = pl.ds(pl.multiple_of(i * SUB, SUB), SUB)
        whole = pl.ds(pl.multiple_of(base + i * SUB, SUB), SUB)
        k = [taps_s[ds, slab(t)] for t in range(9)]
        exc, gp = exc_s[whole, :], 0.5 * gp_s[whole, :]
        half = 0.5 * exc

        def grad_conv(s, mask):
            act, slope = silu_twice_slope(conv_ref[ds, slab(s)])
            if 1 <= s <= ROWS:
                gated_s[whole, slab(s - 1)] = (act * exc).astype(BF16)
            if 1 <= s <= ROWS:
                g = gg_ref[ds, slab(s - 1)]
            else:
                g = gg_s[whole, slab(0 if s == 0 else s - ROWS)]
            g = (g * half + gp) * slope
            if mask is not None:
                g = jnp.where(mask_ref[mask : mask + 1, :] > 0.5, g, 0.0)
            return rounded(g)

        def hidden(r):
            act, slope = silu_twice_slope(pre_ref[ds, slab(r)])
            return rounded(act), slope

        strip = grad_conv(CS - 1, 2)
        tap = [None] * 9
        state = {}
        gh = {}
        for s in range(ROWS + 2):
            g = grad_conv(s, 0 if s == 0 else 1 if s == ROWS + 1 else None)
            gl, gr = neighbours(g, strip, s + 1, first, last)
            for a in (-1, 0, 1):
                r = s + a - 1
                if 0 <= r < ROWS:
                    if r not in state:
                        state[r] = hidden(r)
                    h = state[r][0]
                    t = 3 * (a + 1)
                    term = k[t] * gr + k[t + 1] * g + k[t + 2] * gl
                    gh[r] = term if r not in gh else gh[r] + term
                    for c, v in enumerate((gr, g, gl)):
                        tap[t + c] = h * v if tap[t + c] is None else tap[t + c] + h * v
            r = s - 2
            if 0 <= r:
                gpre_s[whole, slab(r)] = (gh.pop(r) * state.pop(r)[1]).astype(BF16)
        total = jnp.zeros((SUB, LANES), F32)
        for t in range(9):
            total = jnp.where(lane == t, lane_sum(tap[t]), total)
        acc_s[ds, :] = total
        return carry

    lax.fori_loop(0, EB // SUB, body, 0, unroll=2)
    for n in range(EB // LANES):
        taps = acc_s[n * LANES : (n + 1) * LANES, :].T
        block = step * (EB // LANES) + n
        for t in range(9):
            tsum_s[pl.ds(BLOCKS * t + block, 1), :] = taps[t : t + 1]

    @pl.when(step == STEPS - 1)
    def _():
        gated, gpre = gated_s[...], gpre_s[...]
        for which, w in enumerate(
            (
                lax.dot_general(scaled_ref[...], gpre, NT, preferred_element_type=F32),
                lax.dot_general(cot_s[...], gated, NT, preferred_element_type=F32),
            )
        ):
            for i in range(CH // 8):
                for n in range(BLOCKS):
                    group = (which * (CH // 8) + i) * BLOCKS + n
                    part = group // 9
                    row = PACK * (part % 2 * PARTS // 2 + part // 2) + 8 * (group % 9)
                    packed_s[row : row + 8, :] = w[8 * i : 8 * i + 8, slab(n)]
        gs_all = jnp.dot(wexp_ref[...], gpre, preferred_element_type=F32)
        ggain = jnp.zeros((CH, LANES), F32)
        for r in range(ROWS):
            normed = x_ref[r].astype(F32) * inv_ref[r : r + 1, :]
            ggain = ggain + gs_all[:, r * LANES : (r + 1) * LANES] * normed
        sums = jnp.broadcast_to(lane_sum(ggain), (CH, LANES)).T[:1]
        tsum_s[54:55, :] = sums[:, :LANES]
        tsum_s[55:56, :] = jnp.zeros((1, LANES), F32)
        tsum_s[55:56, : CH - LANES] = sums[:, LANES:]
        spare = lax.broadcasted_iota(jnp.int32, (8, LANES), 0)
        for d in range(PARTS):
            base = (d % 2 * PARTS // 2 + d // 2) * PACK
            packed_s[base + 72 : base + PACK, :] = jnp.zeros((8, LANES), F32)
            if d < 28:
                packed_s[base + 72 : base + 74, :] = tsum_s[2 * d : 2 * d + 2, :]
            tail = packed_s[base + 72 : base + PACK, :]
            big = jnp.max(jnp.abs(packed_s[base : base + 72, :]), axis=0, keepdims=True)
            tail = jnp.where(spare == 2, big, tail)
            small = jnp.max(jnp.where(spare < 2, jnp.abs(tail), 0.0), axis=0, keepdims=True)
            packed_s[base + 72 : base + PACK, :] = jnp.where(spare == 3, small, tail)
        core, half = core_ref[0], PARTS // 2 * PACK
        sends = [
            pltpu.make_async_copy(
                packed_s.at[pl.ds(pl.multiple_of(half * which, 8), half), :], dst, out_sems.at[n]
            )
            for n, (which, dst) in enumerate(((core, keep_any), (1 - core, send_any)))
        ]
        for copy in sends:
            copy.start()
        proj = jnp.dot(wprojt_ref[...], gated, preferred_element_type=F32)
        gain = spread_gain(gain_ref)
        for r in range(ROWS):
            x = x_ref[r].astype(F32)
            out_out[r] = (x + proj[:, r * LANES : (r + 1) * LANES]).astype(BF16)
            inverse = inv_ref[r : r + 1, :]
            normed = x * inverse
            gnormed = gs_all[:, r * LANES : (r + 1) * LANES] * gain
            mean = jnp.sum(gnormed * normed, axis=0, keepdims=True) / CH
            gin_out[r] = (inverse * (gnormed - normed * mean) + c_ref[r].astype(F32)).astype(BF16)
        for copy in sends:
            copy.wait()


def scale_kernel(x_ref, out_ref):
    def exponent(v):
        top = jnp.max(jnp.max(jnp.abs(v), axis=0, keepdims=True), axis=1, keepdims=True)
        return jnp.ceil(jnp.log2(jnp.maximum(jnp.broadcast_to(top, (8, LANES)), 1e-30)))

    row = lax.broadcasted_iota(jnp.int32, (8, LANES), 0)
    rest = x_ref[72:80, :]
    e_big = exponent(x_ref[:72, :])
    e_small = exponent(jnp.where(row < 2, rest, 0.0))
    factor = jnp.exp2(-e_big)
    for i in range(9):
        out_ref[8 * i : 8 * i + 8, :] = x_ref[8 * i : 8 * i + 8, :] * factor
    tail = jnp.where(row < 5, e_big, e_small)
    out_ref[72:80, :] = jnp.where(row < 2, rest * jnp.exp2(-e_small), tail)


def to_half(v, big, small):
    row = lax.broadcasted_iota(jnp.int32, (1, PACK, 1), 1)
    e_big, e_small = (
        jnp.ceil(jnp.log2(jnp.maximum(jnp.max(m, axis=(1, 2), keepdims=True), 1e-30)))
        for m in (big, small)
    )
    scaled = v * jnp.where(row < 72, jnp.exp2(-e_big), jnp.exp2(-e_small))
    return jnp.where(row < 74, scaled, jnp.where(row < 77, e_big, e_small)).astype(jnp.float16)


def from_half(h):
    v = h.astype(F32)
    row = lax.broadcasted_iota(jnp.int32, (1, PACK, 1), 1)
    scale = jnp.where(row < 72, jnp.exp2(v[:, 74:75]), jnp.exp2(v[:, 77:78]))
    return jnp.where(row < 74, v * scale, 0.0)


def shape(*dims, dtype=F32):
    return jax.ShapeDtypeStruct(dims, dtype)


def full(*dims):
    return pl.BlockSpec(dims, lambda j: (0,) * len(dims))


def params(grid=True, kib=VMEM_KIB):
    return pltpu.CompilerParams(
        dimension_semantics=("arbitrary",) if grid else None, vmem_limit_bytes=kib * 1024
    )


def cost(flops, moved):
    return pl.CostEstimate(flops=int(flops), bytes_accessed=int(moved), transcendentals=0)


def exchanged(blocks):
    return lax.all_to_all(blocks, RC, 0, 0, tiled=True, axis_index_groups=CHIPS)


def gathered(block):
    return exchanged(jnp.broadcast_to(block[None], (PARTS // 2,) + block.shape))


def partner(block):
    return lax.ppermute(block, "col", [(i, i ^ 1) for i in range(4)])


def local(inputs, norm_gain, w_expand, kernel, w_squeeze, w_excite, w_project, cotangent):
    nrow, ncol = lax.axis_size("row"), lax.axis_size("col")
    row, col = lax.axis_index("row"), lax.axis_index("col")
    x = inputs[0].transpose(1, 0, 2)
    c = cotangent[0].transpose(1, 0, 2)
    fwd_row = [(i, i + 1) for i in range(nrow - 1)]
    bwd_row = [(i + 1, i) for i in range(nrow - 1)]
    fwd_col = [(i, i + 1) for i in range(ncol - 1)]
    bwd_col = [(i + 1, i) for i in range(ncol - 1)]
    top = lax.ppermute(jnp.concatenate([x[6:8], c[7:8]], axis=0), "row", fwd_row)
    bot = lax.ppermute(jnp.concatenate([x[0:2], c[0:1]], axis=0), "row", bwd_row)
    gain = norm_gain[None, :]
    wprojt, taps = w_project.T, kernel.T
    halo = full(3, CH, LANES)
    tile = full(ROWS, CH, LANES)
    edge = full(CH, LANES)
    weight = full(CH, EX)
    anywhere = pl.BlockSpec(memory_space=pl.ANY)
    chunk_rows = lambda width: pl.BlockSpec((EB, width), lambda j: (j, 0))
    chunk_cols = pl.BlockSpec((CH, EB), lambda j: (0, j))
    chunk_taps = pl.BlockSpec((9, EB), lambda j: (0, j))
    scaled, inv, part, pre, hid, gg = pl.pallas_call(
        expand_kernel,
        grid=(STEPS,),
        in_specs=[tile, tile, full(1, CH), chunk_cols, chunk_cols],
        out_specs=[full(CH, ROWS * LANES), full(ROWS, LANES), edge, chunk_rows(ROWS * LANES),
                   chunk_rows(ROWS * LANES), chunk_rows(ROWS * LANES)],
        out_shape=[shape(CH, ROWS * LANES, dtype=BF16), shape(ROWS, LANES),
                   shape(CH, LANES, dtype=BF16),
                   shape(EX, ROWS * LANES), shape(EX, ROWS * LANES, dtype=BF16),
                   shape(EX, ROWS * LANES)],
        scratch_shapes=[pltpu.VMEM((CH, ROWS * LANES), BF16)],
        compiler_params=params(),
        cost_estimate=cost(600e6, 10e6),
        name="expand",
    )(x, c, gain, w_expand, wprojt)
    own = pl.pallas_call(
        strip_kernel,
        out_shape=shape(CH, LANES, dtype=BF16),
        compiler_params=params(False, 4096),
        cost_estimate=cost(1e6, 1e6),
        name="strip",
    )(part, top, bot)
    left = lax.ppermute(own, "col", fwd_col)
    right = lax.ppermute(own, "col", bwd_col)

    line = lax.broadcasted_iota(jnp.int32, (8, LANES), 1) // 8
    pos = lax.broadcasted_iota(jnp.int32, (8, LANES), 1) % 8
    kind = lax.broadcasted_iota(jnp.int32, (8, LANES), 0)
    top_ok, bot_ok = row > 0, row < nrow - 1
    strip_ok = ((pos == 3) & (col > 0)) | ((pos == 2) & (col < ncol - 1))
    strip_ok &= ((line > 1) | top_ok) & ((line < ROWS + 2) | bot_ok)
    mask = ((kind == 0) & top_ok) | ((kind == 1) & bot_ok) | ((kind == 2) & strip_ok)
    mask = mask.astype(F32)
    conv, sums = pl.pallas_call(
        forward_kernel,
        grid=(STEPS,),
        in_specs=[halo, halo, edge, edge, edge, full(1, CH), chunk_cols, chunk_taps,
                  anywhere, anywhere],
        out_specs=[chunk_rows(CS * LANES), full(16, LANES)],
        out_shape=[shape(EX, CS * LANES), shape(16, LANES)],
        scratch_shapes=[
            pltpu.VMEM((CH, (XS - ROWS) * LANES), BF16),
            pltpu.VMEM((EB, (XS - ROWS) * LANES), F32),
            pltpu.VMEM((EB, 9 * LANES), F32),
            pltpu.VMEM((2, EB, LANES), F32),
            pltpu.VMEM((2, EB, ROWS * LANES), BF16),
            pltpu.VMEM((2, EB, ROWS * LANES), F32),
            pltpu.SemaphoreType.DMA((2, 2)),
        ],
        compiler_params=params(),
        cost_estimate=cost(200e6, 12e6),
        name="forward",
    )(top, bot, own, left, right, gain, w_expand, taps, hid, gg)

    sums = gathered(sums + partner(sums))
    core = (col % 2).astype(jnp.int32).reshape(1)
    out, gin, keep, send, vec = pl.pallas_call(
        backward_kernel,
        grid=(STEPS,),
        in_specs=[pl.BlockSpec(memory_space=pltpu.SMEM), full(PARTS // 2, 16, LANES),
                  full(SQ, EX), full(SQ, EX), tile, tile, halo, halo, edge, edge, full(1, CH),
                  full(8, LANES), full(CH, ROWS * LANES), full(ROWS, LANES),
                  anywhere, anywhere, anywhere, chunk_taps,
                  weight, weight],
        out_specs=[tile, tile, anywhere, anywhere, full(16, LANES)],
        out_shape=[shape(ROWS, CH, LANES, dtype=BF16), shape(ROWS, CH, LANES, dtype=BF16),
                   shape(PARTS // 2 * PACK, LANES), shape(PARTS // 2 * PACK, LANES),
                   shape(16, LANES)],
        scratch_shapes=[
            pltpu.VMEM((PARTS * PACK, LANES), F32),
            pltpu.VMEM((EX, LANES), F32),
            pltpu.VMEM((EX, LANES), F32),
            pltpu.VMEM((CH, 3 * LANES), BF16),
            pltpu.VMEM((CH, ROWS * LANES), BF16),
            pltpu.VMEM((EX, 3 * LANES), F32),
            pltpu.VMEM((EX, ROWS * LANES), BF16),
            pltpu.VMEM((EX, ROWS * LANES), BF16),
            pltpu.VMEM((EB, 9 * LANES), F32),
            pltpu.VMEM((EB, LANES), F32),
            pltpu.VMEM((56, LANES), F32),
            pltpu.VMEM((2, EB, ROWS * LANES), F32),
            pltpu.VMEM((2, EB, ROWS * LANES), F32),
            pltpu.VMEM((2, EB, CS * LANES), F32),
            pltpu.SemaphoreType.DMA((3, 2)),
            pltpu.SemaphoreType.DMA((2,)),
        ],
        compiler_params=params(),
        cost_estimate=cost(1500e6, 16e6),
        name="backward",
    )(core, sums, w_squeeze.T, w_excite, x, c, top, bot, left, right, gain, mask, scaled, inv, gg, pre, conv, taps,
      w_expand, wprojt)

    pair = (keep + partner(send)).reshape(PARTS // 2, PACK, LANES)
    halves = to_half(pair, pair[:, 74:75], pair[:, 75:76])
    mine = exchanged(halves)
    total = jnp.sum(from_half(mine), axis=0)
    vecs = vec[None]
    sample = lax.axis_index("dp")
    members = 1
    for bit in (4, 2, 1):
        both = lax.ppermute(
            jnp.concatenate([total, vecs.reshape(16 * members, LANES)], axis=0),
            "dp",
            [(i, i ^ bit) for i in range(8)],
        )
        total = total + both[:PACK]
        theirs = both[PACK:].reshape(members, 16, LANES)
        ahead = (sample & bit) == 0
        vecs = jnp.concatenate(
            [jnp.where(ahead, vecs, theirs), jnp.where(ahead, theirs, vecs)], axis=0
        )
        members *= 2
    vecs = vecs.reshape(8, 2048)
    grad_wexc = jnp.einsum("bs,be->se", vecs[:, 1536:1584], vecs[:, 768:1536], precision=HIGH)
    grad_wsq = jnp.einsum("be,bs->es", vecs[:, :768], vecs[:, 1664:1712], precision=HIGH)
    scaled = pl.pallas_call(
        scale_kernel,
        out_shape=shape(PACK, LANES),
        compiler_params=params(False, 4096),
        cost_estimate=cost(1e5, 1e5),
        name="scale",
    )(total)
    same = gathered(scaled.astype(jnp.float16))
    other = partner(same)
    even = core[0] == 0
    every = jnp.stack(
        [jnp.where(even, same, other), jnp.where(even, other, same)], axis=1
    ).reshape(PARTS, PACK, LANES).astype(F32)
    big = (every[:, :72] * jnp.exp2(every[:, 74:75])).reshape(2, CH // 8, BLOCKS, 8, LANES)
    big = big.transpose(0, 1, 3, 2, 4).reshape(2, CH, EX)
    small = (every[:, 72:74] * jnp.exp2(every[:, 77:78])).reshape(8192)
    return (
        out.transpose(1, 0, 2)[None],
        gin.transpose(1, 0, 2)[None],
        small[6912:7104],
        big[0],
        small[:6912].reshape(9, 768).T,
        grad_wsq,
        grad_wexc,
        big[1].T,
    )


def solution(mesh):
    placed = (
        P("dp", None, "row", "col"),
        P(),
        P(),
        P(),
        P(),
        P(),
        P(),
        P("dp", None, "row", "col"),
    )
    return jax.shard_map(
        local,
        mesh=mesh,
        in_specs=placed,
        out_specs=(
            P("dp", None, "row", "col"),
            P("dp", None, "row", "col"),
            P(),
            P(),
            P(),
            P(),
            P(),
            P(),
        ),
        check_vma=False,
    )
```

```python
import jax
import jax.numpy as jnp
from jax import lax
from jax.experimental import pallas as pl
from jax.experimental.pallas import tpu as pltpu
from jax.sharding import PartitionSpec as P

EPS = 1e-06
HIGH = lax.Precision.HIGHEST
RC = ("row", "col")
F32, BF16 = jnp.float32, jnp.bfloat16
CH, EX, SQ = 192, 768, 48
ROWS, LANES = 8, 128
EB = 256
SUB = 16
STEPS = EX // EB
BLOCKS = EX // LANES
PARTS, PACK = 32, 80
VMEM_KIB = 60 * 1024
CHIPS = [[2 * q + core for q in range(PARTS // 2)] for core in range(2)]
XS = ROWS + 5
CS = ROWS + 3
NT = (((1,), (1,)), ((), ()))
TN = (((0,), (0,)), ((), ()))


def lane_iota(rows):
    return lax.broadcasted_iota(jnp.int32, (rows, LANES), 1)


def rounded(v):
    return v.astype(BF16).astype(F32)


def tn_dot(a, b):
    return lax.dot_general(a, b, TN, preferred_element_type=F32)


def lane_sum(v):
    return jnp.sum(v, axis=1, keepdims=True)


def silu_twice_slope(half):
    t = jnp.tanh(half)
    act = half * (1.0 + t)
    return act, (1.0 + t) + act * (1.0 - t)


def slab(s, n=1):
    return pl.ds(s * LANES, n * LANES)


def strip_lines(lines, total):
    lane = lane_iota(CH)
    for rr, x, c in lines:
        if x is not None:
            v = pltpu.roll(x.astype(F32), (8 * rr + 2) % LANES, 1)
            total = jnp.where((lane >= 8 * rr) & (lane < 8 * rr + 4), v, total)
        if c is not None:
            v = pltpu.roll(c.astype(F32), (8 * rr + 5) % LANES, 1)
            total = jnp.where((lane >= 8 * rr + 4) & (lane < 8 * rr + 6), v, total)
    return total


def strip_kernel(part_ref, top_ref, bot_ref, out_ref):
    last = ROWS + 2
    lines = [
        (0, top_ref[0], None),
        (1, top_ref[1], top_ref[2]),
        (last, bot_ref[0], bot_ref[2]),
        (last + 1, bot_ref[1], None),
    ]
    out_ref[...] = strip_lines(lines, part_ref[...].astype(F32)).astype(BF16)


def input_strip(own_ref, left_ref, right_ref):
    own, left, right = (r[...].astype(F32) for r in (own_ref, left_ref, right_ref))
    pos = lane_iota(CH) % 8
    value = jnp.where(pos == 0, pltpu.roll(own, LANES - 1, 1), 0.0)
    value = jnp.where(pos == 1, pltpu.roll(left, 1, 1), value)
    value = jnp.where(pos == 2, right, value)
    value = jnp.where(pos == 3, pltpu.roll(left, 2, 1), value)
    value = jnp.where(pos == 4, pltpu.roll(right, 1, 1), value)
    return jnp.where(pos == 5, pltpu.roll(own, 3, 1), value)


def cotangent_strip(left_ref, right_ref):
    left, right = (r[...].astype(F32) for r in (left_ref, right_ref))
    pos = lane_iota(CH) % 8
    value = jnp.where(pos == 3, pltpu.roll(left, LANES - 1, 1), 0.0)
    return jnp.where(pos == 2, pltpu.roll(right, LANES - 3, 1), value)


def neighbours(v, strip, rr, first, last):
    edge = pltpu.roll(strip, (LANES - 8 * rr - 3) % LANES, 1)
    left = jnp.where(first, edge, pltpu.roll(v, 1, 1))
    right = jnp.where(last, edge, pltpu.roll(v, LANES - 1, 1))
    return left, right


def spread_gain(gain_ref):
    return jnp.broadcast_to(gain_ref[...], (LANES, CH)).T


def spread_taps(taps_ref, out_s):
    for n in range(EB // LANES):
        rows = slice(n * LANES, (n + 1) * LANES)
        block = jnp.concatenate([taps_ref[:, rows], jnp.zeros((7, LANES), F32)], axis=0).T
        block = 0.5 * block
        for t in range(9):
            out_s[rows, slab(t)] = jnp.broadcast_to(block[:, t : t + 1], (LANES, LANES))


class Chunks:
    def __init__(self, pairs, sems):
        self.pairs, self.sems = pairs, sems

    def copies(self, step):
        rows = pl.ds(pl.multiple_of(step * EB, EB), EB)
        slot = step % 2
        return [
            pltpu.make_async_copy(src.at[rows, :], dst.at[slot], self.sems.at[n, slot])
            for n, (src, dst) in enumerate(self.pairs)
        ]

    def start(self, step):
        for copy in self.copies(step):
            copy.start()

    def advance(self, step):
        for copy in self.copies(step):
            copy.wait()

        @pl.when(step < STEPS - 1)
        def _():
            self.start(step + 1)


def expand_kernel(
    x_ref, c_ref, gain_ref, wexp_ref, wprojt_ref,
    scaled_out, inv_out, part_out, pre_out, hid_out, gg_out, cot_s,
):
    @pl.when(pl.program_id(0) == 0)
    def _():
        gain = spread_gain(gain_ref)
        for r in range(ROWS):
            x = x_ref[r].astype(F32)
            inverse = lax.rsqrt(jnp.sum(x * x, axis=0, keepdims=True) / CH + EPS)
            inv_out[r : r + 1, :] = inverse
            scaled_out[:, slab(r)] = (x * inverse * gain).astype(BF16)
            cot_s[:, slab(r)] = c_ref[r]
        lines = [(r + 2, x_ref[r], c_ref[r]) for r in range(ROWS)]
        part_out[...] = strip_lines(lines, jnp.zeros((CH, LANES), F32)).astype(BF16)

    pre_out[...] = tn_dot(wexp_ref[...] * 0.5, scaled_out[...])
    gg_out[...] = tn_dot(wprojt_ref[...], cot_s[...])

    def body(i, carry):
        ds = pl.ds(pl.multiple_of(i * SUB, SUB), SUB)
        v = pre_out[ds, :]
        hid_out[ds, :] = (v * (1.0 + jnp.tanh(v))).astype(BF16)
        return carry

    lax.fori_loop(0, EB // SUB, body, 0, unroll=4)


def forward_kernel(
    top_ref, bot_ref, own_ref, left_ref, right_ref, gain_ref, wexp_ref, taps_ref, hid_any, gg_any,
    conv_out, sums_out, scaled_s, pre_s, taps_s, acc_s, hid_s, gg_s, sems,
):
    step = pl.program_id(0)
    chunks = Chunks(((hid_any, hid_s), (gg_any, gg_s)), sems)
    hid_ref, gg_ref = hid_s.at[step % 2], gg_s.at[step % 2]

    @pl.when(step == 0)
    def _():
        chunks.start(0)
        gain = 0.5 * spread_gain(gain_ref)
        for s in range(XS - ROWS):
            if s < 2:
                x = top_ref[s].astype(F32)
            elif s < 4:
                x = bot_ref[s - 2].astype(F32)
            else:
                x = input_strip(own_ref, left_ref, right_ref)
            inverse = lax.rsqrt(jnp.sum(x * x, axis=0, keepdims=True) / CH + EPS)
            scaled_s[:, slab(s)] = (x * inverse * gain).astype(BF16)
        sums_out[...] = jnp.zeros_like(sums_out)

    pre_s[...] = tn_dot(wexp_ref[...], scaled_s[...])
    spread_taps(taps_ref, taps_s)
    chunks.advance(step)
    lane = lane_iota(SUB)
    first, last = lane == 0, lane == LANES - 1

    def body(i, carry):
        ds = pl.ds(pl.multiple_of(i * SUB, SUB), SUB)
        k = [taps_s[ds, slab(t)] for t in range(9)]

        def hidden(s):
            if 2 <= s < ROWS + 2:
                return hid_ref[ds, slab(s - 2)].astype(F32)
            v = pre_s[ds, slab(s if s < 2 else s - ROWS)]
            return rounded(v * (1.0 + jnp.tanh(v)))

        strip = hidden(XS - 1)
        acc = [None] * (ROWS + 4)
        for rr in range(ROWS + 4):
            h = hidden(rr)
            hl, hr = neighbours(h, strip, rr, first, last)
            for a in (-1, 0, 1):
                o = rr - a
                if 1 <= o <= ROWS + 2:
                    t = 3 * (a + 1)
                    term = k[t] * hl + k[t + 1] * h + k[t + 2] * hr
                    acc[o] = term if acc[o] is None else acc[o] + term
        pooled = jnp.zeros((SUB, LANES), F32)
        gexc = jnp.zeros((SUB, LANES), F32)
        for o in range(1, ROWS + 3):
            v = acc[o]
            conv_out[ds, slab(o - 1)] = v
            if 2 <= o <= ROWS + 1:
                act = v * (1.0 + jnp.tanh(v))
                pooled = pooled + act
                gexc = gexc + act * gg_ref[ds, slab(o - 2)]
        edge = None
        for a in (-1, 0, 1):
            for c in (-1, 0, 1):
                shift = (-(8 * a + 2 * c)) % LANES
                term = k[3 * (a + 1) + c + 1] * (pltpu.roll(strip, shift, 1) if shift else strip)
                edge = term if edge is None else edge + term
        conv_out[ds, slab(CS - 1)] = edge
        acc_s[0, ds, :] = pooled
        acc_s[1, ds, :] = gexc
        return carry

    lax.fori_loop(0, EB // SUB, body, 0, unroll=8)
    for n in range(EB // LANES):
        for kind in range(2):
            row = jnp.sum(acc_s[kind, n * LANES : (n + 1) * LANES, :].T, axis=0, keepdims=True)
            sums_out[pl.ds(2 * (step * (EB // LANES) + n) + kind, 1), :] = row


def squeeze_excite(parts_ref, wsq_ref, wexc_ref, exc_s, gp_s, vec_out):
    pixels = 32768.0
    total = jnp.sum(parts_ref[...], axis=0)
    pooled = jnp.concatenate([total[2 * j : 2 * j + 1] for j in range(BLOCKS)], axis=1) / pixels
    gexc = jnp.concatenate([total[2 * j + 1 : 2 * j + 2] for j in range(BLOCKS)], axis=1)
    pooled = jnp.broadcast_to(pooled, (8, EX))
    gexc = jnp.broadcast_to(gexc, (8, EX))
    wsq, wexc = wsq_ref[...], wexc_ref[...]
    spre = lax.dot_general(pooled, wsq, NT, precision=HIGH, preferred_element_type=F32)
    sig = jax.nn.sigmoid(spre)
    squeezed = spre * sig
    epre = jnp.dot(squeezed, wexc, precision=HIGH, preferred_element_type=F32)
    excite = jax.nn.sigmoid(epre)
    gepre = gexc * excite * (1.0 - excite)
    gspre = lax.dot_general(gepre, wexc, NT, precision=HIGH, preferred_element_type=F32)
    gspre = gspre * (sig * (1.0 + spre * (1.0 - sig)))
    gpool = jnp.dot(gspre, wsq, precision=HIGH, preferred_element_type=F32)
    gpool = gpool / pixels
    vec_out[...] = jnp.zeros((16, LANES), F32)
    for j in range(BLOCKS):
        cols = slice(j * LANES, (j + 1) * LANES)
        exc_s[cols, :] = jnp.broadcast_to(excite[:1, cols], (LANES, LANES)).T
        gp_s[cols, :] = jnp.broadcast_to(gpool[:1, cols], (LANES, LANES)).T
        vec_out[j : j + 1, :] = pooled[:1, cols]
        vec_out[BLOCKS + j : BLOCKS + j + 1, :] = gepre[:1, cols]
    vec_out[12:13, :SQ] = squeezed[:1]
    vec_out[13:14, :SQ] = gspre[:1]


def backward_kernel(
    core_ref, parts_ref, wsq_ref, wexc_ref, x_ref, c_ref, top_ref, bot_ref, left_ref, right_ref,
    gain_ref, mask_ref, scaled_ref, inv_ref, gg_any, pre_any, conv_any, taps_ref, wexp_ref, wprojt_ref,
    out_out, gin_out, keep_any, send_any, vec_out,
    packed_s, exc_s, gp_s, rim_s, cot_s, gg_s, gated_s, gpre_s, taps_s, acc_s, tsum_s,
    ggc_s, prec_s, convc_s, sems, out_sems,
):
    step = pl.program_id(0)
    chunks = Chunks(((gg_any, ggc_s), (pre_any, prec_s), (conv_any, convc_s)), sems)
    gg_ref, pre_ref, conv_ref = (r.at[step % 2] for r in (ggc_s, prec_s, convc_s))

    @pl.when(step == 0)
    def _():
        chunks.start(0)
        squeeze_excite(parts_ref, wsq_ref, wexc_ref, exc_s, gp_s, vec_out)
        for r in range(ROWS):
            cot_s[:, slab(r)] = c_ref[r]
        rim_s[:, slab(0)] = top_ref[2]
        rim_s[:, slab(1)] = bot_ref[2]
        rim_s[:, slab(2)] = cotangent_strip(left_ref, right_ref).astype(BF16)
        gg_s[...] = tn_dot(wprojt_ref[...], rim_s[...])

    spread_taps(taps_ref, taps_s)
    chunks.advance(step)
    base = step * EB
    lane = lane_iota(SUB)
    first, last = lane == 0, lane == LANES - 1

    def body(i, carry):
        ds = pl.ds(pl.multiple_of(i * SUB, SUB), SUB)
        whole = pl.ds(pl.multiple_of(base + i * SUB, SUB), SUB)
        k = [taps_s[ds, slab(t)] for t in range(9)]
        exc, gp = exc_s[whole, :], 0.5 * gp_s[whole, :]
        half = 0.5 * exc

        def grad_conv(s, mask):
            act, slope = silu_twice_slope(conv_ref[ds, slab(s)])
            if 1 <= s <= ROWS:
                gated_s[whole, slab(s - 1)] = (act * exc).astype(BF16)
            if 1 <= s <= ROWS:
                g = gg_ref[ds, slab(s - 1)]
            else:
                g = gg_s[whole, slab(0 if s == 0 else s - ROWS)]
            g = (g * half + gp) * slope
            if mask is not None:
                g = jnp.where(mask_ref[mask : mask + 1, :] > 0.5, g, 0.0)
            return rounded(g)

        def hidden(r):
            act, slope = silu_twice_slope(pre_ref[ds, slab(r)])
            return rounded(act), slope

        strip = grad_conv(CS - 1, 2)
        tap = [None] * 9
        state = {}
        gh = {}
        for s in range(ROWS + 2):
            g = grad_conv(s, 0 if s == 0 else 1 if s == ROWS + 1 else None)
            gl, gr = neighbours(g, strip, s + 1, first, last)
            for a in (-1, 0, 1):
                r = s + a - 1
                if 0 <= r < ROWS:
                    if r not in state:
                        state[r] = hidden(r)
                    h = state[r][0]
                    t = 3 * (a + 1)
                    term = k[t] * gr + k[t + 1] * g + k[t + 2] * gl
                    gh[r] = term if r not in gh else gh[r] + term
                    for c, v in enumerate((gr, g, gl)):
                        tap[t + c] = h * v if tap[t + c] is None else tap[t + c] + h * v
            r = s - 2
            if 0 <= r:
                gpre_s[whole, slab(r)] = (gh.pop(r) * state.pop(r)[1]).astype(BF16)
        total = jnp.zeros((SUB, LANES), F32)
        for t in range(9):
            total = jnp.where(lane == t, lane_sum(tap[t]), total)
        acc_s[ds, :] = total
        return carry

    lax.fori_loop(0, EB // SUB, body, 0, unroll=2)
    for n in range(EB // LANES):
        taps = acc_s[n * LANES : (n + 1) * LANES, :].T
        block = step * (EB // LANES) + n
        for t in range(9):
            tsum_s[pl.ds(BLOCKS * t + block, 1), :] = taps[t : t + 1]

    @pl.when(step == STEPS - 1)
    def _():
        gated, gpre = gated_s[...], gpre_s[...]
        for which, w in enumerate(
            (
                lax.dot_general(scaled_ref[...], gpre, NT, preferred_element_type=F32),
                lax.dot_general(cot_s[...], gated, NT, preferred_element_type=F32),
            )
        ):
            for i in range(CH // 8):
                for n in range(BLOCKS):
                    group = (which * (CH // 8) + i) * BLOCKS + n
                    part = group // 9
                    row = PACK * (part % 2 * PARTS // 2 + part // 2) + 8 * (group % 9)
                    packed_s[row : row + 8, :] = w[8 * i : 8 * i + 8, slab(n)]
        gs_all = jnp.dot(wexp_ref[...], gpre, preferred_element_type=F32)
        ggain = jnp.zeros((CH, LANES), F32)
        for r in range(ROWS):
            normed = x_ref[r].astype(F32) * inv_ref[r : r + 1, :]
            ggain = ggain + gs_all[:, r * LANES : (r + 1) * LANES] * normed
        sums = jnp.broadcast_to(lane_sum(ggain), (CH, LANES)).T[:1]
        tsum_s[54:55, :] = sums[:, :LANES]
        tsum_s[55:56, :] = jnp.zeros((1, LANES), F32)
        tsum_s[55:56, : CH - LANES] = sums[:, LANES:]
        spare = lax.broadcasted_iota(jnp.int32, (8, LANES), 0)
        for d in range(PARTS):
            base = (d % 2 * PARTS // 2 + d // 2) * PACK
            packed_s[base + 72 : base + PACK, :] = jnp.zeros((8, LANES), F32)
            if d < 28:
                packed_s[base + 72 : base + 74, :] = tsum_s[2 * d : 2 * d + 2, :]
            tail = packed_s[base + 72 : base + PACK, :]
            big = jnp.max(jnp.abs(packed_s[base : base + 72, :]), axis=0, keepdims=True)
            tail = jnp.where(spare == 2, big, tail)
            small = jnp.max(jnp.where(spare < 2, jnp.abs(tail), 0.0), axis=0, keepdims=True)
            packed_s[base + 72 : base + PACK, :] = jnp.where(spare == 3, small, tail)
        core, half = core_ref[0], PARTS // 2 * PACK
        sends = [
            pltpu.make_async_copy(
                packed_s.at[pl.ds(pl.multiple_of(half * which, 8), half), :], dst, out_sems.at[n]
            )
            for n, (which, dst) in enumerate(((core, keep_any), (1 - core, send_any)))
        ]
        for copy in sends:
            copy.start()
        proj = jnp.dot(wprojt_ref[...], gated, preferred_element_type=F32)
        gain = spread_gain(gain_ref)
        for r in range(ROWS):
            x = x_ref[r].astype(F32)
            out_out[r] = (x + proj[:, r * LANES : (r + 1) * LANES]).astype(BF16)
            inverse = inv_ref[r : r + 1, :]
            normed = x * inverse
            gnormed = gs_all[:, r * LANES : (r + 1) * LANES] * gain
            mean = jnp.sum(gnormed * normed, axis=0, keepdims=True) / CH
            gin_out[r] = (inverse * (gnormed - normed * mean) + c_ref[r].astype(F32)).astype(BF16)
        for copy in sends:
            copy.wait()


def spread_kernel(own_ref, other_ref, out_ref):
    total = own_ref[...] + other_ref[...]
    for q in range(PARTS // 2):
        out_ref[q] = total


def taps_kernel(rows_ref, out_ref):
    for t in range(9):
        for n in range(BLOCKS):
            q = BLOCKS * t + n
            out_ref[t : t + 1, slab(n)] = rows_ref[q // 2, q % 2 : q % 2 + 1, :]


def scale_kernel(x_ref, out_ref):
    def exponent(v):
        top = jnp.max(jnp.max(jnp.abs(v), axis=0, keepdims=True), axis=1, keepdims=True)
        return jnp.ceil(jnp.log2(jnp.maximum(jnp.broadcast_to(top, (8, LANES)), 1e-30)))

    row = lax.broadcasted_iota(jnp.int32, (8, LANES), 0)
    rest = x_ref[72:80, :]
    e_big = exponent(x_ref[:72, :])
    e_small = exponent(jnp.where(row < 2, rest, 0.0))
    factor = jnp.exp2(-e_big)
    for i in range(9):
        out_ref[8 * i : 8 * i + 8, :] = x_ref[8 * i : 8 * i + 8, :] * factor
    tail = jnp.where(row < 5, e_big, e_small)
    out_ref[72:80, :] = jnp.where(row < 2, rest * jnp.exp2(-e_small), tail)


def to_half(v, big, small):
    row = lax.broadcasted_iota(jnp.int32, (1, PACK, 1), 1)
    e_big, e_small = (
        jnp.ceil(jnp.log2(jnp.maximum(jnp.max(m, axis=(1, 2), keepdims=True), 1e-30)))
        for m in (big, small)
    )
    scaled = v * jnp.where(row < 72, jnp.exp2(-e_big), jnp.exp2(-e_small))
    return jnp.where(row < 74, scaled, jnp.where(row < 77, e_big, e_small)).astype(jnp.float16)


def from_half(h):
    v = h.astype(F32)
    row = lax.broadcasted_iota(jnp.int32, (1, PACK, 1), 1)
    scale = jnp.where(row < 72, jnp.exp2(v[:, 74:75]), jnp.exp2(v[:, 77:78]))
    return jnp.where(row < 74, v * scale, 0.0)


def shape(*dims, dtype=F32):
    return jax.ShapeDtypeStruct(dims, dtype)


def full(*dims):
    return pl.BlockSpec(dims, lambda j: (0,) * len(dims))


def params(grid=True, kib=VMEM_KIB):
    return pltpu.CompilerParams(
        dimension_semantics=("arbitrary",) if grid else None, vmem_limit_bytes=kib * 1024
    )


def cost(flops, moved):
    return pl.CostEstimate(flops=int(flops), bytes_accessed=int(moved), transcendentals=0)


def exchanged(blocks):
    return lax.all_to_all(blocks, RC, 0, 0, tiled=True, axis_index_groups=CHIPS)


def gathered(block):
    return exchanged(jnp.broadcast_to(block[None], (PARTS // 2,) + block.shape))


def partner(block):
    return lax.ppermute(block, "col", [(i, i ^ 1) for i in range(4)])


def local(inputs, norm_gain, w_expand, kernel, w_squeeze, w_excite, w_project, cotangent):
    nrow, ncol = lax.axis_size("row"), lax.axis_size("col")
    row, col = lax.axis_index("row"), lax.axis_index("col")
    x = inputs[0].transpose(1, 0, 2)
    c = cotangent[0].transpose(1, 0, 2)
    fwd_row = [(i, i + 1) for i in range(nrow - 1)]
    bwd_row = [(i + 1, i) for i in range(nrow - 1)]
    fwd_col = [(i, i + 1) for i in range(ncol - 1)]
    bwd_col = [(i + 1, i) for i in range(ncol - 1)]
    top = lax.ppermute(jnp.concatenate([x[6:8], c[7:8]], axis=0), "row", fwd_row)
    bot = lax.ppermute(jnp.concatenate([x[0:2], c[0:1]], axis=0), "row", bwd_row)
    gain = norm_gain[None, :]
    wprojt, taps = w_project.T, kernel.T
    halo = full(3, CH, LANES)
    tile = full(ROWS, CH, LANES)
    edge = full(CH, LANES)
    weight = full(CH, EX)
    anywhere = pl.BlockSpec(memory_space=pl.ANY)
    chunk_rows = lambda width: pl.BlockSpec((EB, width), lambda j: (j, 0))
    chunk_cols = pl.BlockSpec((CH, EB), lambda j: (0, j))
    chunk_taps = pl.BlockSpec((9, EB), lambda j: (0, j))
    scaled, inv, part, pre, hid, gg = pl.pallas_call(
        expand_kernel,
        grid=(STEPS,),
        in_specs=[tile, tile, full(1, CH), chunk_cols, chunk_cols],
        out_specs=[full(CH, ROWS * LANES), full(ROWS, LANES), edge, chunk_rows(ROWS * LANES),
                   chunk_rows(ROWS * LANES), chunk_rows(ROWS * LANES)],
        out_shape=[shape(CH, ROWS * LANES, dtype=BF16), shape(ROWS, LANES),
                   shape(CH, LANES, dtype=BF16),
                   shape(EX, ROWS * LANES), shape(EX, ROWS * LANES, dtype=BF16),
                   shape(EX, ROWS * LANES)],
        scratch_shapes=[pltpu.VMEM((CH, ROWS * LANES), BF16)],
        compiler_params=params(),
        cost_estimate=cost(600e6, 10e6),
        name="expand",
    )(x, c, gain, w_expand, wprojt)
    own = pl.pallas_call(
        strip_kernel,
        out_shape=shape(CH, LANES, dtype=BF16),
        compiler_params=params(False, 4096),
        cost_estimate=cost(1e6, 1e6),
        name="strip",
    )(part, top, bot)
    left = lax.ppermute(own, "col", fwd_col)
    right = lax.ppermute(own, "col", bwd_col)

    line = lax.broadcasted_iota(jnp.int32, (8, LANES), 1) // 8
    pos = lax.broadcasted_iota(jnp.int32, (8, LANES), 1) % 8
    kind = lax.broadcasted_iota(jnp.int32, (8, LANES), 0)
    top_ok, bot_ok = row > 0, row < nrow - 1
    strip_ok = ((pos == 3) & (col > 0)) | ((pos == 2) & (col < ncol - 1))
    strip_ok &= ((line > 1) | top_ok) & ((line < ROWS + 2) | bot_ok)
    mask = ((kind == 0) & top_ok) | ((kind == 1) & bot_ok) | ((kind == 2) & strip_ok)
    mask = mask.astype(F32)
    conv, sums = pl.pallas_call(
        forward_kernel,
        grid=(STEPS,),
        in_specs=[halo, halo, edge, edge, edge, full(1, CH), chunk_cols, chunk_taps,
                  anywhere, anywhere],
        out_specs=[chunk_rows(CS * LANES), full(16, LANES)],
        out_shape=[shape(EX, CS * LANES), shape(16, LANES)],
        scratch_shapes=[
            pltpu.VMEM((CH, (XS - ROWS) * LANES), BF16),
            pltpu.VMEM((EB, (XS - ROWS) * LANES), F32),
            pltpu.VMEM((EB, 9 * LANES), F32),
            pltpu.VMEM((2, EB, LANES), F32),
            pltpu.VMEM((2, EB, ROWS * LANES), BF16),
            pltpu.VMEM((2, EB, ROWS * LANES), F32),
            pltpu.SemaphoreType.DMA((2, 2)),
        ],
        compiler_params=params(),
        cost_estimate=cost(200e6, 12e6),
        name="forward",
    )(top, bot, own, left, right, gain, w_expand, taps, hid, gg)

    sums = exchanged(
        pl.pallas_call(
            spread_kernel,
            out_shape=shape(PARTS // 2, 16, LANES),
            compiler_params=params(False, 4096),
            cost_estimate=cost(1e5, 1e5),
            name="spread",
        )(sums, partner(sums))
    )
    core = (col % 2).astype(jnp.int32).reshape(1)
    out, gin, keep, send, vec = pl.pallas_call(
        backward_kernel,
        grid=(STEPS,),
        in_specs=[pl.BlockSpec(memory_space=pltpu.SMEM), full(PARTS // 2, 16, LANES),
                  full(SQ, EX), full(SQ, EX), tile, tile, halo, halo, edge, edge, full(1, CH),
                  full(8, LANES), full(CH, ROWS * LANES), full(ROWS, LANES),
                  anywhere, anywhere, anywhere, chunk_taps,
                  weight, weight],
        out_specs=[tile, tile, anywhere, anywhere, full(16, LANES)],
        out_shape=[shape(ROWS, CH, LANES, dtype=BF16), shape(ROWS, CH, LANES, dtype=BF16),
                   shape(PARTS // 2 * PACK, LANES), shape(PARTS // 2 * PACK, LANES),
                   shape(16, LANES)],
        scratch_shapes=[
            pltpu.VMEM((PARTS * PACK, LANES), F32),
            pltpu.VMEM((EX, LANES), F32),
            pltpu.VMEM((EX, LANES), F32),
            pltpu.VMEM((CH, 3 * LANES), BF16),
            pltpu.VMEM((CH, ROWS * LANES), BF16),
            pltpu.VMEM((EX, 3 * LANES), F32),
            pltpu.VMEM((EX, ROWS * LANES), BF16),
            pltpu.VMEM((EX, ROWS * LANES), BF16),
            pltpu.VMEM((EB, 9 * LANES), F32),
            pltpu.VMEM((EB, LANES), F32),
            pltpu.VMEM((56, LANES), F32),
            pltpu.VMEM((2, EB, ROWS * LANES), F32),
            pltpu.VMEM((2, EB, ROWS * LANES), F32),
            pltpu.VMEM((2, EB, CS * LANES), F32),
            pltpu.SemaphoreType.DMA((3, 2)),
            pltpu.SemaphoreType.DMA((2,)),
        ],
        compiler_params=params(),
        cost_estimate=cost(1500e6, 16e6),
        name="backward",
    )(core, sums, w_squeeze.T, w_excite, x, c, top, bot, left, right, gain, mask, scaled, inv, gg, pre, conv, taps,
      w_expand, wprojt)

    pair = (keep + partner(send)).reshape(PARTS // 2, PACK, LANES)
    halves = to_half(pair, pair[:, 74:75], pair[:, 75:76])
    mine = exchanged(halves)
    total = jnp.sum(from_half(mine), axis=0)
    vecs = vec[None]
    sample = lax.axis_index("dp")
    members = 1
    for bit in (4, 2, 1):
        both = lax.ppermute(
            jnp.concatenate([total, vecs.reshape(16 * members, LANES)], axis=0),
            "dp",
            [(i, i ^ bit) for i in range(8)],
        )
        total = total + both[:PACK]
        theirs = both[PACK:].reshape(members, 16, LANES)
        ahead = (sample & bit) == 0
        vecs = jnp.concatenate(
            [jnp.where(ahead, vecs, theirs), jnp.where(ahead, theirs, vecs)], axis=0
        )
        members *= 2
    vecs = vecs.reshape(8, 2048)
    grad_wexc = jnp.einsum("bs,be->se", vecs[:, 1536:1584], vecs[:, 768:1536], precision=HIGH)
    grad_wsq = jnp.einsum("be,bs->es", vecs[:, :768], vecs[:, 1664:1712], precision=HIGH)
    scaled = pl.pallas_call(
        scale_kernel,
        out_shape=shape(PACK, LANES),
        compiler_params=params(False, 4096),
        cost_estimate=cost(1e5, 1e5),
        name="scale",
    )(total)
    same = gathered(scaled.astype(jnp.float16))
    other = partner(same)
    even = core[0] == 0
    every = jnp.stack(
        [jnp.where(even, same, other), jnp.where(even, other, same)], axis=1
    ).reshape(PARTS, PACK, LANES).astype(F32)
    big = (every[:, :72] * jnp.exp2(every[:, 74:75])).reshape(2, CH // 8, BLOCKS, 8, LANES)
    big = big.transpose(0, 1, 3, 2, 4).reshape(2, CH, EX)
    small = every[:, 72:74] * jnp.exp2(every[:, 77:78])
    grad_taps = pl.pallas_call(
        taps_kernel,
        out_shape=shape(9, EX),
        compiler_params=params(False, 4096),
        cost_estimate=cost(1e5, 1e5),
        name="taps",
    )(small)
    small = small.reshape(8192)
    return (
        out.transpose(1, 0, 2)[None],
        gin.transpose(1, 0, 2)[None],
        small[6912:7104],
        big[0],
        grad_taps.T,
        grad_wsq,
        grad_wexc,
        big[1].T,
    )


def solution(mesh):
    placed = (
        P("dp", None, "row", "col"),
        P(),
        P(),
        P(),
        P(),
        P(),
        P(),
        P("dp", None, "row", "col"),
    )
    return jax.shard_map(
        local,
        mesh=mesh,
        in_specs=placed,
        out_specs=(
            P("dp", None, "row", "col"),
            P("dp", None, "row", "col"),
            P(),
            P(),
            P(),
            P(),
            P(),
            P(),
        ),
        check_vma=False,
    )
```
